128 devices in a mesh: blk: 128 (over x, z, y, core).
Axes of the slice: x: 4, y: 4, z: 4, core: 2. Of those that a mesh axis runs over, the one named last changes fastest.
Arguments:
- estimate: float32 [128, 110592], P('blk'), may hold values from 0.3 to 1.5
- observed: bfloat16 [128, 6, 110592], P('blk'), may hold values from 0.19921875 to 2
- psf_cells: float32 [128, 6, 4913], P('blk'), may hold values from 0.005 to 1.8, as said below
- tissue: int32 [128], P('blk'), may hold values from 0 to 1, as said below
- neighbours: int32 [128, 6], P('blk'), may hold values from -1 to 127, as said below
- psf_list: int32 [128, 6, 2], P('blk'), may hold values from 0 to 127
- psf_blend: float32 [128, 6, 2], P('blk'), may hold values from 0.1 to 1
- cell_row: int32 [128], replicated, may hold values from 0 to 127, each once
- view_order: int32 [6], replicated, may hold values from 0 to 5, each once
Outputs:
- refined: float32 [128, 110592], P('blk')
The draws below stay inside these ranges and needn't reach their ends.
Inputs may be any that keep to these rules, and one draw needn't show every extreme that they name: Block b sits on device b; blocks 0 to 1 and 64 to 65 are always tissue. With h the top bit of a block's number and r the number without it: bit 3j of r is bit j of the first grid coordinate, bit 3j + 1 of the second, bit 3j + 2 is bit j + 1 of the third, whose lowest bit is h. neighbours[b, f] is the block next to b across face f in that grid if both are tissue, else -1. `cell_row`: each grid cell in exactly one row. `view_order`: each view once; the first 2 entries are used. `psf_cells`: Positive.
All inputs are finite; a program needn't handle non-finite values.
Results may differ from the reference program's by a relative error of at most 0.0003.
Values may be sent and summed in bfloat16 or wider, within the bound.
A program may use at most 128 MiB of HBM per device.

```python
import jax
import jax.numpy as jnp
from jax import lax

E = 48
MARGIN = 8
VIEWS = 6
BLEND = 2
UPDATES = 2
BLK_DEV = 1
PAD = 64
KS = 17
E3 = 110592
KS3 = 4913
FACE = 18432
NB = 128
PCELLS = 128


def tissue_mask(key):
    numbers = jnp.arange(NB, dtype=jnp.int32)
    coins = jax.random.randint(jax.random.fold_in(key, 11), (NB,), 0, 4)
    alive = (coins > 0).astype(jnp.int32)
    half_count = NB // 2
    keep = (numbers < 2 * BLK_DEV) | (numbers >= half_count) & (numbers < half_count + 2 * BLK_DEV)
    return jnp.where(keep, 1, alive).astype(jnp.int32)


def draw_tissue(key, part):
    return tissue_mask(key)


def draw_neighbours(key, part):
    alive = tissue_mask(key)
    numbers = jnp.arange(NB, dtype=jnp.int32)
    bit_count = NB.bit_length() - 1
    low_count = bit_count - 1
    coords = [jnp.zeros_like(numbers), jnp.zeros_like(numbers), jnp.zeros_like(numbers)]
    extents = [1, 1, 1]
    for bit_place in range(low_count):
        axis_number = bit_place % 3
        coords[axis_number] = coords[axis_number] + numbers // 2 ** bit_place % 2 * 2 ** (bit_place // 3)
        extents[axis_number] = extents[axis_number] * 2
    top_bit = numbers // 2 ** low_count % 2
    coords[2] = 2 * coords[2] + top_bit
    extents[2] = extents[2] * 2
    columns = []
    for face_index in range(6):
        axis_number = face_index // 2
        step_sign = -1 if face_index % 2 == 0 else 1
        moved = list(coords)
        moved[axis_number] = coords[axis_number] + step_sign
        inside = (moved[axis_number] >= 0) & (moved[axis_number] < extents[axis_number])
        safe = [jnp.maximum(moved[0], 0), jnp.maximum(moved[1], 0), jnp.maximum(moved[2], 0)]
        target = safe[2] % 2 * 2 ** low_count
        reduced = [safe[0], safe[1], safe[2] // 2]
        for bit_place in range(low_count):
            axis_other = bit_place % 3
            level = bit_place // 3
            target = target + reduced[axis_other] // 2 ** level % 2 * 2 ** bit_place
        target = jnp.clip(target, 0, NB - 1)
        valid = inside & (alive > 0) & (alive[target] > 0)
        columns.append(jnp.where(valid, target, -1))
    return jnp.stack(columns, axis=1).astype(jnp.int32)


def draw_psf_cells(key, part):
    places = jnp.arange(KS3, dtype=jnp.int32)
    first = (places // (KS * KS) - MARGIN).astype(jnp.float32)
    second = (places // KS % KS - MARGIN).astype(jnp.float32)
    third = (places % KS - MARGIN).astype(jnp.float32)
    radius = first * first + second * second + third * third
    widths = jax.random.uniform(jax.random.fold_in(key, 21), (PCELLS, VIEWS, 1), jnp.float32, 1.0, 0.6 * MARGIN + 1.0)
    rough = jax.random.uniform(jax.random.fold_in(key, 23), (PCELLS, VIEWS, KS3), jnp.float32, 0.6, 1.4)
    shape_part = jnp.exp(-radius[None, None, :] / (2.0 * widths * widths)) + 0.02
    return (shape_part * rough).astype(jnp.float32)


def with_ends(entries, rng, least, top_value):
    longest = entries.shape.index(max(entries.shape))
    spots = []
    for shift in (0, 1):
        where = [jax.random.randint(jax.random.fold_in(rng, axis), (), 0, length) for axis, length in enumerate(entries.shape)]
        where[longest] = (where[longest] + shift) % entries.shape[longest]
        spots.append(tuple(where))
    return entries.at[spots[0]].set(least).at[spots[1]].set(top_value)


def levels(stream_key, dims, shards, least, largest):
    def one(axis_at, blocks):
        draws = jax.random.uniform(jax.random.fold_in(jax.random.fold_in(stream_key, 6), axis_at), (blocks,), jnp.float32, least / len(shards), largest / len(shards))
        return jnp.repeat(jnp.exp(draws), dims[axis_at] // blocks).reshape((-1,) + (1,) * (len(dims) - axis_at - 1))

    level = one(*shards[0])
    for cut in shards[1:]:
        level = level * one(*cut)
    return level


def setup_inputs(seed: int = 0) -> dict:
    splits = jax.random.split(jax.random.key(seed), 10)
    return {
        "estimate": jnp.clip(0.3 + 1.2 * jax.random.uniform(splits[0], (NB, E3), jnp.float32) ** levels(splits[0], (NB, E3), ((0, 128),), -0.2, 0.2), 0.3, 1.5),
        "observed": jnp.clip(0.19921875 + 1.8007812 * jax.random.uniform(splits[1], (NB, VIEWS, E3), jnp.float32) ** levels(splits[1], (NB, VIEWS, E3), ((0, 128),), -0.2, 0.2), 0.19921875, 2.0).astype(jnp.bfloat16),
        "psf_cells": draw_psf_cells(jax.random.fold_in(splits[9], 71), 0),
        "tissue": draw_tissue(jax.random.fold_in(splits[9], 71), 0),
        "neighbours": draw_neighbours(jax.random.fold_in(splits[9], 71), 0),
        "psf_list": with_ends(jax.random.randint(splits[5], (NB, VIEWS, BLEND), 0, PCELLS), jax.random.fold_in(splits[5], 1), 0, PCELLS - 1).astype(jnp.int32),
        "psf_blend": jnp.clip(0.1 + 0.9 * jax.random.uniform(splits[6], (NB, VIEWS, BLEND), jnp.float32) ** levels(splits[6], (NB, VIEWS, BLEND), ((0, 128),), -0.2, 0.2), 0.1, 1.0),
        "cell_row": jax.random.permutation(splits[7], PCELLS).astype(jnp.int32),
        "view_order": jax.random.permutation(splits[8], VIEWS).astype(jnp.int32),
    }


def side_slab(volume, face_index):
    axis_number = volume.ndim - 3 + face_index // 2
    start_now = 0 if face_index % 2 == 0 else E - MARGIN
    return lax.slice_in_dim(volume, start_now, start_now + MARGIN, axis=axis_number)


def assemble(core_block, margin_rows):
    padded = jnp.zeros((PAD, PAD, PAD), jnp.float32)
    padded = padded.at[MARGIN:MARGIN + E, MARGIN:MARGIN + E, MARGIN:MARGIN + E].set(core_block)
    for face_index in range(6):
        axis_number = face_index // 2
        shape_now = [E, E, E]
        shape_now[axis_number] = MARGIN
        slab_now = margin_rows[face_index].astype(jnp.float32).reshape(shape_now)
        start_now = [MARGIN, MARGIN, MARGIN]
        start_now[axis_number] = 0 if face_index % 2 == 0 else MARGIN + E
        padded = lax.dynamic_update_slice(padded, slab_now, start_now)
    return padded


def place_kernel(kernel):
    grid_cube = jnp.zeros((PAD, PAD, PAD), jnp.float32)
    grid_cube = grid_cube.at[0:KS, 0:KS, 0:KS].set(kernel.reshape(KS, KS, KS))
    return jnp.roll(grid_cube, (-MARGIN, -MARGIN, -MARGIN), axis=(0, 1, 2))


def refine(core_block, margin_rows, kernel, observed_block):
    padded = assemble(core_block, margin_rows)
    spectrum = jnp.fft.fftn(place_kernel(kernel))
    blurred = jnp.real(jnp.fft.ifftn(jnp.fft.fftn(padded) * spectrum))
    blurred = blurred[MARGIN:MARGIN + E, MARGIN:MARGIN + E, MARGIN:MARGIN + E]
    quotient = observed_block.astype(jnp.float32) / blurred
    holder = jnp.zeros((PAD, PAD, PAD), jnp.float32)
    holder = holder.at[MARGIN:MARGIN + E, MARGIN:MARGIN + E, MARGIN:MARGIN + E].set(quotient)
    correction = jnp.real(jnp.fft.ifftn(jnp.fft.fftn(holder) * jnp.conj(spectrum)))
    correction = correction[MARGIN:MARGIN + E, MARGIN:MARGIN + E, MARGIN:MARGIN + E]
    return core_block * correction


def reference(estimate, observed, psf_cells, tissue, neighbours, psf_list, psf_blend, cell_row, view_order):
    current = estimate.reshape(NB, E, E, E)
    opposite = jnp.array([1, 0, 3, 2, 5, 4], jnp.int32)
    for update in range(UPDATES):
        view_now = view_order[update]
        cells_now = lax.dynamic_index_in_dim(psf_cells, view_now, 1, keepdims=False)
        scaled = cells_now / jnp.sum(cells_now, axis=1, keepdims=True)
        listed = lax.dynamic_index_in_dim(psf_list, view_now, 1, keepdims=False)
        cell_rows = cell_row[listed]
        weights = lax.dynamic_index_in_dim(psf_blend, view_now, 1, keepdims=False)
        weights = weights / jnp.sum(weights, axis=1, keepdims=True)
        kernels = jnp.sum(weights[:, :, None] * scaled[cell_rows], axis=1)
        side_slabs = jnp.stack([side_slab(current, face_index).reshape(NB, FACE) for face_index in range(6)], axis=1)
        side_slabs = lax.optimization_barrier(side_slabs.astype(jnp.bfloat16))
        margins = side_slabs[jnp.maximum(neighbours, 0), opposite[None, :]]
        margins = jnp.where((neighbours >= 0)[:, :, None], margins, jnp.zeros_like(margins))
        seen_now = lax.dynamic_index_in_dim(observed, view_now, 1, keepdims=False)

        def one_block(items):
            core_block, margin_rows, kernel, observed_row, alive = items
            refined = refine(core_block, margin_rows, kernel, observed_row.reshape(E, E, E))
            return jnp.where(alive > 0, refined, core_block)

        current = lax.map(one_block, (current, margins, kernels, seen_now, tissue))
    return current.reshape(NB, E3)
```

```python
import functools
import math

import jax
import jax.numpy as jnp
import numpy as np
from jax import lax
from jax.experimental import pallas as pl
from jax.experimental.pallas import tpu as pltpu
from jax.sharding import PartitionSpec as P

E = 48
MARGIN = 8
UPDATES = 2
PAD = 64
KS = 17
E3 = 110592
KS3 = 4913
HALF = 24
PLANES = 40
TAPROWS = 32

F32 = jnp.float32
BF16 = jnp.bfloat16


def split_np(table):
    hi = np.asarray(table, np.float32).astype(jnp.bfloat16)
    lo = (np.asarray(table, np.float64) - hi.astype(np.float64)).astype(np.float32).astype(jnp.bfloat16)
    return hi, lo


def lane_table(table):
    hi, lo = split_np(table)
    row = np.concatenate([hi, lo], axis=1)
    return np.concatenate([row, row], axis=0)


def row_table(table):
    hi, lo = split_np(table)
    return np.concatenate([hi, hi, lo, lo], axis=1)


def make_tables():
    step = 2.0 * math.pi / PAD
    k = np.arange(PAD)
    ang = (k[:, None] * k[None, :] % PAD) * step
    cos, sin = np.cos(ang), np.sin(ang)
    fwd_z = np.block([[cos, -sin], [sin, cos]])
    inv_z = np.block([[cos, sin], [-sin, cos]]) / PAD
    fwd_y = np.concatenate([cos, sin], axis=0)
    inv_y = np.concatenate([cos[MARGIN : MARGIN + E], sin[MARGIN : MARGIN + E]], axis=0) / PAD
    t = np.arange(KS) - MARGIN
    ang_t = (t[:, None] * k[None, :]) % PAD * step
    tap_z = np.zeros((128, 128))
    tap_z[:KS, :PAD] = np.cos(ang_t)
    tap_z[:KS, PAD:] = -np.sin(ang_t)
    tap_y = np.zeros((128, TAPROWS))
    tap_y[:PAD, :KS] = np.cos(ang_t).T
    tap_y[PAD:, :KS] = np.sin(ang_t).T
    pack = np.zeros((2, 8 * 128, 128), np.float32)
    place = np.zeros((2, 128, 8 * 128), np.float32)
    for p in range(8):
        for s in range(2):
            for z in range(MARGIN):
                slot = p * 16 + s * 8 + z
                pack[0, p * 128 + s * 64 + MARGIN + z, slot] = 1
                pack[1, p * 128 + s * 64 + E + z, slot] = 1
                place[0, slot, p * 128 + s * 64 + z] = 1
                place[1, slot, p * 128 + s * 64 + MARGIN + E + z] = 1
    return dict(
        fwd_z=lane_table(fwd_z),
        inv_z=lane_table(inv_z),
        tap_z=lane_table(tap_z),
        fwd_y=row_table(fwd_y),
        inv_y=row_table(inv_y),
        tap_y=row_table(tap_y),
        pack=pack.astype(jnp.bfloat16),
        place=place.astype(jnp.bfloat16),
    )


TABLES = make_tables()


def split(values):
    hi = values.astype(BF16)
    lo = (values - hi.astype(F32)).astype(BF16)
    return hi, lo


def low_lanes(shape):
    return lax.broadcasted_iota(jnp.int32, shape, len(shape) - 1) < 64


def lane_sign(shape):
    return jnp.where(low_lanes(shape), 1.0, -1.0).astype(F32)


def dot(a, b):
    return lax.dot_general(a, b, (((1,), (0,)), ((), ())), preferred_element_type=F32)


def lanes_dft(rows, table):
    hi, lo = split(rows)
    both = dot(jnp.concatenate([hi, lo], axis=1), table)
    return both[:, :128] + both[:, 128:]


def rows_dft(planes, table, count, inverse):
    sign = lane_sign((count, 128))
    if inverse:
        sign = -sign
    out = []
    for a in range(0, len(planes), 2):
        cols = []
        for plane in planes[a : a + 2]:
            hi, lo = split(plane)
            cols.append(jnp.concatenate([hi, lo, hi, lo], axis=0))
        rhs = jnp.concatenate(cols, axis=1) if len(cols) > 1 else cols[0]
        both = dot(table, rhs)
        for b in range(len(cols)):
            c_part = both[:count, b * 128 : (b + 1) * 128]
            s_part = both[count : 2 * count, b * 128 : (b + 1) * 128]
            out.append(c_part + sign * pltpu.roll(s_part, 64, 1))
    return out


def emit_faces(cp_ref, pack_ref, faces):
    xm_ref, xp_ref, ym_ref, yp_ref, zm_ref, zp_ref = faces
    xm_ref[...] = cp_ref[0:8].reshape(8 * E, 128).astype(BF16)
    xp_ref[...] = cp_ref[16:24].reshape(8 * E, 128).astype(BF16)
    ym_ref[...] = cp_ref[:, 0:8, :].reshape(HALF * 8, 128).astype(BF16)
    yp_ref[...] = cp_ref[:, E - 8 : E, :].reshape(HALF * 8, 128).astype(BF16)
    for g in range(3):
        wide = jnp.concatenate([cp_ref[g * 8 + p].astype(BF16) for p in range(8)], axis=1)
        zm_ref[g * E : (g + 1) * E, :] = dot(wide, pack_ref[0]).astype(BF16)
        zp_ref[g * E : (g + 1) * E, :] = dot(wide, pack_ref[1]).astype(BF16)


FACE_SHAPES = [(8 * E, 128), (8 * E, 128), (HALF * 8, 128), (HALF * 8, 128), (3 * E, 128), (3 * E, 128)]


def start_kernel(est_ref, pack_ref, cp_ref, *faces):
    def body(o, carry):
        cp_ref[o] = est_ref[o] + pltpu.roll(est_ref[o + HALF], 64, 1)
        return carry

    lax.fori_loop(0, HALF, body, 0)
    emit_faces(cp_ref, pack_ref, faces)


def forward_planes(src_ref, z_ref, spec_ref, rows, fwd_z, fwd_y):
    group = 8

    def z_body(it, carry):
        block = src_ref[pl.ds(it * group, group)].reshape(group * rows, 128)
        z_ref[pl.ds(it * group, group), 0:rows, :] = lanes_dft(block, fwd_z).reshape(group, rows, 128)
        return carry

    lax.fori_loop(0, PLANES // group, z_body, 0)

    def y_body(it, carry):
        planes = [z_ref[it * group + j, 0:rows, :] for j in range(group)]
        for j, plane in enumerate(rows_dft(planes, fwd_y, PAD, False)):
            spec_ref[it * group + j] = plane
        return carry

    lax.fori_loop(0, PLANES // group, y_body, 0)


def filter_planes(spec_ref, kr_ref, ki_ref, out_ref, conjugate):
    group = 4
    sign = lane_sign((8, 128))
    if not conjugate:
        sign = -sign

    def body(it, carry):
        kb = it // (HALF // group)
        og = it % (HALF // group)
        rows = pl.ds(pl.multiple_of(kb * 8, 8), 8)
        first = og * group
        acc_r = [jnp.zeros((8, 128), F32) for _ in range(group)]
        acc_i = [jnp.zeros((8, 128), F32) for _ in range(group)]
        for m in range(group + KS - 1):
            value = spec_ref[first + m, rows, :]
            for j in range(group):
                d = m - j
                if 0 <= d < KS:
                    tap = d if conjugate else KS - 1 - d
                    acc_r[j] = acc_r[j] + kr_ref[tap, rows, :] * value
                    acc_i[j] = acc_i[j] + ki_ref[tap, rows, :] * value
        for j in range(group):
            out_ref[first + j, rows, :] = acc_r[j] + sign * pltpu.roll(acc_i[j], 64, 1)
        return carry

    lax.fori_loop(0, 8 * (HALF // group), body, 0)


def inverse_planes(spec_ref, y_ref, out_ref, inv_y, inv_z):
    group = 8

    def y_body(it, carry):
        planes = [spec_ref[it * group + j] for j in range(group)]
        for j, plane in enumerate(rows_dft(planes, inv_y, E, True)):
            y_ref[it * group + j, 0:E, :] = plane
        return carry

    lax.fori_loop(0, HALF // group, y_body, 0)

    def z_body(it, carry):
        block = y_ref[pl.ds(it * group, group), 0:E, :].reshape(group * E, 128)
        out_ref[pl.ds(it * group, group)] = lanes_dft(block, inv_z).reshape(group, E, 128)
        return carry

    lax.fori_loop(0, HALF // group, z_body, 0)


def update_kernel(
    last,
    flags_ref,
    cp_ref,
    obs_ref,
    taps_ref,
    hxm_ref,
    hxp_ref,
    hym_ref,
    hyp_ref,
    hzm_ref,
    hzp_ref,
    fwd_z_ref,
    inv_z_ref,
    tap_z_ref,
    fwd_y_ref,
    fwd_yc_ref,
    inv_y_ref,
    tap_y_ref,
    pack_ref,
    place_ref,
    *refs,
):
    if last:
        out_ref, refs = refs[0], refs[1:]
        faces = ()
    else:
        new_ref, faces, refs = refs[0], refs[1:7], refs[7:]
    ext_ref, pp_ref, z_ref, spec_ref, kr_ref, ki_ref, fil_ref, core_ref, q_ref = refs
    low_core = low_lanes((E, 128))
    low_full = low_lanes((PAD, 128))

    def tap_body(d, carry):
        zt = lanes_dft(taps_ref[d], tap_z_ref[...])
        spec = rows_dft([zt], tap_y_ref[...], PAD, False)[0]
        other = pltpu.roll(spec, 64, 1)
        kr_ref[d] = jnp.where(low_full, spec, other)
        ki_ref[d] = jnp.where(low_full, other, spec)
        return carry

    lax.fori_loop(0, KS, tap_body, 0)

    def face(ref, f):
        return ref[...].astype(F32) * flags_ref[1 + f].astype(F32)

    ext_ref[:, 0:8, :] = face(hym_ref, 2).reshape(HALF, 8, 128)
    ext_ref[:, 56:64, :] = face(hyp_ref, 3).reshape(HALF, 8, 128)
    flag_zm = flags_ref[5].astype(F32)
    flag_zp = flags_ref[6].astype(F32)
    for g in range(3):
        zm = dot(hzm_ref[g * E : (g + 1) * E, :], place_ref[0])
        zp = dot(hzp_ref[g * E : (g + 1) * E, :], place_ref[1])
        for p in range(8):
            lanes = slice(p * 128, (p + 1) * 128)
            ext_ref[g * 8 + p, 8:56, :] = cp_ref[g * 8 + p] + flag_zm * zm[:, lanes] + flag_zp * zp[:, lanes]
    xm = face(hxm_ref, 0).reshape(8, E, 128)
    xp = face(hxp_ref, 1).reshape(8, E, 128)
    pp_ref[8:32] = ext_ref[...]
    for j in range(8):
        for rows in (slice(0, 8), slice(56, 64)):
            near = ext_ref[16 + j, rows, :]
            pp_ref[j, rows, :] = pltpu.roll(jnp.where(low_lanes((8, 128)), near, 0.0), 64, 1)
            near = ext_ref[j, rows, :]
            pp_ref[32 + j, rows, :] = pltpu.roll(jnp.where(low_lanes((8, 128)), 0.0, near), 64, 1)
        pp_ref[j, 8:56, :] = pltpu.roll(jnp.where(low_core, ext_ref[16 + j, 8:56, :], xm[j]), 64, 1)
        pp_ref[32 + j, 8:56, :] = pltpu.roll(jnp.where(low_core, xp[j], ext_ref[j, 8:56, :]), 64, 1)

    forward_planes(pp_ref, z_ref, spec_ref, PAD, fwd_z_ref[...], fwd_y_ref[...])
    filter_planes(spec_ref, kr_ref, ki_ref, fil_ref, False)
    inverse_planes(fil_ref, z_ref, core_ref, inv_y_ref[...], inv_z_ref[...])

    lane = lax.broadcasted_iota(jnp.int32, (E, 128), 1) % 64
    inside = (lane >= MARGIN) & (lane < MARGIN + E)

    def ratio_body(o, carry):
        seen = obs_ref[o].astype(F32) + pltpu.roll(obs_ref[o + HALF].astype(F32), 64, 1)
        q_ref[o + 8] = jnp.where(inside, seen / jnp.where(inside, core_ref[o], 1.0), 0.0)
        return carry

    lax.fori_loop(0, HALF, ratio_body, 0)
    for j in range(8):
        q_ref[j] = pltpu.roll(jnp.where(low_core, q_ref[24 + j], 0.0), 64, 1)
        q_ref[32 + j] = pltpu.roll(jnp.where(low_core, 0.0, q_ref[8 + j]), 64, 1)

    forward_planes(q_ref, z_ref, spec_ref, E, fwd_z_ref[...], fwd_yc_ref[...])
    filter_planes(spec_ref, kr_ref, ki_ref, fil_ref, True)
    inverse_planes(fil_ref, z_ref, core_ref, inv_y_ref[...], inv_z_ref[...])

    alive = flags_ref[0] > 0

    def finish(o, carry):
        old = cp_ref[o]
        new = jnp.where(jnp.logical_and(inside, alive), old * core_ref[o], old)
        if last:
            out_ref[o] = new
            out_ref[o + HALF] = pltpu.roll(new, 64, 1)
        else:
            new_ref[o] = new
        return carry

    lax.fori_loop(0, HALF, finish, 0)
    if not last:
        emit_faces(new_ref, pack_ref, faces)


VMEM = pl.BlockSpec(memory_space=pltpu.VMEM)
SMEM = pl.BlockSpec(memory_space=pltpu.SMEM)


def start_call(est):
    return pl.pallas_call(
        start_kernel,
        out_shape=[jax.ShapeDtypeStruct((HALF, E, 128), F32)]
        + [jax.ShapeDtypeStruct(s, BF16) for s in FACE_SHAPES],
        in_specs=[VMEM] * 2,
        out_specs=[VMEM] * 7,
        name="start",
    )(est, jnp.asarray(TABLES["pack"]))


def fwd_y_core():
    full = TABLES["fwd_y"]
    return np.concatenate([full[:, s * PAD + MARGIN : s * PAD + MARGIN + E] for s in range(4)], axis=1)


def update_call(last, flags, cp, obs, taps, halos):
    if last:
        out_shape = jax.ShapeDtypeStruct((E, E, 128), F32)
        out_specs = VMEM
    else:
        out_shape = [jax.ShapeDtypeStruct((HALF, E, 128), F32)] + [
            jax.ShapeDtypeStruct(s, BF16) for s in FACE_SHAPES
        ]
        out_specs = [VMEM] * 7
    tables = [
        TABLES["fwd_z"],
        TABLES["inv_z"],
        TABLES["tap_z"],
        TABLES["fwd_y"],
        fwd_y_core(),
        TABLES["inv_y"],
        TABLES["tap_y"],
        TABLES["pack"],
        TABLES["place"],
    ]
    return pl.pallas_call(
        functools.partial(update_kernel, last),
        out_shape=out_shape,
        in_specs=[SMEM] + [VMEM] * (9 + len(tables)),
        out_specs=out_specs,
        scratch_shapes=[
            pltpu.VMEM((HALF, PAD, 128), F32),
            pltpu.VMEM((PLANES, PAD, 128), F32),
            pltpu.VMEM((PLANES, PAD, 128), F32),
            pltpu.VMEM((PLANES, PAD, 128), F32),
            pltpu.VMEM((KS, PAD, 128), F32),
            pltpu.VMEM((KS, PAD, 128), F32),
            pltpu.VMEM((HALF, PAD, 128), F32),
            pltpu.VMEM((HALF, E, 128), F32),
            pltpu.VMEM((PLANES, E, 128), F32),
        ],
        name="update_last" if last else "update",
    )(flags, cp, obs, taps, *halos, *[jnp.asarray(t) for t in tables])


GRID = (4, 4, 8)


def coords_of(b):
    return (
        b % 2 + 2 * ((b // 8) % 2),
        (b // 2) % 2 + 2 * ((b // 16) % 2),
        (b // 64) % 2 + 2 * ((b // 4) % 2) + 4 * ((b // 32) % 2),
    )


def block_at(c):
    return (
        c[0] % 2 + 2 * (c[1] % 2) + 4 * ((c[2] // 2) % 2) + 8 * (c[0] // 2) + 16 * (c[1] // 2)
        + 32 * (c[2] // 4) + 64 * (c[2] % 2)
    )


def neighbour_of(b, axis, step):
    c = list(coords_of(b))
    c[axis] = (c[axis] + step + GRID[axis]) % GRID[axis]
    return block_at(c)


def exchange(faces):
    halos = [None] * 6
    for f in range(6):
        axis, step = f // 2, (-1 if f % 2 == 0 else 1)
        pairs = [(b, neighbour_of(b, axis, step)) for b in range(128)]
        halos[f ^ 1] = lax.ppermute(faces[f], "blk", pairs)
    return halos


def blend_cells(shard_rows, cell_rows, weights):
    row_count = shard_rows.shape[0]
    picks = cell_rows[:, :, None] == jnp.arange(row_count, dtype=jnp.int32)[None, None, :]
    picks = picks.astype(jnp.float32) * weights[:, :, None]
    return jnp.einsum("bkr,rc->bc", picks, shard_rows, precision=lax.Precision.HIGHEST)


def local(
    estimate, observed, psf_cells, tissue, neighbours, psf_list, psf_blend, cell_row, view_order
):
    flags = jnp.concatenate([tissue, (neighbours[0] >= 0).astype(jnp.int32)])
    est = jnp.pad(estimate.reshape(E, E, E), ((0, 0), (0, 0), (8, 72)))
    cp, *faces = start_call(est)
    taps, seen = [], []
    for update in range(UPDATES):
        view = view_order[update]
        listed = lax.dynamic_index_in_dim(psf_list, view, 1, keepdims=False)
        weights = lax.dynamic_index_in_dim(psf_blend, view, 1, keepdims=False)
        weights = weights / jnp.sum(weights, axis=1, keepdims=True)
        cells = lax.dynamic_index_in_dim(psf_cells, view, 1, keepdims=False)
        cells = cells / jnp.sum(cells, axis=1, keepdims=True)
        rows = lax.all_gather(cells, "blk", axis=0, tiled=True)
        kernel = blend_cells(rows, cell_row[listed], weights)
        taps.append(jnp.pad(kernel.reshape(KS, KS, KS), ((0, 0), (0, TAPROWS - KS), (0, 128 - KS))))
        obs = lax.dynamic_index_in_dim(observed, view, 1, keepdims=False)
        seen.append(jnp.pad(obs.reshape(E, E, E), ((0, 0), (0, 0), (8, 72))))
    for update in range(UPDATES):
        halos = exchange(faces)
        last = update == UPDATES - 1
        result = update_call(last, flags, cp, seen[update], taps[update], halos)
        if not last:
            cp, *faces = result
    return result[:, :, 8:56].reshape(1, E3)


def solution(mesh):
    return jax.shard_map(
        local,
        mesh=mesh,
        in_specs=(
            P("blk", None),
            P("blk", None, None),
            P("blk", None, None),
            P("blk"),
            P("blk", None),
            P("blk", None, None),
            P("blk", None, None),
            P(),
            P(),
        ),
        out_specs=P("blk", None),
        check_vma=False,
    )
```

```python
import functools
import math

import jax
import jax.numpy as jnp
import numpy as np
from jax import lax
from jax.experimental import pallas as pl
from jax.experimental.pallas import tpu as pltpu
from jax.sharding import PartitionSpec as P

E = 48
MARGIN = 8
UPDATES = 2
PAD = 64
KS = 17
E3 = 110592
KS3 = 4913
HALF = 24
PLANES = 40
TAPROWS = 32

F32 = jnp.float32
BF16 = jnp.bfloat16


def split_np(table):
    hi = np.asarray(table, np.float32).astype(jnp.bfloat16)
    lo = (np.asarray(table, np.float64) - hi.astype(np.float64)).astype(np.float32).astype(jnp.bfloat16)
    return hi, lo


def lane_table(table):
    hi, lo = split_np(table)
    row = np.concatenate([hi, lo], axis=1)
    return np.concatenate([row, row], axis=0)


def row_table(table):
    hi, lo = split_np(table)
    return np.concatenate([hi, hi, lo, lo], axis=1)


def make_tables():
    step = 2.0 * math.pi / PAD
    k = np.arange(PAD)
    ang = (k[:, None] * k[None, :] % PAD) * step
    cos, sin = np.cos(ang), np.sin(ang)
    fwd_z = np.block([[cos, -sin], [sin, cos]])
    inv_z = np.block([[cos, sin], [-sin, cos]]) / PAD
    fwd_y = np.concatenate([cos, sin], axis=0)
    inv_y = np.concatenate([cos[MARGIN : MARGIN + E], sin[MARGIN : MARGIN + E]], axis=0) / PAD
    t = np.arange(KS) - MARGIN
    ang_t = (t[:, None] * k[None, :]) % PAD * step
    tap_z = np.zeros((128, 128))
    tap_z[:KS, :PAD] = np.cos(ang_t)
    tap_z[:KS, PAD:] = -np.sin(ang_t)
    tap_y = np.zeros((128, TAPROWS))
    tap_y[:PAD, :KS] = np.cos(ang_t).T
    tap_y[PAD:, :KS] = np.sin(ang_t).T
    pack = np.zeros((2, 8 * 128, 128), np.float32)
    place = np.zeros((2, 128, 8 * 128), np.float32)
    for p in range(8):
        for s in range(2):
            for z in range(MARGIN):
                slot = p * 16 + s * 8 + z
                pack[0, p * 128 + s * 64 + MARGIN + z, slot] = 1
                pack[1, p * 128 + s * 64 + E + z, slot] = 1
                place[0, slot, p * 128 + s * 64 + z] = 1
                place[1, slot, p * 128 + s * 64 + MARGIN + E + z] = 1
    return dict(
        fwd_z=lane_table(fwd_z),
        inv_z=lane_table(inv_z),
        tap_z=lane_table(tap_z),
        fwd_y=row_table(fwd_y),
        inv_y=row_table(inv_y),
        tap_y=row_table(tap_y),
        pack=pack.astype(jnp.bfloat16),
        place=place.astype(jnp.bfloat16),
    )


TABLES = make_tables()


def split(values):
    hi = values.astype(BF16)
    lo = (values - hi.astype(F32)).astype(BF16)
    return hi, lo


def low_lanes(shape):
    return lax.broadcasted_iota(jnp.int32, shape, len(shape) - 1) < 64


def lane_sign(shape):
    return jnp.where(low_lanes(shape), 1.0, -1.0).astype(F32)


def dot(a, b):
    return lax.dot_general(a, b, (((1,), (0,)), ((), ())), preferred_element_type=F32)


def lanes_dft(rows, table):
    hi, lo = split(rows)
    both = dot(jnp.concatenate([hi, lo], axis=1), table)
    return both[:, :128] + both[:, 128:]


def rows_dft(planes, table, count, inverse):
    sign = lane_sign((count, 128))
    if inverse:
        sign = -sign
    out = []
    for a in range(0, len(planes), 2):
        cols = []
        for plane in planes[a : a + 2]:
            hi, lo = split(plane)
            cols.append(jnp.concatenate([hi, lo, hi, lo], axis=0))
        rhs = jnp.concatenate(cols, axis=1) if len(cols) > 1 else cols[0]
        both = dot(table, rhs)
        for b in range(len(cols)):
            c_part = both[:count, b * 128 : (b + 1) * 128]
            s_part = both[count : 2 * count, b * 128 : (b + 1) * 128]
            out.append(c_part + sign * pltpu.roll(s_part, 64, 1))
    return out


def emit_faces(cp_ref, pack_ref, faces):
    xm_ref, xp_ref, ym_ref, yp_ref, zm_ref, zp_ref = faces
    xm_ref[...] = cp_ref[0:8].reshape(8 * E, 128).astype(BF16)
    xp_ref[...] = cp_ref[16:24].reshape(8 * E, 128).astype(BF16)
    ym_ref[...] = cp_ref[:, 0:8, :].reshape(HALF * 8, 128).astype(BF16)
    yp_ref[...] = cp_ref[:, E - 8 : E, :].reshape(HALF * 8, 128).astype(BF16)
    for g in range(3):
        wide = jnp.concatenate([cp_ref[g * 8 + p].astype(BF16) for p in range(8)], axis=1)
        zm_ref[g * E : (g + 1) * E, :] = dot(wide, pack_ref[0]).astype(BF16)
        zp_ref[g * E : (g + 1) * E, :] = dot(wide, pack_ref[1]).astype(BF16)


FACE_SHAPES = [(8 * E, 128), (8 * E, 128), (HALF * 8, 128), (HALF * 8, 128), (3 * E, 128), (3 * E, 128)]


def start_kernel(est_ref, pack_ref, cp_ref, *faces):
    def body(o, carry):
        cp_ref[o] = est_ref[o] + pltpu.roll(est_ref[o + HALF], 64, 1)
        return carry

    lax.fori_loop(0, HALF, body, 0)
    emit_faces(cp_ref, pack_ref, faces)


def forward_planes(src_ref, z_ref, spec_ref, rows, fwd_z, fwd_y):
    group = 8

    def z_body(it, carry):
        block = src_ref[pl.ds(it * group, group)].reshape(group * rows, 128)
        z_ref[pl.ds(it * group, group), 0:rows, :] = lanes_dft(block, fwd_z).reshape(group, rows, 128)
        return carry

    lax.fori_loop(0, PLANES // group, z_body, 0)

    def y_body(it, carry):
        planes = [z_ref[it * group + j, 0:rows, :] for j in range(group)]
        for j, plane in enumerate(rows_dft(planes, fwd_y, PAD, False)):
            spec_ref[it * group + j] = plane
        return carry

    lax.fori_loop(0, PLANES // group, y_body, 0)


def filter_planes(spec_ref, kr_ref, ki_ref, out_ref, conjugate):
    group = 4
    sign = lane_sign((8, 128))
    if not conjugate:
        sign = -sign

    def body(it, carry):
        kb = it // (HALF // group)
        og = it % (HALF // group)
        rows = pl.ds(pl.multiple_of(kb * 8, 8), 8)
        first = og * group
        acc_r = [jnp.zeros((8, 128), F32) for _ in range(group)]
        acc_i = [jnp.zeros((8, 128), F32) for _ in range(group)]
        for m in range(group + KS - 1):
            value = spec_ref[first + m, rows, :]
            for j in range(group):
                d = m - j
                if 0 <= d < KS:
                    tap = d if conjugate else KS - 1 - d
                    acc_r[j] = acc_r[j] + kr_ref[tap, rows, :] * value
                    acc_i[j] = acc_i[j] + ki_ref[tap, rows, :] * value
        for j in range(group):
            out_ref[first + j, rows, :] = acc_r[j] + sign * pltpu.roll(acc_i[j], 64, 1)
        return carry

    lax.fori_loop(0, 8 * (HALF // group), body, 0)


def inverse_planes(spec_ref, y_ref, out_ref, inv_y, inv_z):
    group = 8

    def y_body(it, carry):
        planes = [spec_ref[it * group + j] for j in range(group)]
        for j, plane in enumerate(rows_dft(planes, inv_y, E, True)):
            y_ref[it * group + j, 0:E, :] = plane
        return carry

    lax.fori_loop(0, HALF // group, y_body, 0)

    def z_body(it, carry):
        block = y_ref[pl.ds(it * group, group), 0:E, :].reshape(group * E, 128)
        out_ref[pl.ds(it * group, group)] = lanes_dft(block, inv_z).reshape(group, E, 128)
        return carry

    lax.fori_loop(0, HALF // group, z_body, 0)


def update_kernel(
    last,
    flags_ref,
    cp_ref,
    obs_ref,
    taps_ref,
    hxm_ref,
    hxp_ref,
    hym_ref,
    hyp_ref,
    hzm_ref,
    hzp_ref,
    fwd_z_ref,
    inv_z_ref,
    tap_z_ref,
    fwd_y_ref,
    fwd_yc_ref,
    inv_y_ref,
    tap_y_ref,
    pack_ref,
    place_ref,
    *refs,
):
    if last:
        out_ref, refs = refs[0], refs[1:]
        faces = ()
    else:
        new_ref, faces, refs = refs[0], refs[1:7], refs[7:]
    ext_ref, pp_ref, z_ref, spec_ref, kr_ref, ki_ref, fil_ref, core_ref, q_ref = refs
    low_core = low_lanes((E, 128))
    low_full = low_lanes((PAD, 128))

    def tap_body(d, carry):
        zt = lanes_dft(taps_ref[d], tap_z_ref[...])
        spec = rows_dft([zt], tap_y_ref[...], PAD, False)[0]
        other = pltpu.roll(spec, 64, 1)
        kr_ref[d] = jnp.where(low_full, spec, other)
        ki_ref[d] = jnp.where(low_full, other, spec)
        return carry

    lax.fori_loop(0, KS, tap_body, 0)

    def face(ref, f):
        return ref[...].astype(F32) * flags_ref[1 + f].astype(F32)

    ext_ref[:, 0:8, :] = face(hym_ref, 2).reshape(HALF, 8, 128)
    ext_ref[:, 56:64, :] = face(hyp_ref, 3).reshape(HALF, 8, 128)
    flag_zm = flags_ref[5].astype(F32)
    flag_zp = flags_ref[6].astype(F32)
    for g in range(3):
        zm = dot(hzm_ref[g * E : (g + 1) * E, :], place_ref[0])
        zp = dot(hzp_ref[g * E : (g + 1) * E, :], place_ref[1])
        for p in range(8):
            lanes = slice(p * 128, (p + 1) * 128)
            ext_ref[g * 8 + p, 8:56, :] = cp_ref[g * 8 + p] + flag_zm * zm[:, lanes] + flag_zp * zp[:, lanes]
    xm = face(hxm_ref, 0).reshape(8, E, 128)
    xp = face(hxp_ref, 1).reshape(8, E, 128)
    pp_ref[8:32] = ext_ref[...]
    for j in range(8):
        for rows in (slice(0, 8), slice(56, 64)):
            near = ext_ref[16 + j, rows, :]
            pp_ref[j, rows, :] = pltpu.roll(jnp.where(low_lanes((8, 128)), near, 0.0), 64, 1)
            near = ext_ref[j, rows, :]
            pp_ref[32 + j, rows, :] = pltpu.roll(jnp.where(low_lanes((8, 128)), 0.0, near), 64, 1)
        pp_ref[j, 8:56, :] = pltpu.roll(jnp.where(low_core, ext_ref[16 + j, 8:56, :], xm[j]), 64, 1)
        pp_ref[32 + j, 8:56, :] = pltpu.roll(jnp.where(low_core, xp[j], ext_ref[j, 8:56, :]), 64, 1)

    forward_planes(pp_ref, z_ref, spec_ref, PAD, fwd_z_ref[...], fwd_y_ref[...])
    filter_planes(spec_ref, kr_ref, ki_ref, fil_ref, False)
    inverse_planes(fil_ref, z_ref, core_ref, inv_y_ref[...], inv_z_ref[...])

    lane = lax.broadcasted_iota(jnp.int32, (E, 128), 1) % 64
    inside = (lane >= MARGIN) & (lane < MARGIN + E)

    def ratio_body(o, carry):
        seen = obs_ref[o].astype(F32) + pltpu.roll(obs_ref[o + HALF].astype(F32), 64, 1)
        q_ref[o + 8] = jnp.where(inside, seen / jnp.where(inside, core_ref[o], 1.0), 0.0)
        return carry

    lax.fori_loop(0, HALF, ratio_body, 0)
    for j in range(8):
        q_ref[j] = pltpu.roll(jnp.where(low_core, q_ref[24 + j], 0.0), 64, 1)
        q_ref[32 + j] = pltpu.roll(jnp.where(low_core, 0.0, q_ref[8 + j]), 64, 1)

    forward_planes(q_ref, z_ref, spec_ref, E, fwd_z_ref[...], fwd_yc_ref[...])
    filter_planes(spec_ref, kr_ref, ki_ref, fil_ref, True)
    inverse_planes(fil_ref, z_ref, core_ref, inv_y_ref[...], inv_z_ref[...])

    alive = flags_ref[0] > 0

    def finish(o, carry):
        old = cp_ref[o]
        new = jnp.where(jnp.logical_and(inside, alive), old * core_ref[o], old)
        if last:
            out_ref[o] = new
            out_ref[o + HALF] = pltpu.roll(new, 64, 1)
        else:
            new_ref[o] = new
        return carry

    lax.fori_loop(0, HALF, finish, 0)
    if not last:
        emit_faces(new_ref, pack_ref, faces)


VMEM = pl.BlockSpec(memory_space=pltpu.VMEM)
SMEM = pl.BlockSpec(memory_space=pltpu.SMEM)


def start_call(est):
    return pl.pallas_call(
        start_kernel,
        out_shape=[jax.ShapeDtypeStruct((HALF, E, 128), F32)]
        + [jax.ShapeDtypeStruct(s, BF16) for s in FACE_SHAPES],
        in_specs=[VMEM] * 2,
        out_specs=[VMEM] * 7,
        name="start",
    )(est, jnp.asarray(TABLES["pack"]))


def fwd_y_core():
    full = TABLES["fwd_y"]
    return np.concatenate([full[:, s * PAD + MARGIN : s * PAD + MARGIN + E] for s in range(4)], axis=1)


def update_call(last, flags, cp, obs, taps, halos):
    if last:
        out_shape = jax.ShapeDtypeStruct((E, E, 128), F32)
        out_specs = VMEM
    else:
        out_shape = [jax.ShapeDtypeStruct((HALF, E, 128), F32)] + [
            jax.ShapeDtypeStruct(s, BF16) for s in FACE_SHAPES
        ]
        out_specs = [VMEM] * 7
    tables = [
        TABLES["fwd_z"],
        TABLES["inv_z"],
        TABLES["tap_z"],
        TABLES["fwd_y"],
        fwd_y_core(),
        TABLES["inv_y"],
        TABLES["tap_y"],
        TABLES["pack"],
        TABLES["place"],
    ]
    return pl.pallas_call(
        functools.partial(update_kernel, last),
        out_shape=out_shape,
        in_specs=[SMEM] + [VMEM] * (9 + len(tables)),
        out_specs=out_specs,
        scratch_shapes=[
            pltpu.VMEM((HALF, PAD, 128), F32),
            pltpu.VMEM((PLANES, PAD, 128), F32),
            pltpu.VMEM((PLANES, PAD, 128), F32),
            pltpu.VMEM((PLANES, PAD, 128), F32),
            pltpu.VMEM((KS, PAD, 128), F32),
            pltpu.VMEM((KS, PAD, 128), F32),
            pltpu.VMEM((HALF, PAD, 128), F32),
            pltpu.VMEM((HALF, E, 128), F32),
            pltpu.VMEM((PLANES, E, 128), F32),
        ],
        name="update_last" if last else "update",
    )(flags, cp, obs, taps, *halos, *[jnp.asarray(t) for t in tables])


GRID = (4, 4, 8)


def coords_of(b):
    return (
        b % 2 + 2 * ((b // 8) % 2),
        (b // 2) % 2 + 2 * ((b // 16) % 2),
        (b // 64) % 2 + 2 * ((b // 4) % 2) + 4 * ((b // 32) % 2),
    )


def block_at(c):
    return (
        c[0] % 2 + 2 * (c[1] % 2) + 4 * ((c[2] // 2) % 2) + 8 * (c[0] // 2) + 16 * (c[1] // 2)
        + 32 * (c[2] // 4) + 64 * (c[2] % 2)
    )


def neighbour_of(b, axis, step):
    c = list(coords_of(b))
    c[axis] = (c[axis] + step + GRID[axis]) % GRID[axis]
    return block_at(c)


MESH = pl.DeviceIdType.MESH
NEAR = 8
FAR = 16
CELLROWS = 40


def greet(peers):
    barrier = pltpu.get_barrier_semaphore()
    for peer in peers:
        pl.semaphore_signal(barrier, inc=1, device_id=(peer,), device_id_type=MESH)
    pl.semaphore_wait(barrier, len(peers))


def near_peers(me):
    base = me // NEAR * NEAR
    return [base + (me % NEAR + s) % NEAR for s in range(1, NEAR)]


def far_peers(me):
    return [(me // NEAR + s) % FAR * NEAR + me % NEAR for s in range(1, FAR)]


def face_peers(me):
    return [neighbour_of(me, f // 2, -1 if f % 2 == 0 else 1) for f in range(6)]


def face_copies(faces, halos, peers, send, recv):
    return [
        pltpu.make_async_remote_copy(
            src_ref=faces[f],
            dst_ref=halos[f ^ 1],
            send_sem=send.at[f],
            recv_sem=recv.at[f],
            device_id=(peers[f],),
            device_id_type=MESH,
        )
        for f in range(6)
    ]


def gather_kernel(cells_ref, weights_ref, *refs):
    faces, refs = refs[:6], refs[6:]
    cells_out, weights_out, halos, refs = refs[0], refs[1], refs[2:8], refs[8:]
    own_sem, near_send, near_recv, far_send, far_recv, face_send, face_recv = refs
    me = lax.axis_index("blk")
    near, far, across = near_peers(me), far_peers(me), face_peers(me)
    greet(near + far + across)
    copies = []
    for s, peer in enumerate(near):
        copies.append(
            pltpu.make_async_remote_copy(
                src_ref=cells_ref,
                dst_ref=cells_out.at[me % NEAR],
                send_sem=near_send.at[s],
                recv_sem=near_recv.at[s],
                device_id=(peer,),
                device_id_type=MESH,
            )
        )
    for s, peer in enumerate(far):
        copies.append(
            pltpu.make_async_remote_copy(
                src_ref=weights_ref,
                dst_ref=weights_out.at[me // NEAR],
                send_sem=far_send.at[s],
                recv_sem=far_recv.at[s],
                device_id=(peer,),
                device_id_type=MESH,
            )
        )
    copies += face_copies(faces, halos, across, face_send, face_recv)
    copies.append(pltpu.make_async_copy(cells_ref, cells_out.at[me % NEAR], own_sem.at[0]))
    copies.append(pltpu.make_async_copy(weights_ref, weights_out.at[me // NEAR], own_sem.at[1]))
    for copy in copies:
        copy.start()
    for copy in copies:
        copy.wait()


def blend_kernel(cell_row_ref, cells_ref, weights_ref, out_ref, scaled_ref):
    me = lax.axis_index("blk")
    base = me // NEAR * NEAR
    row = base + lax.broadcasted_iota(jnp.int32, (NEAR, 128), 0)
    pick = (cell_row_ref[...] == row).astype(F32)
    for a in range(NEAR):
        for u in range(UPDATES):
            rows = slice(u * CELLROWS, (u + 1) * CELLROWS)
            cell = cells_ref[a, rows, :]
            total = jnp.sum(jnp.sum(cell, axis=0, keepdims=True), axis=1, keepdims=True)
            scaled_ref[a, rows, :] = cell / total

    def body(dest, carry):
        for u in range(UPDATES):
            rows = slice(u * CELLROWS, (u + 1) * CELLROWS)
            share = jnp.sum(weights_ref[dest, u : u + 1, :] * pick, axis=1, keepdims=True)
            total = share[0:1, :] * scaled_ref[0, rows, :]
            for a in range(1, NEAR):
                total = total + share[a : a + 1, :] * scaled_ref[a, rows, :]
            out_ref[dest, rows, :] = total
        return carry

    lax.fori_loop(0, FAR, body, 0)


def collect_kernel(parts_ref, out_ref, held_ref, send, recv):
    me = lax.axis_index("blk")
    far = far_peers(me)
    greet(far)
    copies = []
    for s, peer in enumerate(far):
        copies.append(
            pltpu.make_async_remote_copy(
                src_ref=parts_ref.at[(me // NEAR + 1 + s) % FAR],
                dst_ref=held_ref.at[s],
                send_sem=send.at[s],
                recv_sem=recv.at[s],
                device_id=(peer,),
                device_id_type=MESH,
            )
        )
    for copy in copies:
        copy.start()
    total = parts_ref[me // NEAR]
    for s, copy in enumerate(copies):
        copy.wait()
        total = total + held_ref[s]
    out_ref[...] = total


def faces_kernel(*refs):
    faces, halos, (send, recv) = refs[:6], refs[6:12], refs[12:]
    across = face_peers(lax.axis_index("blk"))
    greet(across)
    copies = face_copies(faces, halos, across, send, recv)
    for copy in copies:
        copy.start()
    for copy in copies:
        copy.wait()


HALO_SHAPES = [jax.ShapeDtypeStruct(FACE_SHAPES[f ^ 1], BF16) for f in range(6)]
DMA = pltpu.SemaphoreType.DMA
ROWS = UPDATES * CELLROWS


def gather_call(cells, weights, faces):
    result = pl.pallas_call(
        gather_kernel,
        out_shape=[
            jax.ShapeDtypeStruct((NEAR, ROWS, 128), F32),
            jax.ShapeDtypeStruct((FAR, 8, 128), F32),
        ]
        + HALO_SHAPES,
        in_specs=[VMEM] * 8,
        out_specs=[VMEM] * 8,
        scratch_shapes=[
            DMA((2,)),
            DMA((NEAR - 1,)),
            DMA((NEAR - 1,)),
            DMA((FAR - 1,)),
            DMA((FAR - 1,)),
            DMA((6,)),
            DMA((6,)),
        ],
        compiler_params=pltpu.CompilerParams(collective_id=0, has_side_effects=True),
        name="gather",
    )(cells, weights, *faces)
    return result[0], result[1], result[2:]


def blend_call(cell_row, cells, weights):
    return pl.pallas_call(
        blend_kernel,
        out_shape=jax.ShapeDtypeStruct((FAR, ROWS, 128), F32),
        in_specs=[VMEM] * 3,
        out_specs=VMEM,
        scratch_shapes=[pltpu.VMEM((NEAR, ROWS, 128), F32)],
        name="blend",
    )(cell_row.reshape(1, 128), cells, weights)


def collect_call(parts):
    return pl.pallas_call(
        collect_kernel,
        out_shape=jax.ShapeDtypeStruct((ROWS, 128), F32),
        in_specs=[VMEM],
        out_specs=VMEM,
        scratch_shapes=[pltpu.VMEM((FAR - 1, ROWS, 128), F32), DMA((FAR - 1,)), DMA((FAR - 1,))],
        compiler_params=pltpu.CompilerParams(collective_id=1, has_side_effects=True),
        name="collect",
    )(parts)


def faces_call(faces):
    return pl.pallas_call(
        faces_kernel,
        out_shape=HALO_SHAPES,
        in_specs=[VMEM] * 6,
        out_specs=[VMEM] * 6,
        scratch_shapes=[DMA((6,)), DMA((6,))],
        compiler_params=pltpu.CompilerParams(collective_id=2, has_side_effects=True),
        name="faces",
    )(*faces)


def local(
    estimate, observed, psf_cells, tissue, neighbours, psf_list, psf_blend, cell_row, view_order
):
    flags = jnp.concatenate([tissue, (neighbours[0] >= 0).astype(jnp.int32)])
    est = jnp.pad(estimate.reshape(E, E, E), ((0, 0), (0, 0), (8, 72)))
    views = view_order[:UPDATES]
    lists = psf_list[0][views]
    blend = psf_blend[0][views]
    blend = blend / jnp.sum(blend, axis=1, keepdims=True)
    number = jnp.arange(128, dtype=jnp.int32)
    weights = jnp.sum(
        jnp.where(lists[:, :, None] == number[None, None, :], blend[:, :, None], 0.0), axis=1
    )
    weights = jnp.pad(weights, ((0, 8 - UPDATES), (0, 0)))
    cells = jnp.concatenate(
        [
            lax.dynamic_index_in_dim(psf_cells[0], view_order[u], 0, keepdims=False)
            for u in range(UPDATES)
        ]
    ).reshape(UPDATES, KS3)
    cells = jnp.pad(cells, ((0, 0), (0, CELLROWS * 128 - KS3))).reshape(ROWS, 128)
    seen = []
    for update in range(UPDATES):
        obs = lax.dynamic_index_in_dim(observed, view_order[update], 1, keepdims=False)
        seen.append(jnp.pad(obs.reshape(E, E, E), ((0, 0), (0, 0), (8, 72))))
    cp, *faces = start_call(est)
    gathered, shares, halos = gather_call(cells, weights, faces)
    kernel = collect_call(blend_call(cell_row, gathered, shares))
    taps = kernel.reshape(UPDATES, CELLROWS * 128)[:, :KS3].reshape(UPDATES, KS, KS, KS)
    taps = jnp.pad(taps, ((0, 0), (0, 0), (0, TAPROWS - KS), (0, 128 - KS)))
    cp, *faces = update_call(False, flags, cp, seen[0], taps[0], halos)
    halos = faces_call(faces)
    result = update_call(True, flags, cp, seen[1], taps[1], halos)
    return result[:, :, 8:56].reshape(1, E3)


def solution(mesh):
    return jax.shard_map(
        local,
        mesh=mesh,
        in_specs=(
            P("blk", None),
            P("blk", None, None),
            P("blk", None, None),
            P("blk"),
            P("blk", None),
            P("blk", None, None),
            P("blk", None, None),
            P(),
            P(),
        ),
        out_specs=P("blk", None),
        check_vma=False,
    )
```

```python
import functools
import math

import jax
import jax.numpy as jnp
import numpy as np
from jax import lax
from jax.experimental import pallas as pl
from jax.experimental.pallas import tpu as pltpu
from jax.sharding import PartitionSpec as P

E = 48
MARGIN = 8
UPDATES = 2
PAD = 64
KS = 17
E3 = 110592
KS3 = 4913
HALF = 24
PLANES = 40
TAPROWS = 32

F32 = jnp.float32
BF16 = jnp.bfloat16


def split_np(table):
    hi = np.asarray(table, np.float32).astype(jnp.bfloat16)
    lo = (np.asarray(table, np.float64) - hi.astype(np.float64)).astype(np.float32).astype(jnp.bfloat16)
    return hi, lo


def lane_table(table):
    hi, lo = split_np(table)
    row = np.concatenate([hi, lo], axis=1)
    return np.concatenate([row, row], axis=0)


def row_table(table):
    hi, lo = split_np(table)
    return np.concatenate([hi, hi, lo, lo], axis=1)


def make_tables():
    step = 2.0 * math.pi / PAD
    k = np.arange(PAD)
    ang = (k[:, None] * k[None, :] % PAD) * step
    cos, sin = np.cos(ang), np.sin(ang)
    fwd_z = np.block([[cos, -sin], [sin, cos]])
    inv_z = np.block([[cos, sin], [-sin, cos]]) / PAD
    fwd_y = np.concatenate([cos, sin], axis=0)
    inv_y = np.concatenate([cos[MARGIN : MARGIN + E], sin[MARGIN : MARGIN + E]], axis=0) / PAD
    t = np.arange(KS) - MARGIN
    ang_t = (t[:, None] * k[None, :]) % PAD * step
    tap_z = np.zeros((128, 128))
    tap_z[:KS, :PAD] = np.cos(ang_t)
    tap_z[:KS, PAD:] = -np.sin(ang_t)
    tap_y = np.zeros((128, TAPROWS))
    tap_y[:PAD, :KS] = np.cos(ang_t).T
    tap_y[PAD:, :KS] = np.sin(ang_t).T
    pack = np.zeros((2, 8 * 128, 128), np.float32)
    place = np.zeros((2, 128, 8 * 128), np.float32)
    for p in range(8):
        for s in range(2):
            for z in range(MARGIN):
                slot = p * 16 + s * 8 + z
                pack[0, p * 128 + s * 64 + MARGIN + z, slot] = 1
                pack[1, p * 128 + s * 64 + E + z, slot] = 1
                place[0, slot, p * 128 + s * 64 + z] = 1
                place[1, slot, p * 128 + s * 64 + MARGIN + E + z] = 1
    return dict(
        fwd_z=lane_table(fwd_z),
        inv_z=lane_table(inv_z),
        tap_z=lane_table(tap_z),
        fwd_y=row_table(fwd_y),
        inv_y=row_table(inv_y),
        tap_y=row_table(tap_y),
        pack=pack.astype(jnp.bfloat16),
        place=place.astype(jnp.bfloat16),
    )


TABLES = make_tables()


def split(values):
    hi = values.astype(BF16)
    lo = (values - hi.astype(F32)).astype(BF16)
    return hi, lo


def low_lanes(shape):
    return lax.broadcasted_iota(jnp.int32, shape, len(shape) - 1) < 64


def lane_sign(shape):
    return jnp.where(low_lanes(shape), 1.0, -1.0).astype(F32)


def dot(a, b):
    return lax.dot_general(a, b, (((1,), (0,)), ((), ())), preferred_element_type=F32)


def lanes_dft(rows, table):
    hi, lo = split(rows)
    both = dot(jnp.concatenate([hi, lo], axis=1), table)
    return both[:, :128] + both[:, 128:]


def rows_dft(planes, table, count, inverse):
    sign = lane_sign((count, 128))
    if inverse:
        sign = -sign
    out = []
    for a in range(0, len(planes), 2):
        cols = []
        for plane in planes[a : a + 2]:
            hi, lo = split(plane)
            cols.append(jnp.concatenate([hi, lo, hi, lo], axis=0))
        rhs = jnp.concatenate(cols, axis=1) if len(cols) > 1 else cols[0]
        both = dot(table, rhs)
        for b in range(len(cols)):
            c_part = both[:count, b * 128 : (b + 1) * 128]
            s_part = both[count : 2 * count, b * 128 : (b + 1) * 128]
            out.append(c_part + sign * pltpu.roll(s_part, 64, 1))
    return out


def emit_faces(cp_ref, pack_ref, faces):
    xm_ref, xp_ref, ym_ref, yp_ref, zm_ref, zp_ref = faces
    xm_ref[...] = cp_ref[0:8].reshape(8 * E, 128).astype(BF16)
    xp_ref[...] = cp_ref[16:24].reshape(8 * E, 128).astype(BF16)
    ym_ref[...] = cp_ref[:, 0:8, :].reshape(HALF * 8, 128).astype(BF16)
    yp_ref[...] = cp_ref[:, E - 8 : E, :].reshape(HALF * 8, 128).astype(BF16)
    for g in range(3):
        wide = jnp.concatenate([cp_ref[g * 8 + p].astype(BF16) for p in range(8)], axis=1)
        zm_ref[g * E : (g + 1) * E, :] = dot(wide, pack_ref[0]).astype(BF16)
        zp_ref[g * E : (g + 1) * E, :] = dot(wide, pack_ref[1]).astype(BF16)


FACE_SHAPES = [(8 * E, 128), (8 * E, 128), (HALF * 8, 128), (HALF * 8, 128), (3 * E, 128), (3 * E, 128)]


def start_kernel(est_ref, pack_ref, cp_ref, *faces):
    def body(o, carry):
        cp_ref[o] = est_ref[o] + pltpu.roll(est_ref[o + HALF], 64, 1)
        return carry

    lax.fori_loop(0, HALF, body, 0)
    emit_faces(cp_ref, pack_ref, faces)


def forward_planes(src_ref, z_ref, spec_ref, rows, fwd_z_ref, fwd_y_ref):
    group = 20

    def z_body(it, carry):
        block = src_ref[pl.ds(it * group, group)].reshape(group * rows, 128)
        z_ref[pl.ds(it * group, group), 0:rows, :] = lanes_dft(block, fwd_z_ref[...]).reshape(group, rows, 128)
        return carry

    lax.fori_loop(0, PLANES // group, z_body, 0)

    def y_body(it, carry):
        planes = [z_ref[it * group + j, 0:rows, :] for j in range(group)]
        for j, plane in enumerate(rows_dft(planes, fwd_y_ref[...], PAD, False)):
            spec_ref[it * group + j] = plane
        return carry

    lax.fori_loop(0, PLANES // group, y_body, 0)


def filter_planes(spec_ref, kr_ref, ki_ref, out_ref, conjugate):
    group = 12
    sign = lane_sign((8, 128))
    if not conjugate:
        sign = -sign

    def body(kb, carry):
        rows = pl.ds(pl.multiple_of(kb * 8, 8), 8)
        for first in range(0, HALF, group):
            values = {}
            acc_r, acc_i = [None] * group, [None] * group
            for d in range(KS):
                tap = d if conjugate else KS - 1 - d
                kr = kr_ref[tap, rows, :]
                ki = ki_ref[tap, rows, :]
                for j in range(group):
                    m = first + j + d
                    if m not in values:
                        values[m] = spec_ref[m, rows, :]
                    if d == 0:
                        acc_r[j] = kr * values[m]
                        acc_i[j] = ki * values[m]
                    else:
                        acc_r[j] = acc_r[j] + kr * values[m]
                        acc_i[j] = acc_i[j] + ki * values[m]
            for j in range(group):
                out_ref[first + j, rows, :] = acc_r[j] + sign * pltpu.roll(acc_i[j], 64, 1)
        return carry

    lax.fori_loop(0, PAD // 8, body, 0)


def inverse_planes(spec_ref, y_ref, out_ref, inv_y_ref, inv_z_ref):
    group = 12

    def y_body(it, carry):
        planes = [spec_ref[it * group + j] for j in range(group)]
        for j, plane in enumerate(rows_dft(planes, inv_y_ref[...], E, True)):
            y_ref[it * group + j, 0:E, :] = plane
        return carry

    lax.fori_loop(0, HALF // group, y_body, 0)

    def z_body(it, carry):
        block = y_ref[pl.ds(it * group, group), 0:E, :].reshape(group * E, 128)
        out_ref[pl.ds(it * group, group)] = lanes_dft(block, inv_z_ref[...]).reshape(group, E, 128)
        return carry

    lax.fori_loop(0, HALF // group, z_body, 0)


def update_kernel(
    last,
    flags_ref,
    cp_ref,
    obs_ref,
    taps_ref,
    hxm_ref,
    hxp_ref,
    hym_ref,
    hyp_ref,
    hzm_ref,
    hzp_ref,
    fwd_z_ref,
    inv_z_ref,
    tap_z_ref,
    fwd_y_ref,
    fwd_yc_ref,
    inv_y_ref,
    tap_y_ref,
    pack_ref,
    place_ref,
    *refs,
):
    if last:
        out_ref, refs = refs[0], refs[1:]
        faces = ()
    else:
        new_ref, faces, refs = refs[0], refs[1:7], refs[7:]
    ext_ref, pp_ref, z_ref, spec_ref, kr_ref, ki_ref, fil_ref, core_ref, q_ref = refs
    low_core = low_lanes((E, 128))
    low_full = low_lanes((PAD, 128))

    rows = lanes_dft(taps_ref[...].reshape(KS * TAPROWS, 128), tap_z_ref[...])
    z_ref[0:KS, 0:TAPROWS, :] = rows.reshape(KS, TAPROWS, 128)
    planes = [z_ref[d, 0:TAPROWS, :] for d in range(KS)]
    for d, spec in enumerate(rows_dft(planes, tap_y_ref[...], PAD, False)):
        other = pltpu.roll(spec, 64, 1)
        kr_ref[d] = jnp.where(low_full, spec, other)
        ki_ref[d] = jnp.where(low_full, other, spec)

    def face(ref, f):
        return ref[...].astype(F32) * flags_ref[1 + f].astype(F32)

    ext_ref[:, 0:8, :] = face(hym_ref, 2).reshape(HALF, 8, 128)
    ext_ref[:, 56:64, :] = face(hyp_ref, 3).reshape(HALF, 8, 128)
    flag_zm = flags_ref[5].astype(F32)
    flag_zp = flags_ref[6].astype(F32)
    for g in range(3):
        zm = dot(hzm_ref[g * E : (g + 1) * E, :], place_ref[0])
        zp = dot(hzp_ref[g * E : (g + 1) * E, :], place_ref[1])
        for p in range(8):
            lanes = slice(p * 128, (p + 1) * 128)
            ext_ref[g * 8 + p, 8:56, :] = cp_ref[g * 8 + p] + flag_zm * zm[:, lanes] + flag_zp * zp[:, lanes]
    xm = face(hxm_ref, 0).reshape(8, E, 128)
    xp = face(hxp_ref, 1).reshape(8, E, 128)
    pp_ref[8:32] = ext_ref[...]
    for j in range(8):
        for rows in (slice(0, 8), slice(56, 64)):
            near = ext_ref[16 + j, rows, :]
            pp_ref[j, rows, :] = pltpu.roll(jnp.where(low_lanes((8, 128)), near, 0.0), 64, 1)
            near = ext_ref[j, rows, :]
            pp_ref[32 + j, rows, :] = pltpu.roll(jnp.where(low_lanes((8, 128)), 0.0, near), 64, 1)
        pp_ref[j, 8:56, :] = pltpu.roll(jnp.where(low_core, ext_ref[16 + j, 8:56, :], xm[j]), 64, 1)
        pp_ref[32 + j, 8:56, :] = pltpu.roll(jnp.where(low_core, xp[j], ext_ref[j, 8:56, :]), 64, 1)

    forward_planes(pp_ref, z_ref, spec_ref, PAD, fwd_z_ref, fwd_y_ref)
    filter_planes(spec_ref, kr_ref, ki_ref, fil_ref, False)
    inverse_planes(fil_ref, z_ref, core_ref, inv_y_ref, inv_z_ref)

    lane = lax.broadcasted_iota(jnp.int32, (E, 128), 1) % 64
    inside = (lane >= MARGIN) & (lane < MARGIN + E)

    def ratio_body(it, carry):
        for o in [it * 4 + j for j in range(4)]:
            seen = obs_ref[o].astype(F32) + pltpu.roll(obs_ref[o + HALF].astype(F32), 64, 1)
            q_ref[o + 8] = jnp.where(inside, seen / jnp.where(inside, core_ref[o], 1.0), 0.0)
        return carry

    lax.fori_loop(0, HALF // 4, ratio_body, 0)
    for j in range(8):
        q_ref[j] = pltpu.roll(jnp.where(low_core, q_ref[24 + j], 0.0), 64, 1)
        q_ref[32 + j] = pltpu.roll(jnp.where(low_core, 0.0, q_ref[8 + j]), 64, 1)

    forward_planes(q_ref, z_ref, spec_ref, E, fwd_z_ref, fwd_yc_ref)
    filter_planes(spec_ref, kr_ref, ki_ref, fil_ref, True)
    inverse_planes(fil_ref, z_ref, core_ref, inv_y_ref, inv_z_ref)

    alive = flags_ref[0] > 0

    def finish(it, carry):
        for o in [it * 4 + j for j in range(4)]:
            old = cp_ref[o]
            new = jnp.where(jnp.logical_and(inside, alive), old * core_ref[o], old)
            if last:
                out_ref[o] = new
                out_ref[o + HALF] = pltpu.roll(new, 64, 1)
            else:
                new_ref[o] = new
        return carry

    lax.fori_loop(0, HALF // 4, finish, 0)
    if not last:
        emit_faces(new_ref, pack_ref, faces)


VMEM = pl.BlockSpec(memory_space=pltpu.VMEM)
SMEM = pl.BlockSpec(memory_space=pltpu.SMEM)


def start_call(est):
    return pl.pallas_call(
        start_kernel,
        out_shape=[jax.ShapeDtypeStruct((HALF, E, 128), F32)]
        + [jax.ShapeDtypeStruct(s, BF16) for s in FACE_SHAPES],
        in_specs=[VMEM] * 2,
        out_specs=[VMEM] * 7,
        name="start",
    )(est, jnp.asarray(TABLES["pack"]))


def fwd_y_core():
    full = TABLES["fwd_y"]
    return np.concatenate([full[:, s * PAD + MARGIN : s * PAD + MARGIN + E] for s in range(4)], axis=1)


def update_call(last, flags, cp, obs, taps, halos):
    if last:
        out_shape = jax.ShapeDtypeStruct((E, E, 128), F32)
        out_specs = VMEM
    else:
        out_shape = [jax.ShapeDtypeStruct((HALF, E, 128), F32)] + [
            jax.ShapeDtypeStruct(s, BF16) for s in FACE_SHAPES
        ]
        out_specs = [VMEM] * 7
    tables = [
        TABLES["fwd_z"],
        TABLES["inv_z"],
        TABLES["tap_z"],
        TABLES["fwd_y"],
        fwd_y_core(),
        TABLES["inv_y"],
        TABLES["tap_y"],
        TABLES["pack"],
        TABLES["place"],
    ]
    return pl.pallas_call(
        functools.partial(update_kernel, last),
        out_shape=out_shape,
        in_specs=[SMEM] + [VMEM] * (9 + len(tables)),
        out_specs=out_specs,
        scratch_shapes=[
            pltpu.VMEM((HALF, PAD, 128), F32),
            pltpu.VMEM((PLANES, PAD, 128), F32),
            pltpu.VMEM((PLANES, PAD, 128), F32),
            pltpu.VMEM((PLANES, PAD, 128), F32),
            pltpu.VMEM((KS, PAD, 128), F32),
            pltpu.VMEM((KS, PAD, 128), F32),
            pltpu.VMEM((HALF, PAD, 128), F32),
            pltpu.VMEM((HALF, E, 128), F32),
            pltpu.VMEM((PLANES, E, 128), F32),
        ],
        name="update_last" if last else "update",
    )(flags, cp, obs, taps, *halos, *[jnp.asarray(t) for t in tables])


GRID = (4, 4, 8)


def coords_of(b):
    return (
        b % 2 + 2 * ((b // 8) % 2),
        (b // 2) % 2 + 2 * ((b // 16) % 2),
        (b // 64) % 2 + 2 * ((b // 4) % 2) + 4 * ((b // 32) % 2),
    )


def block_at(c):
    return (
        c[0] % 2 + 2 * (c[1] % 2) + 4 * ((c[2] // 2) % 2) + 8 * (c[0] // 2) + 16 * (c[1] // 2)
        + 32 * (c[2] // 4) + 64 * (c[2] % 2)
    )


def neighbour_of(b, axis, step):
    c = list(coords_of(b))
    c[axis] = (c[axis] + step + GRID[axis]) % GRID[axis]
    return block_at(c)


MESH = pl.DeviceIdType.MESH
NEAR = 8
FAR = 16
CELLROWS = 40


def greet(peers):
    barrier = pltpu.get_barrier_semaphore()
    for peer in peers:
        pl.semaphore_signal(barrier, inc=1, device_id=(peer,), device_id_type=MESH)
    pl.semaphore_wait(barrier, len(peers))


def near_peers(me):
    base = me // NEAR * NEAR
    return [base + (me % NEAR + s) % NEAR for s in range(1, NEAR)]


def far_peers(me):
    return [(me // NEAR + s) % FAR * NEAR + me % NEAR for s in range(1, FAR)]


def face_peers(me):
    return [neighbour_of(me, f // 2, -1 if f % 2 == 0 else 1) for f in range(6)]


def face_copies(faces, halos, peers, send, recv):
    return [
        pltpu.make_async_remote_copy(
            src_ref=faces[f],
            dst_ref=halos[f ^ 1],
            send_sem=send.at[f],
            recv_sem=recv.at[f],
            device_id=(peers[f],),
            device_id_type=MESH,
        )
        for f in range(6)
    ]


def gather_kernel(cells_ref, weights_ref, *refs):
    faces, refs = refs[:6], refs[6:]
    cells_out, weights_out, halos, refs = refs[0], refs[1], refs[2:8], refs[8:]
    own_sem, near_send, near_recv, far_send, far_recv, face_send, face_recv = refs
    me = lax.axis_index("blk")
    near, far, across = near_peers(me), far_peers(me), face_peers(me)
    greet(near + far + across)
    copies = []
    for s, peer in enumerate(near):
        copies.append(
            pltpu.make_async_remote_copy(
                src_ref=cells_ref,
                dst_ref=cells_out.at[me % NEAR],
                send_sem=near_send.at[s],
                recv_sem=near_recv.at[s],
                device_id=(peer,),
                device_id_type=MESH,
            )
        )
    for s, peer in enumerate(far):
        copies.append(
            pltpu.make_async_remote_copy(
                src_ref=weights_ref,
                dst_ref=weights_out.at[me // NEAR],
                send_sem=far_send.at[s],
                recv_sem=far_recv.at[s],
                device_id=(peer,),
                device_id_type=MESH,
            )
        )
    copies += face_copies(faces, halos, across, face_send, face_recv)
    copies.append(pltpu.make_async_copy(cells_ref, cells_out.at[me % NEAR], own_sem.at[0]))
    copies.append(pltpu.make_async_copy(weights_ref, weights_out.at[me // NEAR], own_sem.at[1]))
    for copy in copies:
        copy.start()
    for copy in copies:
        copy.wait()


def blend_kernel(cell_row_ref, cells_ref, weights_ref, out_ref, scaled_ref):
    me = lax.axis_index("blk")
    base = me // NEAR * NEAR
    row = base + lax.broadcasted_iota(jnp.int32, (NEAR, 128), 0)
    pick = (cell_row_ref[...] == row).astype(F32)
    for a in range(NEAR):
        for u in range(UPDATES):
            rows = slice(u * CELLROWS, (u + 1) * CELLROWS)
            cell = cells_ref[a, rows, :]
            total = jnp.sum(jnp.sum(cell, axis=0, keepdims=True), axis=1, keepdims=True)
            scaled_ref[a, rows, :] = cell / total

    def body(dest, carry):
        for u in range(UPDATES):
            rows = slice(u * CELLROWS, (u + 1) * CELLROWS)
            share = jnp.sum(weights_ref[dest, u : u + 1, :] * pick, axis=1, keepdims=True)
            total = share[0:1, :] * scaled_ref[0, rows, :]
            for a in range(1, NEAR):
                total = total + share[a : a + 1, :] * scaled_ref[a, rows, :]
            out_ref[dest, rows, :] = total
        return carry

    lax.fori_loop(0, FAR, body, 0)


def collect_kernel(parts_ref, out_ref, held_ref, send, recv):
    me = lax.axis_index("blk")
    far = far_peers(me)
    greet(far)
    copies = []
    for s, peer in enumerate(far):
        copies.append(
            pltpu.make_async_remote_copy(
                src_ref=parts_ref.at[(me // NEAR + 1 + s) % FAR],
                dst_ref=held_ref.at[s],
                send_sem=send.at[s],
                recv_sem=recv.at[s],
                device_id=(peer,),
                device_id_type=MESH,
            )
        )
    for copy in copies:
        copy.start()
    total = parts_ref[me // NEAR]
    for s, copy in enumerate(copies):
        copy.wait()
        total = total + held_ref[s]
    out_ref[...] = total


def faces_kernel(*refs):
    faces, halos, (send, recv) = refs[:6], refs[6:12], refs[12:]
    across = face_peers(lax.axis_index("blk"))
    greet(across)
    copies = face_copies(faces, halos, across, send, recv)
    for copy in copies:
        copy.start()
    for copy in copies:
        copy.wait()


HALO_SHAPES = [jax.ShapeDtypeStruct(FACE_SHAPES[f ^ 1], BF16) for f in range(6)]
DMA = pltpu.SemaphoreType.DMA
ROWS = UPDATES * CELLROWS


def gather_call(cells, weights, faces):
    result = pl.pallas_call(
        gather_kernel,
        out_shape=[
            jax.ShapeDtypeStruct((NEAR, ROWS, 128), F32),
            jax.ShapeDtypeStruct((FAR, 8, 128), F32),
        ]
        + HALO_SHAPES,
        in_specs=[VMEM] * 8,
        out_specs=[VMEM] * 8,
        scratch_shapes=[
            DMA((2,)),
            DMA((NEAR - 1,)),
            DMA((NEAR - 1,)),
            DMA((FAR - 1,)),
            DMA((FAR - 1,)),
            DMA((6,)),
            DMA((6,)),
        ],
        compiler_params=pltpu.CompilerParams(collective_id=0, has_side_effects=True),
        name="gather",
    )(cells, weights, *faces)
    return result[0], result[1], result[2:]


def blend_call(cell_row, cells, weights):
    return pl.pallas_call(
        blend_kernel,
        out_shape=jax.ShapeDtypeStruct((FAR, ROWS, 128), F32),
        in_specs=[VMEM] * 3,
        out_specs=VMEM,
        scratch_shapes=[pltpu.VMEM((NEAR, ROWS, 128), F32)],
        name="blend",
    )(cell_row.reshape(1, 128), cells, weights)


def collect_call(parts):
    return pl.pallas_call(
        collect_kernel,
        out_shape=jax.ShapeDtypeStruct((ROWS, 128), F32),
        in_specs=[VMEM],
        out_specs=VMEM,
        scratch_shapes=[pltpu.VMEM((FAR - 1, ROWS, 128), F32), DMA((FAR - 1,)), DMA((FAR - 1,))],
        compiler_params=pltpu.CompilerParams(collective_id=1, has_side_effects=True),
        name="collect",
    )(parts)


def faces_call(faces):
    return pl.pallas_call(
        faces_kernel,
        out_shape=HALO_SHAPES,
        in_specs=[VMEM] * 6,
        out_specs=[VMEM] * 6,
        scratch_shapes=[DMA((6,)), DMA((6,))],
        compiler_params=pltpu.CompilerParams(collective_id=2, has_side_effects=True),
        name="faces",
    )(*faces)


def local(
    estimate, observed, psf_cells, tissue, neighbours, psf_list, psf_blend, cell_row, view_order
):
    flags = jnp.concatenate([tissue, (neighbours[0] >= 0).astype(jnp.int32)])
    est = jnp.pad(estimate.reshape(E, E, E), ((0, 0), (0, 0), (8, 72)))
    views = view_order[:UPDATES]
    lists = psf_list[0][views]
    blend = psf_blend[0][views]
    blend = blend / jnp.sum(blend, axis=1, keepdims=True)
    number = jnp.arange(128, dtype=jnp.int32)
    weights = jnp.sum(
        jnp.where(lists[:, :, None] == number[None, None, :], blend[:, :, None], 0.0), axis=1
    )
    weights = jnp.pad(weights, ((0, 8 - UPDATES), (0, 0)))
    cells = jnp.concatenate(
        [
            lax.dynamic_index_in_dim(psf_cells[0], view_order[u], 0, keepdims=False)
            for u in range(UPDATES)
        ]
    ).reshape(UPDATES, KS3)
    cells = jnp.pad(cells, ((0, 0), (0, CELLROWS * 128 - KS3))).reshape(ROWS, 128)
    seen = []
    for update in range(UPDATES):
        obs = lax.dynamic_index_in_dim(observed, view_order[update], 1, keepdims=False)
        seen.append(jnp.pad(obs.reshape(E, E, E), ((0, 0), (0, 0), (8, 72))))
    cp, *faces = start_call(est)
    gathered, shares, halos = gather_call(cells, weights, faces)
    kernel = collect_call(blend_call(cell_row, gathered, shares))
    taps = kernel.reshape(UPDATES, CELLROWS * 128)[:, :KS3].reshape(UPDATES, KS, KS, KS)
    taps = jnp.pad(taps, ((0, 0), (0, 0), (0, TAPROWS - KS), (0, 128 - KS)))
    cp, *faces = update_call(False, flags, cp, seen[0], taps[0], halos)
    halos = faces_call(faces)
    result = update_call(True, flags, cp, seen[1], taps[1], halos)
    return result[:, :, 8:56].reshape(1, E3)


def solution(mesh):
    return jax.shard_map(
        local,
        mesh=mesh,
        in_specs=(
            P("blk", None),
            P("blk", None, None),
            P("blk", None, None),
            P("blk"),
            P("blk", None),
            P("blk", None, None),
            P("blk", None, None),
            P(),
            P(),
        ),
        out_specs=P("blk", None),
        check_vma=False,
    )
```

```python
import functools
import math

import jax
import jax.numpy as jnp
import numpy as np
from jax import lax
from jax.experimental import pallas as pl
from jax.experimental.pallas import tpu as pltpu
from jax.sharding import PartitionSpec as P

E = 48
MARGIN = 8
UPDATES = 2
PAD = 64
KS = 17
E3 = 110592
KS3 = 4913
HALF = 24
PLANES = 40
TAPROWS = 32

CELLROWS = 40
ROWS = UPDATES * CELLROWS

F32 = jnp.float32
BF16 = jnp.bfloat16


def split_np(table):
    hi = np.asarray(table, np.float32).astype(jnp.bfloat16)
    lo = (np.asarray(table, np.float64) - hi.astype(np.float64)).astype(np.float32).astype(jnp.bfloat16)
    return hi, lo


def lane_table(table):
    hi, lo = split_np(table)
    row = np.concatenate([hi, lo], axis=1)
    return np.concatenate([row, row], axis=0)


def row_table(table):
    hi, lo = split_np(table)
    return np.concatenate([hi, hi, lo, lo], axis=1)


def make_tables():
    step = 2.0 * math.pi / PAD
    k = np.arange(PAD)
    ang = (k[:, None] * k[None, :] % PAD) * step
    cos, sin = np.cos(ang), np.sin(ang)
    fwd_z = np.block([[cos, -sin], [sin, cos]])
    inv_z = np.block([[cos, sin], [-sin, cos]]) / PAD
    fwd_y = np.concatenate([cos, sin], axis=0)
    inv_y = np.concatenate([cos[MARGIN : MARGIN + E], sin[MARGIN : MARGIN + E]], axis=0) / PAD
    t = np.arange(KS) - MARGIN
    ang_t = (t[:, None] * k[None, :]) % PAD * step
    tap_z = np.zeros((128, 128))
    tap_z[:KS, :PAD] = np.cos(ang_t)
    tap_z[:KS, PAD:] = -np.sin(ang_t)
    tap_y = np.zeros((128, TAPROWS))
    tap_y[:PAD, :KS] = np.cos(ang_t).T
    tap_y[PAD:, :KS] = np.sin(ang_t).T
    pack = np.zeros((2, 8 * 128, 128), np.float32)
    place = np.zeros((2, 128, 8 * 128), np.float32)
    for p in range(8):
        for s in range(2):
            for z in range(MARGIN):
                slot = p * 16 + s * 8 + z
                pack[0, p * 128 + s * 64 + MARGIN + z, slot] = 1
                pack[1, p * 128 + s * 64 + E + z, slot] = 1
                place[0, slot, p * 128 + s * 64 + z] = 1
                place[1, slot, p * 128 + s * 64 + MARGIN + E + z] = 1
    return dict(
        fwd_z=lane_table(fwd_z),
        inv_z=lane_table(inv_z),
        tap_z=lane_table(tap_z),
        fwd_y=row_table(fwd_y),
        inv_y=row_table(inv_y),
        tap_y=row_table(tap_y),
        pack=pack.astype(jnp.bfloat16),
        place=place.astype(jnp.bfloat16),
    )


TABLES = make_tables()


def split(values):
    hi = values.astype(BF16)
    lo = (values - hi.astype(F32)).astype(BF16)
    return hi, lo


def low_lanes(shape):
    return lax.broadcasted_iota(jnp.int32, shape, len(shape) - 1) < 64


def lane_sign(shape):
    return jnp.where(low_lanes(shape), 1.0, -1.0).astype(F32)


def dot(a, b):
    return lax.dot_general(a, b, (((1,), (0,)), ((), ())), preferred_element_type=F32)


def lanes_dft(rows, table):
    hi, lo = split(rows)
    both = dot(jnp.concatenate([hi, lo], axis=1), table)
    return both[:, :128] + both[:, 128:]


def rows_dft(planes, table, count, inverse):
    sign = lane_sign((count, 128))
    if inverse:
        sign = -sign
    out = []
    for a in range(0, len(planes), 2):
        cols = []
        for plane in planes[a : a + 2]:
            hi, lo = split(plane)
            cols.append(jnp.concatenate([hi, lo, hi, lo], axis=0))
        rhs = jnp.concatenate(cols, axis=1) if len(cols) > 1 else cols[0]
        both = dot(table, rhs)
        for b in range(len(cols)):
            c_part = both[:count, b * 128 : (b + 1) * 128]
            s_part = both[count : 2 * count, b * 128 : (b + 1) * 128]
            out.append(c_part + sign * pltpu.roll(s_part, 64, 1))
    return out


def emit_faces(cp_ref, pack_ref, faces):
    xm_ref, xp_ref, ym_ref, yp_ref, zm_ref, zp_ref = faces
    xm_ref[...] = cp_ref[0:8].reshape(8 * E, 128).astype(BF16)
    xp_ref[...] = cp_ref[16:24].reshape(8 * E, 128).astype(BF16)
    ym_ref[...] = cp_ref[:, 0:8, :].reshape(HALF * 8, 128).astype(BF16)
    yp_ref[...] = cp_ref[:, E - 8 : E, :].reshape(HALF * 8, 128).astype(BF16)
    for g in range(3):
        wide = jnp.concatenate([cp_ref[g * 8 + p].astype(BF16) for p in range(8)], axis=1)
        zm_ref[g * E : (g + 1) * E, :] = dot(wide, pack_ref[0]).astype(BF16)
        zp_ref[g * E : (g + 1) * E, :] = dot(wide, pack_ref[1]).astype(BF16)


FACE_SHAPES = [(8 * E, 128), (8 * E, 128), (HALF * 8, 128), (HALF * 8, 128), (3 * E, 128), (3 * E, 128)]


def flat_to_pairs(load, store):
    for j in range(8):
        total = None
        for half in range(2):
            first = 48 * j
            k, lane = first // 128, first % 128
            base = MARGIN + 64 * half
            value = load(k, half)
            part = value if lane == base else pltpu.roll(value, (base - lane) % 128, 1)
            at = lax.broadcasted_iota(jnp.int32, part.shape, 1) - base
            length = min(48, 128 - lane)
            picked = jnp.where((at >= 0) & (at < length), part, 0.0)
            if length < 48:
                more = pltpu.roll(load(k + 1, half), base + length, 1)
                picked = jnp.where((at >= length) & (at < 48), more, picked)
            total = picked if total is None else total + picked
        store(j, total)


def pairs_to_flat(load, store):
    for half in range(2):
        for k in range(3):
            total = None
            for j in range(8):
                lane = 48 * j - 128 * k
                if lane <= -48 or lane >= 128:
                    continue
                value = pltpu.roll(load(j), (lane - MARGIN - 64 * half) % 128, 1)
                at = lax.broadcasted_iota(jnp.int32, value.shape, 1) - lane
                picked = jnp.where((at >= 0) & (at < 48), value, 0.0)
                total = picked if total is None else total + picked
            store(k, half, total)


GROUPS = HALF * E // 8
FLAT = E3 // 128


def start_kernel(ints_ref, blend_ref, est_ref, cells_ref, pack_ref, *refs):
    cp_ref, flat_ref = refs[0], refs[-1]
    weights_ref, own_ref, faces = refs[1], refs[2], refs[3:9]

    def load(k, half):
        return est_ref[pl.ds(half * 3 * GROUPS + k, GROUPS, stride=3), :]

    def store(j, rows):
        flat_ref[pl.ds(j, GROUPS, stride=8), :] = rows

    flat_to_pairs(load, store)
    cp_ref[...] = flat_ref[...].reshape(HALF, E, 128)
    emit_faces(cp_ref, pack_ref, faces)

    number = lax.broadcasted_iota(jnp.int32, (1, 128), 1)
    weights_ref[...] = jnp.zeros_like(weights_ref)
    own_ref[...] = jnp.zeros_like(own_ref)
    for u in range(UPDATES):
        view = ints_ref[u]
        first = jnp.full((1, 128), blend_ref[2 * view], F32)
        second = jnp.full((1, 128), blend_ref[2 * view + 1], F32)
        total = first + second
        weights_ref[u : u + 1, :] = jnp.where(number == ints_ref[6 + 2 * view], first / total, 0.0) + jnp.where(
            number == ints_ref[7 + 2 * view], second / total, 0.0
        )
        for i in range(KS3 // 128):
            own_ref[u * CELLROWS + i : u * CELLROWS + i + 1, :] = cells_ref[view, :, i * 128 : (i + 1) * 128]
        tail = KS3 // 128 * 128
        i = u * CELLROWS + KS3 // 128
        own_ref[i : i + 1, 0 : KS3 - tail] = cells_ref[view, :, tail:KS3]


def forward_planes(src_ref, z_ref, spec_ref, rows, fwd_z_ref, fwd_y_ref):
    group = 20

    def z_body(it, carry):
        block = src_ref[pl.ds(it * group, group)].reshape(group * rows, 128)
        z_ref[pl.ds(it * group, group), 0:rows, :] = lanes_dft(block, fwd_z_ref[...]).reshape(group, rows, 128)
        return carry

    lax.fori_loop(0, PLANES // group, z_body, 0)

    def y_body(it, carry):
        planes = [z_ref[it * group + j, 0:rows, :] for j in range(group)]
        for j, plane in enumerate(rows_dft(planes, fwd_y_ref[...], PAD, False)):
            spec_ref[it * group + j] = plane
        return carry

    lax.fori_loop(0, PLANES // group, y_body, 0)


def filter_planes(spec_ref, kr_ref, ki_ref, out_ref, conjugate):
    group = 12
    sign = lane_sign((8, 128))
    if not conjugate:
        sign = -sign

    def body(kb, carry):
        rows = pl.ds(pl.multiple_of(kb * 8, 8), 8)
        for first in range(0, HALF, group):
            values = {}
            acc_r, acc_i = [None] * group, [None] * group
            for d in range(KS):
                tap = d if conjugate else KS - 1 - d
                kr = kr_ref[tap, rows, :]
                ki = ki_ref[tap, rows, :]
                for j in range(group):
                    m = first + j + d
                    if m not in values:
                        values[m] = spec_ref[m, rows, :]
                    if d == 0:
                        acc_r[j] = kr * values[m]
                        acc_i[j] = ki * values[m]
                    else:
                        acc_r[j] = acc_r[j] + kr * values[m]
                        acc_i[j] = acc_i[j] + ki * values[m]
            for j in range(group):
                out_ref[first + j, rows, :] = acc_r[j] + sign * pltpu.roll(acc_i[j], 64, 1)
        return carry

    lax.fori_loop(0, PAD // 8, body, 0)


def inverse_planes(spec_ref, y_ref, out_ref, inv_y_ref, inv_z_ref):
    group = 12

    def y_body(it, carry):
        planes = [spec_ref[it * group + j] for j in range(group)]
        for j, plane in enumerate(rows_dft(planes, inv_y_ref[...], E, True)):
            y_ref[it * group + j, 0:E, :] = plane
        return carry

    lax.fori_loop(0, HALF // group, y_body, 0)

    def z_body(it, carry):
        block = y_ref[pl.ds(it * group, group), 0:E, :].reshape(group * E, 128)
        out_ref[pl.ds(it * group, group)] = lanes_dft(block, inv_z_ref[...]).reshape(group, E, 128)
        return carry

    lax.fori_loop(0, HALF // group, z_body, 0)


def update_kernel(
    last,
    flags_ref,
    cp_ref,
    obs_ref,
    taps_ref,
    hxm_ref,
    hxp_ref,
    hym_ref,
    hyp_ref,
    hzm_ref,
    hzp_ref,
    fwd_z_ref,
    inv_z_ref,
    tap_z_ref,
    fwd_y_ref,
    fwd_yc_ref,
    inv_y_ref,
    tap_y_ref,
    pack_ref,
    place_ref,
    *refs,
):
    if last:
        out_ref, refs = refs[0], refs[1:]
        faces = ()
    else:
        new_ref, faces, refs = refs[0], refs[1:7], refs[7:]
    ext_ref, pp_ref, z_ref, spec_ref, kr_ref, ki_ref, fil_ref, core_ref, q_ref, wide_ref, flat_ref = refs
    low_core = low_lanes((E, 128))
    low_full = low_lanes((PAD, 128))

    rows = lanes_dft(taps_ref[...].reshape(KS * TAPROWS, 128), tap_z_ref[...])
    z_ref[0:KS, 0:TAPROWS, :] = rows.reshape(KS, TAPROWS, 128)
    planes = [z_ref[d, 0:TAPROWS, :] for d in range(KS)]
    for d, spec in enumerate(rows_dft(planes, tap_y_ref[...], PAD, False)):
        other = pltpu.roll(spec, 64, 1)
        kr_ref[d] = jnp.where(low_full, spec, other)
        ki_ref[d] = jnp.where(low_full, other, spec)

    def face(ref, f):
        return jnp.where(flags_ref[19 + f] >= 0, ref[...].astype(F32), 0.0)

    ext_ref[:, 0:8, :] = face(hym_ref, 2).reshape(HALF, 8, 128)
    ext_ref[:, 56:64, :] = face(hyp_ref, 3).reshape(HALF, 8, 128)
    near_zm = flags_ref[23] >= 0
    near_zp = flags_ref[24] >= 0
    for g in range(3):
        zm = dot(jnp.where(near_zm, hzm_ref[g * E : (g + 1) * E, :].astype(F32), 0.0).astype(BF16), place_ref[0])
        zp = dot(jnp.where(near_zp, hzp_ref[g * E : (g + 1) * E, :].astype(F32), 0.0).astype(BF16), place_ref[1])
        for p in range(8):
            lanes = slice(p * 128, (p + 1) * 128)
            ext_ref[g * 8 + p, 8:56, :] = cp_ref[g * 8 + p] + zm[:, lanes] + zp[:, lanes]
    xm = face(hxm_ref, 0).reshape(8, E, 128)
    xp = face(hxp_ref, 1).reshape(8, E, 128)
    pp_ref[8:32] = ext_ref[...]
    for j in range(8):
        for rows in (slice(0, 8), slice(56, 64)):
            near = ext_ref[16 + j, rows, :]
            pp_ref[j, rows, :] = pltpu.roll(jnp.where(low_lanes((8, 128)), near, 0.0), 64, 1)
            near = ext_ref[j, rows, :]
            pp_ref[32 + j, rows, :] = pltpu.roll(jnp.where(low_lanes((8, 128)), 0.0, near), 64, 1)
        pp_ref[j, 8:56, :] = pltpu.roll(jnp.where(low_core, ext_ref[16 + j, 8:56, :], xm[j]), 64, 1)
        pp_ref[32 + j, 8:56, :] = pltpu.roll(jnp.where(low_core, xp[j], ext_ref[j, 8:56, :]), 64, 1)

    forward_planes(pp_ref, z_ref, spec_ref, PAD, fwd_z_ref, fwd_y_ref)
    filter_planes(spec_ref, kr_ref, ki_ref, fil_ref, False)
    inverse_planes(fil_ref, z_ref, core_ref, inv_y_ref, inv_z_ref)

    wide_ref[...] = obs_ref[...].astype(F32)

    def load_seen(k, half):
        return wide_ref[pl.ds(half * 3 * GROUPS + k, GROUPS, stride=3), :]

    def store_seen(j, rows):
        row_ref[pl.ds(j, GROUPS, stride=8), :] = rows

    row_ref = flat_ref.reshape(HALF * E, 128)
    flat_to_pairs(load_seen, store_seen)

    lane = lax.broadcasted_iota(jnp.int32, (E, 128), 1) % 64
    inside = (lane >= MARGIN) & (lane < MARGIN + E)

    def ratio_body(it, carry):
        for o in [it * 4 + j for j in range(4)]:
            seen = flat_ref[o]
            q_ref[o + 8] = jnp.where(inside, seen / jnp.where(inside, core_ref[o], 1.0), 0.0)
        return carry

    lax.fori_loop(0, HALF // 4, ratio_body, 0)
    for j in range(8):
        q_ref[j] = pltpu.roll(jnp.where(low_core, q_ref[24 + j], 0.0), 64, 1)
        q_ref[32 + j] = pltpu.roll(jnp.where(low_core, 0.0, q_ref[8 + j]), 64, 1)

    forward_planes(q_ref, z_ref, spec_ref, E, fwd_z_ref, fwd_yc_ref)
    filter_planes(spec_ref, kr_ref, ki_ref, fil_ref, True)
    inverse_planes(fil_ref, z_ref, core_ref, inv_y_ref, inv_z_ref)

    alive = flags_ref[18] > 0

    def finish(it, carry):
        for o in [it * 4 + j for j in range(4)]:
            old = cp_ref[o]
            new = jnp.where(jnp.logical_and(inside, alive), old * core_ref[o], old)
            if last:
                flat_ref[o] = new
            else:
                new_ref[o] = new
        return carry

    lax.fori_loop(0, HALF // 4, finish, 0)
    if not last:
        emit_faces(new_ref, pack_ref, faces)
        return

    def load_new(j):
        return row_ref[pl.ds(j, GROUPS, stride=8), :]

    def store_new(k, half, rows):
        out_ref[pl.ds(half * 3 * GROUPS + k, GROUPS, stride=3), :] = rows

    pairs_to_flat(load_new, store_new)


VMEM = pl.BlockSpec(memory_space=pltpu.VMEM)
SMEM = pl.BlockSpec(memory_space=pltpu.SMEM)


def start_call(ints, blend, est, cells):
    result = pl.pallas_call(
        start_kernel,
        out_shape=[
            jax.ShapeDtypeStruct((HALF, E, 128), F32),
            jax.ShapeDtypeStruct((8, 128), F32),
            jax.ShapeDtypeStruct((ROWS, 128), F32),
        ]
        + [jax.ShapeDtypeStruct(s, BF16) for s in FACE_SHAPES],
        in_specs=[SMEM] * 2 + [VMEM] * 3,
        out_specs=[VMEM] * 9,
        scratch_shapes=[pltpu.VMEM((HALF * E, 128), F32)],
        name="start",
    )(ints, blend, est, cells, jnp.asarray(TABLES["pack"]))
    return result[0], result[1], result[2], result[3:]


def fwd_y_core():
    full = TABLES["fwd_y"]
    return np.concatenate([full[:, s * PAD + MARGIN : s * PAD + MARGIN + E] for s in range(4)], axis=1)


def update_call(last, flags, cp, obs, taps, halos):
    if last:
        out_shape = jax.ShapeDtypeStruct((FLAT, 128), F32)
        out_specs = VMEM
    else:
        out_shape = [jax.ShapeDtypeStruct((HALF, E, 128), F32)] + [
            jax.ShapeDtypeStruct(s, BF16) for s in FACE_SHAPES
        ]
        out_specs = [VMEM] * 7
    tables = [
        TABLES["fwd_z"],
        TABLES["inv_z"],
        TABLES["tap_z"],
        TABLES["fwd_y"],
        fwd_y_core(),
        TABLES["inv_y"],
        TABLES["tap_y"],
        TABLES["pack"],
        TABLES["place"],
    ]
    return pl.pallas_call(
        functools.partial(update_kernel, last),
        out_shape=out_shape,
        in_specs=[SMEM] + [VMEM] * (9 + len(tables)),
        out_specs=out_specs,
        scratch_shapes=[
            pltpu.VMEM((HALF, PAD, 128), F32),
            pltpu.VMEM((PLANES, PAD, 128), F32),
            pltpu.VMEM((PLANES, PAD, 128), F32),
            pltpu.VMEM((PLANES, PAD, 128), F32),
            pltpu.VMEM((KS, PAD, 128), F32),
            pltpu.VMEM((KS, PAD, 128), F32),
            pltpu.VMEM((HALF, PAD, 128), F32),
            pltpu.VMEM((HALF, E, 128), F32),
            pltpu.VMEM((PLANES, E, 128), F32),
            pltpu.VMEM((FLAT, 128), F32),
            pltpu.VMEM((HALF, E, 128), F32),
        ],
        name="update_last" if last else "update",
    )(flags, cp, obs, taps, *halos, *[jnp.asarray(t) for t in tables])


GRID = (4, 4, 8)


def coords_of(b):
    return (
        b % 2 + 2 * ((b // 8) % 2),
        (b // 2) % 2 + 2 * ((b // 16) % 2),
        (b // 64) % 2 + 2 * ((b // 4) % 2) + 4 * ((b // 32) % 2),
    )


def block_at(c):
    return (
        c[0] % 2 + 2 * (c[1] % 2) + 4 * ((c[2] // 2) % 2) + 8 * (c[0] // 2) + 16 * (c[1] // 2)
        + 32 * (c[2] // 4) + 64 * (c[2] % 2)
    )


def neighbour_of(b, axis, step):
    c = list(coords_of(b))
    c[axis] = (c[axis] + step + GRID[axis]) % GRID[axis]
    return block_at(c)


MESH = pl.DeviceIdType.MESH
NEAR = 8
FAR = 16


def greet(peers):
    barrier = pltpu.get_barrier_semaphore()
    for peer in peers:
        pl.semaphore_signal(barrier, inc=1, device_id=(peer,), device_id_type=MESH)
    pl.semaphore_wait(barrier, len(peers))


def near_peers(me):
    base = me // NEAR * NEAR
    return [base + (me % NEAR + s) % NEAR for s in range(1, NEAR)]


def far_peers(me):
    return [(me // NEAR + s) % FAR * NEAR + me % NEAR for s in range(1, FAR)]


def face_peers(me):
    return [neighbour_of(me, f // 2, -1 if f % 2 == 0 else 1) for f in range(6)]


def face_copies(faces, halos, peers, send, recv):
    return [
        pltpu.make_async_remote_copy(
            src_ref=faces[f],
            dst_ref=halos[f ^ 1],
            send_sem=send.at[f],
            recv_sem=recv.at[f],
            device_id=(peers[f],),
            device_id_type=MESH,
        )
        for f in range(6)
    ]


def gather_kernel(cells_ref, weights_ref, *refs):
    faces, refs = refs[:6], refs[6:]
    cells_out, weights_out, halos, refs = refs[0], refs[1], refs[2:8], refs[8:]
    own_sem, near_send, near_recv, far_send, far_recv, face_send, face_recv = refs
    me = lax.axis_index("blk")
    near, far, across = near_peers(me), far_peers(me), face_peers(me)
    greet(near + far + across)
    copies = []
    for s, peer in enumerate(near):
        copies.append(
            pltpu.make_async_remote_copy(
                src_ref=cells_ref,
                dst_ref=cells_out.at[me % NEAR],
                send_sem=near_send.at[s],
                recv_sem=near_recv.at[s],
                device_id=(peer,),
                device_id_type=MESH,
            )
        )
    for s, peer in enumerate(far):
        copies.append(
            pltpu.make_async_remote_copy(
                src_ref=weights_ref,
                dst_ref=weights_out.at[me // NEAR],
                send_sem=far_send.at[s],
                recv_sem=far_recv.at[s],
                device_id=(peer,),
                device_id_type=MESH,
            )
        )
    copies += face_copies(faces, halos, across, face_send, face_recv)
    copies.append(pltpu.make_async_copy(cells_ref, cells_out.at[me % NEAR], own_sem.at[0]))
    copies.append(pltpu.make_async_copy(weights_ref, weights_out.at[me // NEAR], own_sem.at[1]))
    for copy in copies:
        copy.start()
    for copy in copies:
        copy.wait()


def blend_kernel(cell_row_ref, cells_ref, weights_ref, out_ref, scaled_ref):
    me = lax.axis_index("blk")
    base = me // NEAR * NEAR
    row = base + lax.broadcasted_iota(jnp.int32, (NEAR, 128), 0)
    pick = (cell_row_ref[...] == row).astype(F32)
    for a in range(NEAR):
        for u in range(UPDATES):
            rows = slice(u * CELLROWS, (u + 1) * CELLROWS)
            cell = cells_ref[a, rows, :]
            total = jnp.sum(jnp.sum(cell, axis=0, keepdims=True), axis=1, keepdims=True)
            scaled_ref[a, rows, :] = cell / total

    def body(dest, carry):
        for u in range(UPDATES):
            rows = slice(u * CELLROWS, (u + 1) * CELLROWS)
            share = jnp.sum(weights_ref[dest, u : u + 1, :] * pick, axis=1, keepdims=True)
            total = share[0:1, :] * scaled_ref[0, rows, :]
            for a in range(1, NEAR):
                total = total + share[a : a + 1, :] * scaled_ref[a, rows, :]
            out_ref[dest, rows, :] = total
        return carry

    lax.fori_loop(0, FAR, body, 0)


def collect_kernel(parts_ref, out_ref, held_ref, send, recv):
    me = lax.axis_index("blk")
    far = far_peers(me)
    greet(far)
    copies = []
    for s, peer in enumerate(far):
        copies.append(
            pltpu.make_async_remote_copy(
                src_ref=parts_ref.at[(me // NEAR + 1 + s) % FAR],
                dst_ref=held_ref.at[s],
                send_sem=send.at[s],
                recv_sem=recv.at[s],
                device_id=(peer,),
                device_id_type=MESH,
            )
        )
    for copy in copies:
        copy.start()
    total = parts_ref[me // NEAR]
    for s, copy in enumerate(copies):
        copy.wait()
        total = total + held_ref[s]
    out_ref[...] = total


def faces_kernel(*refs):
    faces, halos, (send, recv) = refs[:6], refs[6:12], refs[12:]
    across = face_peers(lax.axis_index("blk"))
    greet(across)
    copies = face_copies(faces, halos, across, send, recv)
    for copy in copies:
        copy.start()
    for copy in copies:
        copy.wait()


HALO_SHAPES = [jax.ShapeDtypeStruct(FACE_SHAPES[f ^ 1], BF16) for f in range(6)]
DMA = pltpu.SemaphoreType.DMA


def gather_call(cells, weights, faces):
    result = pl.pallas_call(
        gather_kernel,
        out_shape=[
            jax.ShapeDtypeStruct((NEAR, ROWS, 128), F32),
            jax.ShapeDtypeStruct((FAR, 8, 128), F32),
        ]
        + HALO_SHAPES,
        in_specs=[VMEM] * 8,
        out_specs=[VMEM] * 8,
        scratch_shapes=[
            DMA((2,)),
            DMA((NEAR - 1,)),
            DMA((NEAR - 1,)),
            DMA((FAR - 1,)),
            DMA((FAR - 1,)),
            DMA((6,)),
            DMA((6,)),
        ],
        compiler_params=pltpu.CompilerParams(collective_id=0, has_side_effects=True),
        name="gather",
    )(cells, weights, *faces)
    return result[0], result[1], result[2:]


def blend_call(cell_row, cells, weights):
    return pl.pallas_call(
        blend_kernel,
        out_shape=jax.ShapeDtypeStruct((FAR, ROWS, 128), F32),
        in_specs=[VMEM] * 3,
        out_specs=VMEM,
        scratch_shapes=[pltpu.VMEM((NEAR, ROWS, 128), F32)],
        name="blend",
    )(cell_row.reshape(1, 128), cells, weights)


def collect_call(parts):
    return pl.pallas_call(
        collect_kernel,
        out_shape=jax.ShapeDtypeStruct((ROWS, 128), F32),
        in_specs=[VMEM],
        out_specs=VMEM,
        scratch_shapes=[pltpu.VMEM((FAR - 1, ROWS, 128), F32), DMA((FAR - 1,)), DMA((FAR - 1,))],
        compiler_params=pltpu.CompilerParams(collective_id=1, has_side_effects=True),
        name="collect",
    )(parts)


def faces_call(faces):
    return pl.pallas_call(
        faces_kernel,
        out_shape=HALO_SHAPES,
        in_specs=[VMEM] * 6,
        out_specs=[VMEM] * 6,
        scratch_shapes=[DMA((6,)), DMA((6,))],
        compiler_params=pltpu.CompilerParams(collective_id=2, has_side_effects=True),
        name="faces",
    )(*faces)


def local(
    estimate, observed, psf_cells, tissue, neighbours, psf_list, psf_blend, cell_row, view_order
):
    ints = jnp.concatenate([view_order, psf_list.reshape(12), tissue, neighbours.reshape(6)])
    cp, weights, cells, faces = start_call(
        ints, psf_blend.reshape(12), estimate.reshape(FLAT, 128), psf_cells.reshape(6, 1, KS3)
    )
    seen = [
        lax.dynamic_index_in_dim(observed[0], view_order[u].astype(jnp.uint32), 0, keepdims=False).reshape(FLAT, 128)
        for u in range(UPDATES)
    ]
    gathered, shares, halos = gather_call(cells, weights, faces)
    kernel = collect_call(blend_call(cell_row, gathered, shares))
    taps = kernel.reshape(UPDATES, CELLROWS * 128)[:, :KS3].reshape(UPDATES, KS, KS, KS)
    taps = jnp.pad(taps, ((0, 0), (0, 0), (0, TAPROWS - KS), (0, 128 - KS)))
    cp, *faces = update_call(False, ints, cp, seen[0], taps[0], halos)
    halos = faces_call(faces)
    result = update_call(True, ints, cp, seen[1], taps[1], halos)
    return result.reshape(1, E3)


def solution(mesh):
    return jax.shard_map(
        local,
        mesh=mesh,
        in_specs=(
            P("blk", None),
            P("blk", None, None),
            P("blk", None, None),
            P("blk"),
            P("blk", None),
            P("blk", None, None),
            P("blk", None, None),
            P(),
            P(),
        ),
        out_specs=P("blk", None),
        check_vma=False,
    )
```

```python
import functools
import math

import jax
import jax.numpy as jnp
import numpy as np
from jax import lax
from jax.experimental import pallas as pl
from jax.experimental.pallas import tpu as pltpu
from jax.sharding import PartitionSpec as P

E = 48
MARGIN = 8
UPDATES = 2
PAD = 64
KS = 17
E3 = 110592
KS3 = 4913
HALF = 24
PLANES = 40
TAPROWS = 32

CELLROWS = 40
ROWS = UPDATES * CELLROWS

F32 = jnp.float32
BF16 = jnp.bfloat16


def split_np(table):
    hi = np.asarray(table, np.float32).astype(jnp.bfloat16)
    lo = (np.asarray(table, np.float64) - hi.astype(np.float64)).astype(np.float32).astype(jnp.bfloat16)
    return hi, lo


def lane_table(table):
    hi, lo = split_np(table)
    row = np.concatenate([hi, lo], axis=1)
    return np.concatenate([row, row], axis=0)


def row_table(table):
    hi, lo = split_np(table)
    return np.concatenate([hi, hi, lo, lo], axis=1)


def make_tables():
    step = 2.0 * math.pi / PAD
    k = np.arange(PAD)
    ang = (k[:, None] * k[None, :] % PAD) * step
    cos, sin = np.cos(ang), np.sin(ang)
    fwd_z = np.block([[cos, -sin], [sin, cos]])
    inv_z = np.block([[cos, sin], [-sin, cos]]) / PAD
    fwd_y = np.concatenate([cos, sin], axis=0)
    inv_y = np.concatenate([cos[MARGIN : MARGIN + E], sin[MARGIN : MARGIN + E]], axis=0) / PAD
    t = np.arange(KS) - MARGIN
    ang_t = (t[:, None] * k[None, :]) % PAD * step
    tap_z = np.zeros((128, 128))
    tap_z[:KS, :PAD] = np.cos(ang_t)
    tap_z[:KS, PAD:] = -np.sin(ang_t)
    tap_y = np.zeros((128, TAPROWS))
    tap_y[:PAD, :KS] = np.cos(ang_t).T
    tap_y[PAD:, :KS] = np.sin(ang_t).T
    pack = np.zeros((2, 8 * 128, 128), np.float32)
    place = np.zeros((2, 128, 8 * 128), np.float32)
    for p in range(8):
        for s in range(2):
            for z in range(MARGIN):
                slot = p * 16 + s * 8 + z
                pack[0, p * 128 + s * 64 + MARGIN + z, slot] = 1
                pack[1, p * 128 + s * 64 + E + z, slot] = 1
                place[0, slot, p * 128 + s * 64 + z] = 1
                place[1, slot, p * 128 + s * 64 + MARGIN + E + z] = 1
    return dict(
        fwd_z=lane_table(fwd_z),
        inv_z=lane_table(inv_z),
        tap_z=lane_table(tap_z),
        fwd_y=row_table(fwd_y),
        inv_y=row_table(inv_y),
        tap_y=row_table(tap_y),
        pack=pack.astype(jnp.bfloat16),
        place=place.astype(jnp.bfloat16),
    )


TABLES = make_tables()


def split(values):
    hi = values.astype(BF16)
    lo = (values - hi.astype(F32)).astype(BF16)
    return hi, lo


def low_lanes(shape):
    return lax.broadcasted_iota(jnp.int32, shape, len(shape) - 1) < 64


def lane_sign(shape):
    return jnp.where(low_lanes(shape), 1.0, -1.0).astype(F32)


def dot(a, b):
    return lax.dot_general(a, b, (((1,), (0,)), ((), ())), preferred_element_type=F32)


def lanes_dft(rows, table):
    hi, lo = split(rows)
    both = dot(jnp.concatenate([hi, lo], axis=1), table)
    return both[:, :128] + both[:, 128:]


def rows_dft(planes, table, count, inverse):
    sign = lane_sign((count, 128))
    if inverse:
        sign = -sign
    out = []
    for a in range(0, len(planes), 2):
        cols = []
        for plane in planes[a : a + 2]:
            hi, lo = split(plane)
            cols.append(jnp.concatenate([hi, lo, hi, lo], axis=0))
        rhs = jnp.concatenate(cols, axis=1) if len(cols) > 1 else cols[0]
        both = dot(table, rhs)
        for b in range(len(cols)):
            c_part = both[:count, b * 128 : (b + 1) * 128]
            s_part = both[count : 2 * count, b * 128 : (b + 1) * 128]
            out.append(c_part + sign * pltpu.roll(s_part, 64, 1))
    return out


def emit_faces(cp_ref, pack_ref, faces):
    xm_ref, xp_ref, ym_ref, yp_ref, zm_ref, zp_ref = faces
    low = low_lanes((E, 128))
    for j in range(4):
        near = jnp.where(low, cp_ref[j], pltpu.roll(cp_ref[4 + j], 64, 1))
        xm_ref[j * E : (j + 1) * E, :] = near.astype(BF16)
        near = jnp.where(low, pltpu.roll(cp_ref[16 + j], 64, 1), cp_ref[20 + j])
        xp_ref[j * E : (j + 1) * E, :] = near.astype(BF16)
    ym_ref[...] = cp_ref[:, 0:8, :].reshape(HALF * 8, 128).astype(BF16)
    yp_ref[...] = cp_ref[:, E - 8 : E, :].reshape(HALF * 8, 128).astype(BF16)
    for g in range(3):
        wide = jnp.concatenate([cp_ref[g * 8 + p].astype(BF16) for p in range(8)], axis=1)
        zm_ref[g * E : (g + 1) * E, :] = dot(wide, pack_ref[0]).astype(BF16)
        zp_ref[g * E : (g + 1) * E, :] = dot(wide, pack_ref[1]).astype(BF16)


FACE_SHAPES = [(4 * E, 128), (4 * E, 128), (HALF * 8, 128), (HALF * 8, 128), (3 * E, 128), (3 * E, 128)]


def flat_to_pairs(load, store):
    for j in range(8):
        total = None
        for half in range(2):
            first = 48 * j
            k, lane = first // 128, first % 128
            base = MARGIN + 64 * half
            value = load(k, half)
            part = value if lane == base else pltpu.roll(value, (base - lane) % 128, 1)
            at = lax.broadcasted_iota(jnp.int32, part.shape, 1) - base
            length = min(48, 128 - lane)
            picked = jnp.where((at >= 0) & (at < length), part, 0.0)
            if length < 48:
                more = pltpu.roll(load(k + 1, half), base + length, 1)
                picked = jnp.where((at >= length) & (at < 48), more, picked)
            total = picked if total is None else total + picked
        store(j, total)


def pairs_to_flat(load, store):
    for half in range(2):
        for k in range(3):
            total = None
            for j in range(8):
                lane = 48 * j - 128 * k
                if lane <= -48 or lane >= 128:
                    continue
                value = pltpu.roll(load(j), (lane - MARGIN - 64 * half) % 128, 1)
                at = lax.broadcasted_iota(jnp.int32, value.shape, 1) - lane
                picked = jnp.where((at >= 0) & (at < 48), value, 0.0)
                total = picked if total is None else total + picked
            store(k, half, total)


GROUPS = HALF * E // 8
FLAT = E3 // 128


def load_flat(ref):
    return lambda k, half: ref[pl.ds(half * 3 * GROUPS + k, GROUPS, stride=3), :]


def store_rows(ref):
    def store(j, rows):
        ref[pl.ds(j, GROUPS, stride=8), :] = rows

    return store


def prepare(ints_ref, blend_ref, est_ref, cells_ref, pack_ref, cp_ref, weights_ref, own_ref, faces, flat_ref):
    number = lax.broadcasted_iota(jnp.int32, (1, 128), 1)
    weights_ref[...] = jnp.zeros_like(weights_ref)
    own_ref[...] = jnp.zeros_like(own_ref)
    for u in range(UPDATES):
        view = ints_ref[u]
        first = jnp.full((1, 128), blend_ref[2 * view], F32)
        second = jnp.full((1, 128), blend_ref[2 * view + 1], F32)
        total = first + second
        weights_ref[u : u + 1, :] = jnp.where(number == ints_ref[6 + 2 * view], first / total, 0.0) + jnp.where(
            number == ints_ref[7 + 2 * view], second / total, 0.0
        )
        for i in range(KS3 // 128):
            own_ref[u, i : i + 1, :] = cells_ref[view, :, i * 128 : (i + 1) * 128]
        tail = KS3 // 128 * 128
        i = KS3 // 128
        own_ref[u, i : i + 1, 0 : KS3 - tail] = cells_ref[view, :, tail:KS3]
    flat_to_pairs(load_flat(est_ref), store_rows(flat_ref))
    cp_ref[...] = flat_ref[...].reshape(HALF, E, 128)
    emit_faces(cp_ref, pack_ref, faces)


def forward_planes(src_ref, z_ref, spec_ref, rows, fwd_z_ref, fwd_y_ref):
    group = 20

    def z_body(it, carry):
        block = src_ref[pl.ds(it * group, group)].reshape(group * rows, 128)
        z_ref[pl.ds(it * group, group), 0:rows, :] = lanes_dft(block, fwd_z_ref[...]).reshape(group, rows, 128)
        return carry

    lax.fori_loop(0, PLANES // group, z_body, 0)

    def y_body(it, carry):
        planes = [z_ref[it * group + j, 0:rows, :] for j in range(group)]
        for j, plane in enumerate(rows_dft(planes, fwd_y_ref[...], PAD, False)):
            spec_ref[it * group + j] = plane
        return carry

    lax.fori_loop(0, PLANES // group, y_body, 0)


def filter_planes(spec_ref, kr_ref, ki_ref, out_ref, conjugate):
    group = 12
    sign = lane_sign((8, 128))
    if not conjugate:
        sign = -sign

    def body(kb, carry):
        rows = pl.ds(pl.multiple_of(kb * 8, 8), 8)
        for first in range(0, HALF, group):
            values = {}
            acc_r, acc_i = [None] * group, [None] * group
            for d in range(KS):
                tap = d if conjugate else KS - 1 - d
                kr = kr_ref[tap, rows, :]
                ki = ki_ref[tap, rows, :]
                for j in range(group):
                    m = first + j + d
                    if m not in values:
                        values[m] = spec_ref[m, rows, :]
                    if d == 0:
                        acc_r[j] = kr * values[m]
                        acc_i[j] = ki * values[m]
                    else:
                        acc_r[j] = acc_r[j] + kr * values[m]
                        acc_i[j] = acc_i[j] + ki * values[m]
            for j in range(group):
                out_ref[first + j, rows, :] = acc_r[j] + sign * pltpu.roll(acc_i[j], 64, 1)
        return carry

    lax.fori_loop(0, PAD // 8, body, 0)


def inverse_planes(spec_ref, y_ref, out_ref, inv_y_ref, inv_z_ref):
    group = 12

    def y_body(it, carry):
        planes = [spec_ref[it * group + j] for j in range(group)]
        for j, plane in enumerate(rows_dft(planes, inv_y_ref[...], E, True)):
            y_ref[it * group + j, 0:E, :] = plane
        return carry

    lax.fori_loop(0, HALF // group, y_body, 0)

    def z_body(it, carry):
        block = y_ref[pl.ds(it * group, group), 0:E, :].reshape(group * E, 128)
        out_ref[pl.ds(it * group, group)] = lanes_dft(block, inv_z_ref[...]).reshape(group, E, 128)
        return carry

    lax.fori_loop(0, HALF // group, z_body, 0)


def tap_spectra(flat_ref, taps_ref, z_ref, kr_ref, ki_ref, tap_z_ref, tap_y_ref):
    lane = lax.broadcasted_iota(jnp.int32, (1, 128), 1)
    for r in range(KS * KS):
        i, at = KS * r // 128, KS * r % 128
        run = pltpu.roll(flat_ref[i : i + 1, :], (-at) % 128, 1)
        if at + KS > 128:
            more = pltpu.roll(flat_ref[i + 1 : i + 2, :], (-at) % 128, 1)
            run = jnp.where(lane < 128 - at, run, more)
        taps_ref[r // KS, r % KS : r % KS + 1, :] = run
    low_full = low_lanes((PAD, 128))
    rows = lanes_dft(taps_ref[...].reshape(KS * TAPROWS, 128), tap_z_ref[...])
    z_ref[0:KS, 0:TAPROWS, :] = rows.reshape(KS, TAPROWS, 128)
    planes = [z_ref[d, 0:TAPROWS, :] for d in range(KS)]
    for d, spec in enumerate(rows_dft(planes, tap_y_ref[...], PAD, False)):
        other = pltpu.roll(spec, 64, 1)
        kr_ref[d] = jnp.where(low_full, spec, other)
        ki_ref[d] = jnp.where(low_full, other, spec)


def assemble(ints_ref, cp_ref, halos, place_ref, ext_ref, pp_ref):
    hxm_ref, hxp_ref, hym_ref, hyp_ref, hzm_ref, hzp_ref = halos
    low_core = low_lanes((E, 128))
    low_row = low_lanes((8, 128))

    def face(ref, f):
        return jnp.where(ints_ref[19 + f] >= 0, ref[...].astype(F32), 0.0)

    ext_ref[:, 0:8, :] = face(hym_ref, 2).reshape(HALF, 8, 128)
    ext_ref[:, 56:64, :] = face(hyp_ref, 3).reshape(HALF, 8, 128)
    zm_all = face(hzm_ref, 4).astype(BF16)
    zp_all = face(hzp_ref, 5).astype(BF16)
    for g in range(3):
        zm = dot(zm_all[g * E : (g + 1) * E], place_ref[0])
        zp = dot(zp_all[g * E : (g + 1) * E], place_ref[1])
        for p in range(8):
            lanes = slice(p * 128, (p + 1) * 128)
            ext_ref[g * 8 + p, 8:56, :] = cp_ref[g * 8 + p] + zm[:, lanes] + zp[:, lanes]
    xm = face(hxm_ref, 0).reshape(4, E, 128)
    xp = face(hxp_ref, 1).reshape(4, E, 128)
    pp_ref[8:32] = ext_ref[...]
    for j in range(8):
        for rows in (slice(0, 8), slice(56, 64)):
            near = ext_ref[16 + j, rows, :]
            pp_ref[j, rows, :] = pltpu.roll(jnp.where(low_row, near, 0.0), 64, 1)
            near = ext_ref[j, rows, :]
            pp_ref[32 + j, rows, :] = pltpu.roll(jnp.where(low_row, 0.0, near), 64, 1)
        before = xm[j] if j < 4 else pltpu.roll(xm[j - 4], 64, 1)
        after = pltpu.roll(xp[j], 64, 1) if j < 4 else xp[j - 4]
        pp_ref[j, 8:56, :] = jnp.where(low_core, before, pltpu.roll(ext_ref[16 + j, 8:56, :], 64, 1))
        pp_ref[32 + j, 8:56, :] = jnp.where(low_core, pltpu.roll(ext_ref[j, 8:56, :], 64, 1), after)


def correct(ints_ref, cp_ref, new_ref, seen_ref, tables, work):
    fwd_z_ref, inv_z_ref, fwd_yc_ref, inv_y_ref = tables
    z_ref, spec_ref, kr_ref, ki_ref, fil_ref, core_ref, q_ref = work
    low_core = low_lanes((E, 128))
    filter_planes(spec_ref, kr_ref, ki_ref, fil_ref, False)
    inverse_planes(fil_ref, z_ref, core_ref, inv_y_ref, inv_z_ref)

    lane = lax.broadcasted_iota(jnp.int32, (E, 128), 1) % 64
    inside = (lane >= MARGIN) & (lane < MARGIN + E)

    def ratio_body(it, carry):
        for o in [it * 4 + j for j in range(4)]:
            q_ref[o + 8] = jnp.where(inside, seen_ref[o] / jnp.where(inside, core_ref[o], 1.0), 0.0)
        return carry

    lax.fori_loop(0, HALF // 4, ratio_body, 0)
    for j in range(8):
        q_ref[j] = pltpu.roll(jnp.where(low_core, q_ref[24 + j], 0.0), 64, 1)
        q_ref[32 + j] = pltpu.roll(jnp.where(low_core, 0.0, q_ref[8 + j]), 64, 1)

    forward_planes(q_ref, z_ref, spec_ref, E, fwd_z_ref, fwd_yc_ref)
    filter_planes(spec_ref, kr_ref, ki_ref, fil_ref, True)
    inverse_planes(fil_ref, z_ref, core_ref, inv_y_ref, inv_z_ref)

    alive = ints_ref[18] > 0

    def finish(it, carry):
        for o in [it * 4 + j for j in range(4)]:
            old = cp_ref[o]
            new_ref[o] = jnp.where(jnp.logical_and(inside, alive), old * core_ref[o], old)
        return carry

    lax.fori_loop(0, HALF // 4, finish, 0)


VMEM = pl.BlockSpec(memory_space=pltpu.VMEM)
SMEM = pl.BlockSpec(memory_space=pltpu.SMEM)


def fwd_y_core():
    full = TABLES["fwd_y"]
    return np.concatenate([full[:, s * PAD + MARGIN : s * PAD + MARGIN + E] for s in range(4)], axis=1)


GRID = (4, 4, 8)


def coords_of(b):
    return (
        b % 2 + 2 * ((b // 8) % 2),
        (b // 2) % 2 + 2 * ((b // 16) % 2),
        (b // 64) % 2 + 2 * ((b // 4) % 2) + 4 * ((b // 32) % 2),
    )


def block_at(c):
    return (
        c[0] % 2 + 2 * (c[1] % 2) + 4 * ((c[2] // 2) % 2) + 8 * (c[0] // 2) + 16 * (c[1] // 2)
        + 32 * (c[2] // 4) + 64 * (c[2] % 2)
    )


def neighbour_of(b, axis, step):
    c = list(coords_of(b))
    c[axis] = (c[axis] + step + GRID[axis]) % GRID[axis]
    return block_at(c)


MESH = pl.DeviceIdType.MESH
NEAR = 8
FAR = 16


def near_peers(me):
    base = me // NEAR * NEAR
    return [base + (me % NEAR + s) % NEAR for s in range(1, NEAR)]


def far_peers(me):
    return [(me // NEAR + s) % FAR * NEAR + me % NEAR for s in range(1, FAR)]


def face_peers(me):
    return [neighbour_of(me, f // 2, -1 if f % 2 == 0 else 1) for f in range(6)]


def face_copies(faces, halos, peers, send, recv):
    return [
        pltpu.make_async_remote_copy(
            src_ref=faces[f],
            dst_ref=halos[f ^ 1],
            send_sem=send.at[f],
            recv_sem=recv.at[f],
            device_id=(peers[f],),
            device_id_type=MESH,
        )
        for f in range(6)
    ]


def remote(src, dst, send, recv, peer):
    return pltpu.make_async_remote_copy(
        src_ref=src, dst_ref=dst, send_sem=send, recv_sem=recv, device_id=(peer,), device_id_type=MESH
    )


def blend_cells(u, cells_ref, weights_ref, pick, scaled_ref, parts_ref):
    for a in range(NEAR):
        cell = cells_ref[a]
        total = jnp.sum(jnp.sum(cell, axis=0, keepdims=True), axis=1, keepdims=True)
        scaled_ref[a] = cell / total

    def body(dest, carry):
        share = jnp.sum(weights_ref[dest, u : u + 1, :] * pick, axis=1, keepdims=True)
        total = share[0:1, :] * scaled_ref[0]
        for a in range(1, NEAR):
            total = total + share[a : a + 1, :] * scaled_ref[a]
        parts_ref[dest] = total
        return carry

    lax.fori_loop(0, FAR, body, 0)


def whole_kernel(*refs):
    ints_ref, blend_ref, est_ref, cells_ref, cell_row_ref = refs[:5]
    seen_in = refs[5:7]
    fwd_z_ref, inv_z_ref, tap_z_ref, fwd_y_ref, fwd_yc_ref, inv_y_ref, tap_y_ref, pack_ref, place_ref = refs[7:16]
    out_ref = refs[16]
    refs = refs[17:]
    cp_refs, own_ref, weights_ref = refs[:2], refs[2], refs[3]
    faces = (refs[4:10], refs[10:16])
    halos = (refs[16:22], refs[22:28])
    near_all, weights_all, parts, held = refs[28:30], refs[30], refs[31:33], refs[33:35]
    scaled_ref, kernel_ref, taps_ref, ext_ref, pp_ref, z_ref, spec_ref = refs[35:42]
    kr_ref, ki_ref, fil_ref, core_ref, q_ref, wide_ref, flat_ref = refs[42:49]
    own_sem, near_send, near_recv, share_send, share_recv = refs[49:54]
    far_send, far_recv, face_send, face_recv = refs[54:58]
    row_ref = flat_ref.reshape(HALF * E, 128)
    tables = (fwd_z_ref, inv_z_ref, fwd_yc_ref, inv_y_ref)
    work = (z_ref, spec_ref, kr_ref, ki_ref, fil_ref, core_ref, q_ref)

    me = lax.axis_index("blk")
    near, far, across = near_peers(me), far_peers(me), face_peers(me)
    barrier = pltpu.get_barrier_semaphore()
    for peer in near + far + across:
        pl.semaphore_signal(barrier, inc=1, device_id=(peer,), device_id_type=MESH)

    taps_ref[...] = jnp.zeros_like(taps_ref)
    prepare(
        ints_ref, blend_ref, est_ref, cells_ref, pack_ref, cp_refs[0], weights_ref, own_ref, faces[0], row_ref
    )
    pl.semaphore_wait(barrier, len(near + far + across))

    near_copies = [
        [
            remote(own_ref.at[u], near_all[u].at[me % NEAR], near_send.at[u, s], near_recv.at[u, s], peer)
            for s, peer in enumerate(near)
        ]
        + [pltpu.make_async_copy(own_ref.at[u], near_all[u].at[me % NEAR], own_sem.at[u])]
        for u in range(UPDATES)
    ]
    share_copies = [
        remote(weights_ref, weights_all.at[me // NEAR], share_send.at[s], share_recv.at[s], peer)
        for s, peer in enumerate(far)
    ] + [pltpu.make_async_copy(weights_ref, weights_all.at[me // NEAR], own_sem.at[2])]
    face_copies = [
        [
            remote(faces[u][f], halos[u][f ^ 1], face_send.at[u, f], face_recv.at[u, f], across[f])
            for f in range(6)
        ]
        for u in range(UPDATES)
    ]
    far_copies = [
        [
            remote(parts[u].at[(me // NEAR + 1 + s) % FAR], held[u].at[s], far_send.at[u, s], far_recv.at[u, s], peer)
            for s, peer in enumerate(far)
        ]
        for u in range(UPDATES)
    ]

    def start(copies):
        for copy in copies:
            copy.start()

    def wait(copies):
        for copy in copies:
            copy.wait()

    base = me // NEAR * NEAR
    pick = (cell_row_ref[...] == base + lax.broadcasted_iota(jnp.int32, (NEAR, 128), 0)).astype(F32)

    def seen_pairs(u):
        wide_ref[...] = seen_in[u][...].astype(F32)
        flat_to_pairs(load_flat(wide_ref), store_rows(row_ref))

    def spectra(u):
        wait(far_copies[u])
        total = parts[u][me // NEAR]
        for s in range(FAR - 1):
            total = total + held[u][s]
        kernel_ref[...] = total
        tap_spectra(kernel_ref, taps_ref, z_ref, kr_ref, ki_ref, tap_z_ref, tap_y_ref)

    def padded_spectra(u):
        wait(face_copies[u])
        assemble(ints_ref, cp_refs[u], halos[u], place_ref, ext_ref, pp_ref)
        forward_planes(pp_ref, z_ref, spec_ref, PAD, fwd_z_ref, fwd_y_ref)

    start(near_copies[0])
    start(share_copies)
    start(face_copies[0])
    start(near_copies[1])
    seen_pairs(0)
    wait(near_copies[0])
    wait(share_copies)
    blend_cells(0, near_all[0], weights_all, pick, scaled_ref, parts[0])
    start(far_copies[0])
    padded_spectra(0)
    wait(near_copies[1])
    blend_cells(1, near_all[1], weights_all, pick, scaled_ref, parts[1])
    start(far_copies[1])
    spectra(0)
    correct(ints_ref, cp_refs[0], cp_refs[1], flat_ref, tables, work)
    emit_faces(cp_refs[1], pack_ref, faces[1])
    start(face_copies[1])
    spectra(1)
    seen_pairs(1)
    padded_spectra(1)
    correct(ints_ref, cp_refs[1], flat_ref, flat_ref, tables, work)

    def load_new(j):
        return row_ref[pl.ds(j, GROUPS, stride=8), :]

    def store_new(k, half, rows):
        out_ref[pl.ds(half * 3 * GROUPS + k, GROUPS, stride=3), :] = rows

    pairs_to_flat(load_new, store_new)


HALO_SHAPES = [FACE_SHAPES[f ^ 1] for f in range(6)]
DMA = pltpu.SemaphoreType.DMA


def whole_call(ints, blend, est, cells, cell_row, seen):
    tables = [
        TABLES["fwd_z"],
        TABLES["inv_z"],
        TABLES["tap_z"],
        TABLES["fwd_y"],
        fwd_y_core(),
        TABLES["inv_y"],
        TABLES["tap_y"],
        TABLES["pack"],
        TABLES["place"],
    ]
    f32 = [
        (NEAR, CELLROWS, 128),
        (NEAR, CELLROWS, 128),
        (FAR, 8, 128),
        (FAR, CELLROWS, 128),
        (FAR, CELLROWS, 128),
        (FAR - 1, CELLROWS, 128),
        (FAR - 1, CELLROWS, 128),
        (NEAR, CELLROWS, 128),
        (CELLROWS, 128),
        (KS, TAPROWS, 128),
        (HALF, PAD, 128),
        (PLANES, PAD, 128),
        (PLANES, PAD, 128),
        (PLANES, PAD, 128),
        (KS, PAD, 128),
        (KS, PAD, 128),
        (HALF, PAD, 128),
        (HALF, E, 128),
        (PLANES, E, 128),
        (FLAT, 128),
        (HALF, E, 128),
    ]
    scratch = [pltpu.VMEM(s, F32) for s in [(HALF, E, 128)] * 2 + [(UPDATES, CELLROWS, 128), (8, 128)]]
    scratch += [pltpu.VMEM(s, BF16) for s in FACE_SHAPES * 2 + HALO_SHAPES * 2]
    scratch += [pltpu.VMEM(s, F32) for s in f32]
    scratch += [DMA((3,)), DMA((2, NEAR - 1)), DMA((2, NEAR - 1)), DMA((FAR - 1,)), DMA((FAR - 1,))]
    scratch += [DMA((2, FAR - 1)), DMA((2, FAR - 1)), DMA((2, 6)), DMA((2, 6))]
    return pl.pallas_call(
        whole_kernel,
        out_shape=jax.ShapeDtypeStruct((FLAT, 128), F32),
        in_specs=[SMEM] * 2 + [VMEM] * (5 + len(tables)),
        out_specs=VMEM,
        scratch_shapes=scratch,
        compiler_params=pltpu.CompilerParams(collective_id=0, has_side_effects=True),
        name="whole",
    )(ints, blend, est, cells, cell_row.reshape(1, 128), *seen, *[jnp.asarray(t) for t in tables])


def local(
    estimate, observed, psf_cells, tissue, neighbours, psf_list, psf_blend, cell_row, view_order
):
    ints = jnp.concatenate([view_order, psf_list.reshape(12), tissue, neighbours.reshape(6)])
    seen = [
        lax.dynamic_index_in_dim(observed[0], view_order[u].astype(jnp.uint32), 0, keepdims=False).reshape(FLAT, 128)
        for u in range(UPDATES)
    ]
    result = whole_call(
        ints, psf_blend.reshape(12), estimate.reshape(FLAT, 128), psf_cells.reshape(6, 1, KS3), cell_row, seen
    )
    return result.reshape(1, E3)


def solution(mesh):
    return jax.shard_map(
        local,
        mesh=mesh,
        in_specs=(
            P("blk", None),
            P("blk", None, None),
            P("blk", None, None),
            P("blk"),
            P("blk", None),
            P("blk", None, None),
            P("blk", None, None),
            P(),
            P(),
        ),
        out_specs=P("blk", None),
        check_vma=False,
    )
```

```python
import functools
import math

import jax
import jax.numpy as jnp
import numpy as np
from jax import lax
from jax.experimental import pallas as pl
from jax.experimental.pallas import tpu as pltpu
from jax.sharding import PartitionSpec as P

E = 48
MARGIN = 8
UPDATES = 2
PAD = 64
KS = 17
E3 = 110592
KS3 = 4913
HALF = 24
PLANES = 40
TAPROWS = 32

CELLROWS = 40
ROWS = UPDATES * CELLROWS

F32 = jnp.float32
BF16 = jnp.bfloat16


def split_np(table):
    hi = np.asarray(table, np.float32).astype(jnp.bfloat16)
    lo = (np.asarray(table, np.float64) - hi.astype(np.float64)).astype(np.float32).astype(jnp.bfloat16)
    return hi, lo


def lane_table(table):
    hi, lo = split_np(table)
    row = np.concatenate([hi, lo], axis=1)
    return np.concatenate([row, row], axis=0)


def row_table(table):
    hi, lo = split_np(table)
    return np.concatenate([hi, hi, lo, lo], axis=1)


def make_tables():
    step = 2.0 * math.pi / PAD
    k = np.arange(PAD)
    ang = (k[:, None] * k[None, :] % PAD) * step
    cos, sin = np.cos(ang), np.sin(ang)
    fwd_z = np.block([[cos, -sin], [sin, cos]])
    inv_z = np.block([[cos, sin], [-sin, cos]]) / PAD
    fwd_y = np.concatenate([cos, sin], axis=0)
    inv_y = np.concatenate([cos[MARGIN : MARGIN + E], sin[MARGIN : MARGIN + E]], axis=0) / PAD
    t = np.arange(KS) - MARGIN
    ang_t = (t[:, None] * k[None, :]) % PAD * step
    tap_z = np.zeros((128, 128))
    tap_z[:KS, :PAD] = np.cos(ang_t)
    tap_z[:KS, PAD:] = -np.sin(ang_t)
    tap_y = np.zeros((128, TAPROWS))
    tap_y[:PAD, :KS] = np.cos(ang_t).T
    tap_y[PAD:, :KS] = np.sin(ang_t).T
    pack = np.zeros((2, 8 * 128, 128), np.float32)
    place = np.zeros((2, 128, 8 * 128), np.float32)
    for p in range(8):
        for s in range(2):
            for z in range(MARGIN):
                slot = p * 16 + s * 8 + z
                pack[0, p * 128 + s * 64 + MARGIN + z, slot] = 1
                pack[1, p * 128 + s * 64 + E + z, slot] = 1
                place[0, slot, p * 128 + s * 64 + z] = 1
                place[1, slot, p * 128 + s * 64 + MARGIN + E + z] = 1
    return dict(
        fwd_z=lane_table(fwd_z),
        inv_z=lane_table(inv_z),
        tap_z=lane_table(tap_z),
        fwd_y=row_table(fwd_y),
        inv_y=row_table(inv_y),
        tap_y=row_table(tap_y),
        pack=pack.astype(jnp.bfloat16),
        place=place.astype(jnp.bfloat16),
    )


TABLES = make_tables()


def split(values):
    hi = values.astype(BF16)
    lo = (values - hi.astype(F32)).astype(BF16)
    return hi, lo


def low_lanes(shape):
    return lax.broadcasted_iota(jnp.int32, shape, len(shape) - 1) < 64


def lane_sign(shape):
    return jnp.where(low_lanes(shape), 1.0, -1.0).astype(F32)


def dot(a, b):
    return lax.dot_general(a, b, (((1,), (0,)), ((), ())), preferred_element_type=F32)


def lanes_dft(rows, table):
    hi, lo = split(rows)
    both = dot(jnp.concatenate([hi, lo], axis=1), table)
    return both[:, :128] + both[:, 128:]


def rows_dft(planes, table, count, inverse):
    sign = lane_sign((count, 128))
    if inverse:
        sign = -sign
    out = []
    for a in range(0, len(planes), 2):
        cols = []
        for plane in planes[a : a + 2]:
            hi, lo = split(plane)
            cols.append(jnp.concatenate([hi, lo, hi, lo], axis=0))
        rhs = jnp.concatenate(cols, axis=1) if len(cols) > 1 else cols[0]
        both = dot(table, rhs)
        for b in range(len(cols)):
            c_part = both[:count, b * 128 : (b + 1) * 128]
            s_part = both[count : 2 * count, b * 128 : (b + 1) * 128]
            out.append(c_part + sign * pltpu.roll(s_part, 64, 1))
    return out


def emit_faces(cp_ref, pack_ref, faces):
    xm_ref, xp_ref, ym_ref, yp_ref, zm_ref, zp_ref = faces
    low = low_lanes((E, 128))
    for j in range(4):
        near = jnp.where(low, cp_ref[j], pltpu.roll(cp_ref[4 + j], 64, 1))
        xm_ref[j * E : (j + 1) * E, :] = near.astype(BF16)
        near = jnp.where(low, pltpu.roll(cp_ref[16 + j], 64, 1), cp_ref[20 + j])
        xp_ref[j * E : (j + 1) * E, :] = near.astype(BF16)
    ym_ref[...] = cp_ref[:, 0:8, :].reshape(HALF * 8, 128).astype(BF16)
    yp_ref[...] = cp_ref[:, E - 8 : E, :].reshape(HALF * 8, 128).astype(BF16)
    for g in range(3):
        wide = jnp.concatenate([cp_ref[g * 8 + p].astype(BF16) for p in range(8)], axis=1)
        zm_ref[g * E : (g + 1) * E, :] = dot(wide, pack_ref[0]).astype(BF16)
        zp_ref[g * E : (g + 1) * E, :] = dot(wide, pack_ref[1]).astype(BF16)


FACE_SHAPES = [(4 * E, 128), (4 * E, 128), (HALF * 8, 128), (HALF * 8, 128), (3 * E, 128), (3 * E, 128)]


def flat_to_pairs(load, store):
    for j in range(8):
        total = None
        for half in range(2):
            first = 48 * j
            k, lane = first // 128, first % 128
            base = MARGIN + 64 * half
            value = load(k, half)
            part = value if lane == base else pltpu.roll(value, (base - lane) % 128, 1)
            at = lax.broadcasted_iota(jnp.int32, part.shape, 1) - base
            length = min(48, 128 - lane)
            picked = jnp.where((at >= 0) & (at < length), part, 0.0)
            if length < 48:
                more = pltpu.roll(load(k + 1, half), base + length, 1)
                picked = jnp.where((at >= length) & (at < 48), more, picked)
            total = picked if total is None else total + picked
        store(j, total)


def pairs_to_flat(load, store):
    for half in range(2):
        for k in range(3):
            total = None
            for j in range(8):
                lane = 48 * j - 128 * k
                if lane <= -48 or lane >= 128:
                    continue
                value = pltpu.roll(load(j), (lane - MARGIN - 64 * half) % 128, 1)
                at = lax.broadcasted_iota(jnp.int32, value.shape, 1) - lane
                picked = jnp.where((at >= 0) & (at < 48), value, 0.0)
                total = picked if total is None else total + picked
            store(k, half, total)


GROUPS = HALF * E // 8
FLAT = E3 // 128


def load_flat(ref):
    return lambda k, half: ref[pl.ds(half * 3 * GROUPS + k, GROUPS, stride=3), :]


def store_rows(ref):
    def store(j, rows):
        ref[pl.ds(j, GROUPS, stride=8), :] = rows

    return store


def prepare(order_ref, list_ref, blend_ref, est_ref, cells_ref, pack_ref, cp_ref, weights_ref, own_ref, faces, flat_ref):
    number = lax.broadcasted_iota(jnp.int32, (1, 128), 1)
    weights_ref[...] = jnp.zeros_like(weights_ref)
    own_ref[...] = jnp.zeros_like(own_ref)
    for u in range(UPDATES):
        view = order_ref[u]
        first = jnp.full((1, 128), blend_ref[0, view], F32)
        second = jnp.full((1, 128), blend_ref[1, view], F32)
        total = first + second
        weights_ref[u : u + 1, :] = jnp.where(number == list_ref[0, view], first / total, 0.0) + jnp.where(
            number == list_ref[1, view], second / total, 0.0
        )
        for i in range(KS3 // 128):
            own_ref[u, i : i + 1, :] = cells_ref[view, :, i * 128 : (i + 1) * 128]
        tail = KS3 // 128 * 128
        i = KS3 // 128
        own_ref[u, i : i + 1, 0 : KS3 - tail] = cells_ref[view, :, tail:KS3]
    flat_to_pairs(load_flat(est_ref), store_rows(flat_ref))
    cp_ref[...] = flat_ref[...].reshape(HALF, E, 128)
    emit_faces(cp_ref, pack_ref, faces)


def forward_planes(src_ref, z_ref, spec_ref, rows, fwd_z_ref, fwd_y_ref):
    group = 20

    def z_body(it, carry):
        block = src_ref[pl.ds(it * group, group)].reshape(group * rows, 128)
        z_ref[pl.ds(it * group, group), 0:rows, :] = lanes_dft(block, fwd_z_ref[...]).reshape(group, rows, 128)
        return carry

    lax.fori_loop(0, PLANES // group, z_body, 0)

    def y_body(it, carry):
        planes = [z_ref[it * group + j, 0:rows, :] for j in range(group)]
        for j, plane in enumerate(rows_dft(planes, fwd_y_ref[...], PAD, False)):
            spec_ref[it * group + j] = plane
        return carry

    lax.fori_loop(0, PLANES // group, y_body, 0)


def filter_planes(spec_ref, kr_ref, ki_ref, out_ref, conjugate):
    group = 12
    sign = lane_sign((8, 128))
    if not conjugate:
        sign = -sign

    def body(kb, carry):
        rows = pl.ds(pl.multiple_of(kb * 8, 8), 8)
        for first in range(0, HALF, group):
            values = {}
            acc_r, acc_i = [None] * group, [None] * group
            for d in range(KS):
                tap = d if conjugate else KS - 1 - d
                kr = kr_ref[tap, rows, :]
                ki = ki_ref[tap, rows, :]
                for j in range(group):
                    m = first + j + d
                    if m not in values:
                        values[m] = spec_ref[m, rows, :]
                    if d == 0:
                        acc_r[j] = kr * values[m]
                        acc_i[j] = ki * values[m]
                    else:
                        acc_r[j] = acc_r[j] + kr * values[m]
                        acc_i[j] = acc_i[j] + ki * values[m]
            for j in range(group):
                out_ref[first + j, rows, :] = acc_r[j] + sign * pltpu.roll(acc_i[j], 64, 1)
        return carry

    lax.fori_loop(0, PAD // 8, body, 0)


def inverse_planes(spec_ref, y_ref, out_ref, inv_y_ref, inv_z_ref):
    group = 12

    def y_body(it, carry):
        planes = [spec_ref[it * group + j] for j in range(group)]
        for j, plane in enumerate(rows_dft(planes, inv_y_ref[...], E, True)):
            y_ref[it * group + j, 0:E, :] = plane
        return carry

    lax.fori_loop(0, HALF // group, y_body, 0)

    def z_body(it, carry):
        block = y_ref[pl.ds(it * group, group), 0:E, :].reshape(group * E, 128)
        out_ref[pl.ds(it * group, group)] = lanes_dft(block, inv_z_ref[...]).reshape(group, E, 128)
        return carry

    lax.fori_loop(0, HALF // group, z_body, 0)


def tap_spectra(flat_ref, taps_ref, z_ref, kr_ref, ki_ref, tap_z_ref, tap_y_ref):
    lane = lax.broadcasted_iota(jnp.int32, (1, 128), 1)
    for r in range(KS * KS):
        i, at = KS * r // 128, KS * r % 128
        run = pltpu.roll(flat_ref[i : i + 1, :], (-at) % 128, 1)
        if at + KS > 128:
            more = pltpu.roll(flat_ref[i + 1 : i + 2, :], (-at) % 128, 1)
            run = jnp.where(lane < 128 - at, run, more)
        taps_ref[r // KS, r % KS : r % KS + 1, :] = run
    low_full = low_lanes((PAD, 128))
    rows = lanes_dft(taps_ref[...].reshape(KS * TAPROWS, 128), tap_z_ref[...])
    z_ref[0:KS, 0:TAPROWS, :] = rows.reshape(KS, TAPROWS, 128)
    planes = [z_ref[d, 0:TAPROWS, :] for d in range(KS)]
    for d, spec in enumerate(rows_dft(planes, tap_y_ref[...], PAD, False)):
        other = pltpu.roll(spec, 64, 1)
        kr_ref[d] = jnp.where(low_full, spec, other)
        ki_ref[d] = jnp.where(low_full, other, spec)


def assemble(next_ref, cp_ref, halos, place_ref, ext_ref, pp_ref):
    hxm_ref, hxp_ref, hym_ref, hyp_ref, hzm_ref, hzp_ref = halos
    low_core = low_lanes((E, 128))
    low_row = low_lanes((8, 128))

    def face(ref, f):
        return jnp.where(next_ref[0, f] >= 0, ref[...].astype(F32), 0.0)

    ext_ref[:, 0:8, :] = face(hym_ref, 2).reshape(HALF, 8, 128)
    ext_ref[:, 56:64, :] = face(hyp_ref, 3).reshape(HALF, 8, 128)
    zm_all = face(hzm_ref, 4).astype(BF16)
    zp_all = face(hzp_ref, 5).astype(BF16)
    for g in range(3):
        zm = dot(zm_all[g * E : (g + 1) * E], place_ref[0])
        zp = dot(zp_all[g * E : (g + 1) * E], place_ref[1])
        for p in range(8):
            lanes = slice(p * 128, (p + 1) * 128)
            ext_ref[g * 8 + p, 8:56, :] = cp_ref[g * 8 + p] + zm[:, lanes] + zp[:, lanes]
    xm = face(hxm_ref, 0).reshape(4, E, 128)
    xp = face(hxp_ref, 1).reshape(4, E, 128)
    pp_ref[8:32] = ext_ref[...]
    for j in range(8):
        for rows in (slice(0, 8), slice(56, 64)):
            near = ext_ref[16 + j, rows, :]
            pp_ref[j, rows, :] = pltpu.roll(jnp.where(low_row, near, 0.0), 64, 1)
            near = ext_ref[j, rows, :]
            pp_ref[32 + j, rows, :] = pltpu.roll(jnp.where(low_row, 0.0, near), 64, 1)
        before = xm[j] if j < 4 else pltpu.roll(xm[j - 4], 64, 1)
        after = pltpu.roll(xp[j], 64, 1) if j < 4 else xp[j - 4]
        pp_ref[j, 8:56, :] = jnp.where(low_core, before, pltpu.roll(ext_ref[16 + j, 8:56, :], 64, 1))
        pp_ref[32 + j, 8:56, :] = jnp.where(low_core, pltpu.roll(ext_ref[j, 8:56, :], 64, 1), after)


def correct(tissue_ref, cp_ref, new_ref, seen_ref, tables, work):
    fwd_z_ref, inv_z_ref, fwd_yc_ref, inv_y_ref = tables
    z_ref, spec_ref, kr_ref, ki_ref, fil_ref, core_ref, q_ref = work
    low_core = low_lanes((E, 128))
    filter_planes(spec_ref, kr_ref, ki_ref, fil_ref, False)
    inverse_planes(fil_ref, z_ref, core_ref, inv_y_ref, inv_z_ref)

    lane = lax.broadcasted_iota(jnp.int32, (E, 128), 1) % 64
    inside = (lane >= MARGIN) & (lane < MARGIN + E)

    def ratio_body(it, carry):
        for o in [it * 4 + j for j in range(4)]:
            q_ref[o + 8] = jnp.where(inside, seen_ref[o] / jnp.where(inside, core_ref[o], 1.0), 0.0)
        return carry

    lax.fori_loop(0, HALF // 4, ratio_body, 0)
    for j in range(8):
        q_ref[j] = pltpu.roll(jnp.where(low_core, q_ref[24 + j], 0.0), 64, 1)
        q_ref[32 + j] = pltpu.roll(jnp.where(low_core, 0.0, q_ref[8 + j]), 64, 1)

    forward_planes(q_ref, z_ref, spec_ref, E, fwd_z_ref, fwd_yc_ref)
    filter_planes(spec_ref, kr_ref, ki_ref, fil_ref, True)
    inverse_planes(fil_ref, z_ref, core_ref, inv_y_ref, inv_z_ref)

    alive = tissue_ref[0] > 0

    def finish(it, carry):
        for o in [it * 4 + j for j in range(4)]:
            old = cp_ref[o]
            new_ref[o] = jnp.where(jnp.logical_and(inside, alive), old * core_ref[o], old)
        return carry

    lax.fori_loop(0, HALF // 4, finish, 0)


VMEM = pl.BlockSpec(memory_space=pltpu.VMEM)
SMEM = pl.BlockSpec(memory_space=pltpu.SMEM)


def fwd_y_core():
    full = TABLES["fwd_y"]
    return np.concatenate([full[:, s * PAD + MARGIN : s * PAD + MARGIN + E] for s in range(4)], axis=1)


GRID = (4, 4, 8)


def coords_of(b):
    return (
        b % 2 + 2 * ((b // 8) % 2),
        (b // 2) % 2 + 2 * ((b // 16) % 2),
        (b // 64) % 2 + 2 * ((b // 4) % 2) + 4 * ((b // 32) % 2),
    )


def block_at(c):
    return (
        c[0] % 2 + 2 * (c[1] % 2) + 4 * ((c[2] // 2) % 2) + 8 * (c[0] // 2) + 16 * (c[1] // 2)
        + 32 * (c[2] // 4) + 64 * (c[2] % 2)
    )


def neighbour_of(b, axis, step):
    c = list(coords_of(b))
    c[axis] = (c[axis] + step + GRID[axis]) % GRID[axis]
    return block_at(c)


MESH = pl.DeviceIdType.MESH
NEAR = 8
FAR = 16


def near_peers(me):
    base = me // NEAR * NEAR
    return [base + (me % NEAR + s) % NEAR for s in range(1, NEAR)]


def far_peers(me):
    return [(me // NEAR + s) % FAR * NEAR + me % NEAR for s in range(1, FAR)]


def face_peers(me):
    return [neighbour_of(me, f // 2, -1 if f % 2 == 0 else 1) for f in range(6)]


def face_copies(faces, halos, peers, send, recv):
    return [
        pltpu.make_async_remote_copy(
            src_ref=faces[f],
            dst_ref=halos[f ^ 1],
            send_sem=send.at[f],
            recv_sem=recv.at[f],
            device_id=(peers[f],),
            device_id_type=MESH,
        )
        for f in range(6)
    ]


def remote(src, dst, send, recv, peer):
    return pltpu.make_async_remote_copy(
        src_ref=src, dst_ref=dst, send_sem=send, recv_sem=recv, device_id=(peer,), device_id_type=MESH
    )


def blend_cells(u, cells_ref, weights_ref, pick, scaled_ref, parts_ref):
    for a in range(NEAR):
        cell = cells_ref[a]
        total = jnp.sum(jnp.sum(cell, axis=0, keepdims=True), axis=1, keepdims=True)
        scaled_ref[a] = cell / total

    def body(dest, carry):
        share = jnp.sum(weights_ref[dest, u : u + 1, :] * pick, axis=1, keepdims=True)
        total = share[0:1, :] * scaled_ref[0]
        for a in range(1, NEAR):
            total = total + share[a : a + 1, :] * scaled_ref[a]
        parts_ref[dest] = total
        return carry

    lax.fori_loop(0, FAR, body, 0)


def whole_kernel(*refs):
    order_ref, list_ref, blend_ref, tissue_ref, next_ref = refs[:5]
    inputs = refs[5 : 5 + INPUTS]
    out_ref = refs[5 + INPUTS]
    local_refs = refs[6 + INPUTS : 6 + 2 * INPUTS]
    load_sem = refs[6 + 2 * INPUTS]
    refs = refs[7 + 2 * INPUTS :]
    loads = [pltpu.make_async_copy(inputs[i], local_refs[i], load_sem.at[i]) for i in range(INPUTS)]
    est_ref, cells_ref, cell_row_ref, pack_ref, seen_in, place_ref = local_refs[:6]
    fwd_z_ref, fwd_y_ref, tap_z_ref, tap_y_ref, inv_y_ref, inv_z_ref, fwd_yc_ref = local_refs[6:]
    for load in loads:
        load.start()
    cp_refs, own_ref, weights_ref = refs[:2], refs[2], refs[3]
    faces = (refs[4:10], refs[10:16])
    halos = (refs[16:22], refs[22:28])
    near_all, weights_all, parts, held = refs[28:30], refs[30], refs[31:33], refs[33:35]
    scaled_ref, kernel_ref, taps_ref, ext_ref, pp_ref, z_ref, spec_ref = refs[35:42]
    kr_ref, ki_ref, fil_ref, core_ref, q_ref, wide_ref, flat_ref = refs[42:49]
    own_sem, near_send, near_recv, share_send, share_recv = refs[49:54]
    far_send, far_recv, face_send, face_recv = refs[54:58]
    row_ref = flat_ref.reshape(HALF * E, 128)
    tables = (fwd_z_ref, inv_z_ref, fwd_yc_ref, inv_y_ref)
    work = (z_ref, spec_ref, kr_ref, ki_ref, fil_ref, core_ref, q_ref)

    me = lax.axis_index("blk")
    near, far, across = near_peers(me), far_peers(me), face_peers(me)
    barrier = pltpu.get_barrier_semaphore()
    for peer in near + far + across:
        pl.semaphore_signal(barrier, inc=1, device_id=(peer,), device_id_type=MESH)

    taps_ref[...] = jnp.zeros_like(taps_ref)
    for load in loads[:4]:
        load.wait()
    prepare(
        order_ref,
        list_ref,
        blend_ref,
        est_ref,
        cells_ref,
        pack_ref,
        cp_refs[0],
        weights_ref,
        own_ref,
        faces[0],
        row_ref,
    )
    pl.semaphore_wait(barrier, len(near + far + across))

    near_copies = [
        [
            remote(own_ref.at[u], near_all[u].at[me % NEAR], near_send.at[u, s], near_recv.at[u, s], peer)
            for s, peer in enumerate(near)
        ]
        + [pltpu.make_async_copy(own_ref.at[u], near_all[u].at[me % NEAR], own_sem.at[u])]
        for u in range(UPDATES)
    ]
    share_copies = [
        remote(weights_ref, weights_all.at[me // NEAR], share_send.at[s], share_recv.at[s], peer)
        for s, peer in enumerate(far)
    ] + [pltpu.make_async_copy(weights_ref, weights_all.at[me // NEAR], own_sem.at[2])]
    face_copies = [
        [
            remote(faces[u][f], halos[u][f ^ 1], face_send.at[u, f], face_recv.at[u, f], across[f])
            for f in range(6)
        ]
        for u in range(UPDATES)
    ]
    far_copies = [
        [
            remote(parts[u].at[(me // NEAR + 1 + s) % FAR], held[u].at[s], far_send.at[u, s], far_recv.at[u, s], peer)
            for s, peer in enumerate(far)
        ]
        for u in range(UPDATES)
    ]

    def start(copies):
        for copy in copies:
            copy.start()

    def wait(copies):
        for copy in copies:
            copy.wait()

    base = me // NEAR * NEAR
    pick = (cell_row_ref[...] == base + lax.broadcasted_iota(jnp.int32, (NEAR, 128), 0)).astype(F32)

    def widen(it, carry):
        for j in range(8):
            at = pl.multiple_of(it * 1024 + j * 128, 128)
            wide_ref[pl.ds(pl.multiple_of(it * 64 + j * 8, 8), 6), :] = seen_in[:, pl.ds(at, 128)].astype(F32)
        return carry

    def seen_pairs(u):
        view = order_ref[u]

        def load(k, half):
            return wide_ref[pl.ds((half * 3 * GROUPS + k) * 8 + view, GROUPS, stride=24), :]

        flat_to_pairs(load, store_rows(row_ref))

    def spectra(u):
        wait(far_copies[u])
        total = parts[u][me // NEAR]
        for s in range(FAR - 1):
            total = total + held[u][s]
        kernel_ref[...] = total
        tap_spectra(kernel_ref, taps_ref, z_ref, kr_ref, ki_ref, tap_z_ref, tap_y_ref)

    def padded_spectra(u):
        wait(face_copies[u])
        assemble(next_ref, cp_refs[u], halos[u], place_ref, ext_ref, pp_ref)
        forward_planes(pp_ref, z_ref, spec_ref, PAD, fwd_z_ref, fwd_y_ref)

    start(near_copies[0])
    start(share_copies)
    start(face_copies[0])
    start(near_copies[1])
    for load in loads[4:]:
        load.wait()
    lax.fori_loop(0, FLAT // 8, widen, 0)
    seen_pairs(0)
    wait(near_copies[0])
    wait(share_copies)
    blend_cells(0, near_all[0], weights_all, pick, scaled_ref, parts[0])
    start(far_copies[0])
    padded_spectra(0)
    wait(near_copies[1])
    blend_cells(1, near_all[1], weights_all, pick, scaled_ref, parts[1])
    start(far_copies[1])
    spectra(0)
    correct(tissue_ref, cp_refs[0], cp_refs[1], flat_ref, tables, work)
    emit_faces(cp_refs[1], pack_ref, faces[1])
    start(face_copies[1])
    spectra(1)
    seen_pairs(1)
    padded_spectra(1)
    correct(tissue_ref, cp_refs[1], flat_ref, flat_ref, tables, work)

    def load_new(j):
        return row_ref[pl.ds(j, GROUPS, stride=8), :]

    def store_new(k, half, rows):
        out_ref[pl.ds(half * 3 * GROUPS + k, GROUPS, stride=3), :] = rows

    pairs_to_flat(load_new, store_new)


HALO_SHAPES = [FACE_SHAPES[f ^ 1] for f in range(6)]
DMA = pltpu.SemaphoreType.DMA
INPUTS = 13


def whole_call(scalars, est, cells, cell_row, seen):
    inputs = [
        est,
        cells,
        cell_row,
        jnp.asarray(TABLES["pack"]),
        seen,
        jnp.asarray(TABLES["place"]),
        jnp.asarray(TABLES["fwd_z"]),
        jnp.asarray(TABLES["fwd_y"]),
        jnp.asarray(TABLES["tap_z"]),
        jnp.asarray(TABLES["tap_y"]),
        jnp.asarray(TABLES["inv_y"]),
        jnp.asarray(TABLES["inv_z"]),
        jnp.asarray(fwd_y_core()),
    ]
    f32 = [
        (NEAR, CELLROWS, 128),
        (NEAR, CELLROWS, 128),
        (FAR, 8, 128),
        (FAR, CELLROWS, 128),
        (FAR, CELLROWS, 128),
        (FAR - 1, CELLROWS, 128),
        (FAR - 1, CELLROWS, 128),
        (NEAR, CELLROWS, 128),
        (CELLROWS, 128),
        (KS, TAPROWS, 128),
        (HALF, PAD, 128),
        (PLANES, PAD, 128),
        (PLANES, PAD, 128),
        (PLANES, PAD, 128),
        (KS, PAD, 128),
        (KS, PAD, 128),
        (HALF, PAD, 128),
        (HALF, E, 128),
        (PLANES, E, 128),
        (FLAT * 8, 128),
        (HALF, E, 128),
    ]
    scratch = [pltpu.VMEM(x.shape, x.dtype) for x in inputs] + [DMA((INPUTS,))]
    scratch += [pltpu.VMEM(s, F32) for s in [(HALF, E, 128)] * 2 + [(UPDATES, CELLROWS, 128), (8, 128)]]
    scratch += [pltpu.VMEM(s, BF16) for s in FACE_SHAPES * 2 + HALO_SHAPES * 2]
    scratch += [pltpu.VMEM(s, F32) for s in f32]
    scratch += [DMA((3,)), DMA((2, NEAR - 1)), DMA((2, NEAR - 1)), DMA((FAR - 1,)), DMA((FAR - 1,))]
    scratch += [DMA((2, FAR - 1)), DMA((2, FAR - 1)), DMA((2, 6)), DMA((2, 6))]
    return pl.pallas_call(
        whole_kernel,
        out_shape=jax.ShapeDtypeStruct((FLAT, 128), F32),
        in_specs=[SMEM] * 5 + [pl.BlockSpec(memory_space=pl.ANY)] * INPUTS,
        out_specs=VMEM,
        scratch_shapes=scratch,
        compiler_params=pltpu.CompilerParams(collective_id=0, has_side_effects=True),
        name="whole",
    )(*scalars, *inputs)


def local(
    estimate, observed, psf_cells, tissue, neighbours, psf_list, psf_blend, cell_row, view_order
):
    scalars = (
        view_order,
        psf_list.transpose(0, 2, 1).reshape(2, 6),
        psf_blend.transpose(0, 2, 1).reshape(2, 6),
        tissue,
        neighbours,
    )
    result = whole_call(
        scalars,
        estimate.reshape(FLAT, 128),
        psf_cells.reshape(6, 1, KS3),
        cell_row.reshape(1, 128),
        observed.reshape(6, E3),
    )
    return result.reshape(1, E3)


def solution(mesh):
    return jax.shard_map(
        local,
        mesh=mesh,
        in_specs=(
            P("blk", None),
            P("blk", None, None),
            P("blk", None, None),
            P("blk"),
            P("blk", None),
            P("blk", None, None),
            P("blk", None, None),
            P(),
            P(),
        ),
        out_specs=P("blk", None),
        check_vma=False,
    )
```

```python
import functools
import math

import jax
import jax.numpy as jnp
import numpy as np
from jax import lax
from jax.experimental import pallas as pl
from jax.experimental.pallas import tpu as pltpu
from jax.sharding import PartitionSpec as P

E = 48
MARGIN = 8
UPDATES = 2
PAD = 64
KS = 17
E3 = 110592
KS3 = 4913
HALF = 24
PLANES = 40
TAPROWS = 32

CELLROWS = 40
ROWS = UPDATES * CELLROWS

F32 = jnp.float32
BF16 = jnp.bfloat16


def split_np(table):
    hi = np.asarray(table, np.float32).astype(jnp.bfloat16)
    lo = (np.asarray(table, np.float64) - hi.astype(np.float64)).astype(np.float32).astype(jnp.bfloat16)
    return hi, lo


def lane_table(table):
    hi, lo = split_np(table)
    row = np.concatenate([hi, lo], axis=1)
    return np.concatenate([row, row], axis=0)


def row_table(table):
    hi, lo = split_np(table)
    return np.concatenate([hi, hi, lo, lo], axis=1)


def make_tables():
    step = 2.0 * math.pi / PAD
    k = np.arange(PAD)
    ang = (k[:, None] * k[None, :] % PAD) * step
    cos, sin = np.cos(ang), np.sin(ang)
    fwd_z = np.block([[cos, -sin], [sin, cos]])
    inv_z = np.block([[cos, sin], [-sin, cos]]) / PAD
    fwd_y = np.concatenate([cos, sin], axis=0)
    inv_y = np.concatenate([cos[MARGIN : MARGIN + E], sin[MARGIN : MARGIN + E]], axis=0) / PAD
    t = np.arange(KS) - MARGIN
    ang_t = (t[:, None] * k[None, :]) % PAD * step
    tap_z = np.zeros((128, 128))
    tap_z[:KS, :PAD] = np.cos(ang_t)
    tap_z[:KS, PAD:] = -np.sin(ang_t)
    tap_y = np.zeros((128, TAPROWS))
    tap_y[:PAD, :KS] = np.cos(ang_t).T
    tap_y[PAD:, :KS] = np.sin(ang_t).T
    pack = np.zeros((2, 8 * 128, 128), np.float32)
    place = np.zeros((2, 128, 8 * 128), np.float32)
    for p in range(8):
        for s in range(2):
            for z in range(MARGIN):
                slot = p * 16 + s * 8 + z
                pack[0, p * 128 + s * 64 + MARGIN + z, slot] = 1
                pack[1, p * 128 + s * 64 + E + z, slot] = 1
                place[0, slot, p * 128 + s * 64 + z] = 1
                place[1, slot, p * 128 + s * 64 + MARGIN + E + z] = 1
    return dict(
        fwd_z=lane_table(fwd_z),
        inv_z=lane_table(inv_z),
        tap_z=lane_table(tap_z),
        fwd_y=row_table(fwd_y),
        inv_y=row_table(inv_y),
        tap_y=row_table(tap_y),
        pack=pack.astype(jnp.bfloat16),
        place=place.astype(jnp.bfloat16),
    )


TABLES = make_tables()


def split(values):
    hi = values.astype(BF16)
    lo = (values - hi.astype(F32)).astype(BF16)
    return hi, lo


def low_lanes(shape):
    return lax.broadcasted_iota(jnp.int32, shape, len(shape) - 1) < 64


def lane_sign(shape):
    return jnp.where(low_lanes(shape), 1.0, -1.0).astype(F32)


def dot(a, b):
    return lax.dot_general(a, b, (((1,), (0,)), ((), ())), preferred_element_type=F32)


def lanes_dft(rows, table):
    hi, lo = split(rows)
    both = dot(jnp.concatenate([hi, lo], axis=1), table)
    return both[:, :128] + both[:, 128:]


def rows_dft(planes, table, count, inverse):
    sign = lane_sign((count, 128))
    if inverse:
        sign = -sign
    out = []
    for a in range(0, len(planes), 2):
        cols = []
        for plane in planes[a : a + 2]:
            hi, lo = split(plane)
            cols.append(jnp.concatenate([hi, lo, hi, lo], axis=0))
        rhs = jnp.concatenate(cols, axis=1) if len(cols) > 1 else cols[0]
        both = dot(table, rhs)
        for b in range(len(cols)):
            c_part = both[:count, b * 128 : (b + 1) * 128]
            s_part = both[count : 2 * count, b * 128 : (b + 1) * 128]
            out.append(c_part + sign * pltpu.roll(s_part, 64, 1))
    return out


def emit_faces(cp_ref, pack_ref, faces):
    xm_ref, xp_ref, ym_ref, yp_ref, zm_ref, zp_ref = faces
    low = low_lanes((E, 128))
    for j in range(4):
        near = jnp.where(low, cp_ref[j], pltpu.roll(cp_ref[4 + j], 64, 1))
        xm_ref[j * E : (j + 1) * E, :] = near.astype(BF16)
        near = jnp.where(low, pltpu.roll(cp_ref[16 + j], 64, 1), cp_ref[20 + j])
        xp_ref[j * E : (j + 1) * E, :] = near.astype(BF16)
    ym_ref[...] = cp_ref[:, 0:8, :].reshape(HALF * 8, 128).astype(BF16)
    yp_ref[...] = cp_ref[:, E - 8 : E, :].reshape(HALF * 8, 128).astype(BF16)
    for g in range(3):
        wide = jnp.concatenate([cp_ref[g * 8 + p].astype(BF16) for p in range(8)], axis=1)
        zm_ref[g * E : (g + 1) * E, :] = dot(wide, pack_ref[0]).astype(BF16)
        zp_ref[g * E : (g + 1) * E, :] = dot(wide, pack_ref[1]).astype(BF16)


FACE_SHAPES = [(4 * E, 128), (4 * E, 128), (HALF * 8, 128), (HALF * 8, 128), (3 * E, 128), (3 * E, 128)]


def flat_to_pairs(load, store):
    for j in range(8):
        total = None
        for half in range(2):
            first = 48 * j
            k, lane = first // 128, first % 128
            base = MARGIN + 64 * half
            value = load(k, half)
            part = value if lane == base else pltpu.roll(value, (base - lane) % 128, 1)
            at = lax.broadcasted_iota(jnp.int32, part.shape, 1) - base
            length = min(48, 128 - lane)
            picked = jnp.where((at >= 0) & (at < length), part, 0.0)
            if length < 48:
                more = pltpu.roll(load(k + 1, half), base + length, 1)
                picked = jnp.where((at >= length) & (at < 48), more, picked)
            total = picked if total is None else total + picked
        store(j, total)


def pairs_to_flat(load, store):
    for half in range(2):
        for k in range(3):
            total = None
            for j in range(8):
                lane = 48 * j - 128 * k
                if lane <= -48 or lane >= 128:
                    continue
                value = pltpu.roll(load(j), (lane - MARGIN - 64 * half) % 128, 1)
                at = lax.broadcasted_iota(jnp.int32, value.shape, 1) - lane
                picked = jnp.where((at >= 0) & (at < 48), value, 0.0)
                total = picked if total is None else total + picked
            store(k, half, total)


GROUPS = HALF * E // 8
FLAT = E3 // 128


def load_flat(ref):
    return lambda k, half: ref[pl.ds(half * 3 * GROUPS + k, GROUPS, stride=3), :]


def store_rows(ref):
    def store(j, rows):
        ref[pl.ds(j, GROUPS, stride=8), :] = rows

    return store


def prepare_cells(order_ref, list_ref, blend_ref, cells_ref, weights_ref, own_ref):
    number = lax.broadcasted_iota(jnp.int32, (1, 128), 1)
    weights_ref[...] = jnp.zeros_like(weights_ref)
    own_ref[...] = jnp.zeros_like(own_ref)
    for u in range(UPDATES):
        view = order_ref[u]
        first = jnp.full((1, 128), blend_ref[0, view], F32)
        second = jnp.full((1, 128), blend_ref[1, view], F32)
        total = first + second
        weights_ref[u : u + 1, :] = jnp.where(number == list_ref[0, view], first / total, 0.0) + jnp.where(
            number == list_ref[1, view], second / total, 0.0
        )
        for i in range(KS3 // 128):
            own_ref[u, i : i + 1, :] = cells_ref[view, :, i * 128 : (i + 1) * 128]
        tail = KS3 // 128 * 128
        i = KS3 // 128
        own_ref[u, i : i + 1, 0 : KS3 - tail] = cells_ref[view, :, tail:KS3]


def prepare_block(est_ref, pack_ref, cp_ref, faces):
    row_ref = cp_ref.reshape(HALF * E, 128)
    flat_to_pairs(load_flat(est_ref), store_rows(row_ref))
    emit_faces(cp_ref, pack_ref, faces)


def forward_planes(src_ref, z_ref, spec_ref, rows, fwd_z_ref, fwd_y_ref):
    group = 20

    def z_body(it, carry):
        block = src_ref[pl.ds(it * group, group)].reshape(group * rows, 128)
        z_ref[pl.ds(it * group, group), 0:rows, :] = lanes_dft(block, fwd_z_ref[...]).reshape(group, rows, 128)
        return carry

    lax.fori_loop(0, PLANES // group, z_body, 0)

    def y_body(it, carry):
        planes = [z_ref[it * group + j, 0:rows, :] for j in range(group)]
        for j, plane in enumerate(rows_dft(planes, fwd_y_ref[...], PAD, False)):
            spec_ref[it * group + j] = plane
        return carry

    lax.fori_loop(0, PLANES // group, y_body, 0)


def filter_planes(spec_ref, kr_ref, ki_ref, out_ref, conjugate):
    group = 12
    sign = lane_sign((8, 128))
    if not conjugate:
        sign = -sign

    def body(kb, carry):
        rows = pl.ds(pl.multiple_of(kb * 8, 8), 8)
        for first in range(0, HALF, group):
            values = {}
            acc_r, acc_i = [None] * group, [None] * group
            for d in range(KS):
                tap = d if conjugate else KS - 1 - d
                kr = kr_ref[tap, rows, :]
                ki = ki_ref[tap, rows, :]
                for j in range(group):
                    m = first + j + d
                    if m not in values:
                        values[m] = spec_ref[m, rows, :]
                    if d == 0:
                        acc_r[j] = kr * values[m]
                        acc_i[j] = ki * values[m]
                    else:
                        acc_r[j] = acc_r[j] + kr * values[m]
                        acc_i[j] = acc_i[j] + ki * values[m]
            for j in range(group):
                out_ref[first + j, rows, :] = acc_r[j] + sign * pltpu.roll(acc_i[j], 64, 1)
        return carry

    lax.fori_loop(0, PAD // 8, body, 0)


def inverse_planes(spec_ref, y_ref, out_ref, inv_y_ref, inv_z_ref):
    group = 12

    def y_body(it, carry):
        planes = [spec_ref[it * group + j] for j in range(group)]
        for j, plane in enumerate(rows_dft(planes, inv_y_ref[...], E, True)):
            y_ref[it * group + j, 0:E, :] = plane
        return carry

    lax.fori_loop(0, HALF // group, y_body, 0)

    def z_body(it, carry):
        block = y_ref[pl.ds(it * group, group), 0:E, :].reshape(group * E, 128)
        out_ref[pl.ds(it * group, group)] = lanes_dft(block, inv_z_ref[...]).reshape(group, E, 128)
        return carry

    lax.fori_loop(0, HALF // group, z_body, 0)


def tap_spectra(flat_ref, taps_ref, z_ref, kr_ref, ki_ref, tap_z_ref, tap_y_ref):
    lane = lax.broadcasted_iota(jnp.int32, (1, 128), 1)
    for r in range(KS * KS):
        i, at = KS * r // 128, KS * r % 128
        run = pltpu.roll(flat_ref[i : i + 1, :], (-at) % 128, 1)
        if at + KS > 128:
            more = pltpu.roll(flat_ref[i + 1 : i + 2, :], (-at) % 128, 1)
            run = jnp.where(lane < 128 - at, run, more)
        taps_ref[r // KS, r % KS : r % KS + 1, :] = run
    low_full = low_lanes((PAD, 128))
    rows = lanes_dft(taps_ref[...].reshape(KS * TAPROWS, 128), tap_z_ref[...])
    z_ref[0:KS, 0:TAPROWS, :] = rows.reshape(KS, TAPROWS, 128)
    planes = [z_ref[d, 0:TAPROWS, :] for d in range(KS)]
    for d, spec in enumerate(rows_dft(planes, tap_y_ref[...], PAD, False)):
        other = pltpu.roll(spec, 64, 1)
        kr_ref[d] = jnp.where(low_full, spec, other)
        ki_ref[d] = jnp.where(low_full, other, spec)


def assemble(next_ref, cp_ref, halos, place_ref, ext_ref, pp_ref):
    hxm_ref, hxp_ref, hym_ref, hyp_ref, hzm_ref, hzp_ref = halos
    low_core = low_lanes((E, 128))
    low_row = low_lanes((8, 128))

    def face(ref, f):
        return jnp.where(next_ref[0, f] >= 0, ref[...].astype(F32), 0.0)

    ext_ref[:, 0:8, :] = face(hym_ref, 2).reshape(HALF, 8, 128)
    ext_ref[:, 56:64, :] = face(hyp_ref, 3).reshape(HALF, 8, 128)
    zm_all = face(hzm_ref, 4).astype(BF16)
    zp_all = face(hzp_ref, 5).astype(BF16)
    for g in range(3):
        zm = dot(zm_all[g * E : (g + 1) * E], place_ref[0])
        zp = dot(zp_all[g * E : (g + 1) * E], place_ref[1])
        for p in range(8):
            lanes = slice(p * 128, (p + 1) * 128)
            ext_ref[g * 8 + p, 8:56, :] = cp_ref[g * 8 + p] + zm[:, lanes] + zp[:, lanes]
    xm = face(hxm_ref, 0).reshape(4, E, 128)
    xp = face(hxp_ref, 1).reshape(4, E, 128)
    pp_ref[8:32] = ext_ref[...]
    for j in range(8):
        for rows in (slice(0, 8), slice(56, 64)):
            near = ext_ref[16 + j, rows, :]
            pp_ref[j, rows, :] = pltpu.roll(jnp.where(low_row, near, 0.0), 64, 1)
            near = ext_ref[j, rows, :]
            pp_ref[32 + j, rows, :] = pltpu.roll(jnp.where(low_row, 0.0, near), 64, 1)
        before = xm[j] if j < 4 else pltpu.roll(xm[j - 4], 64, 1)
        after = pltpu.roll(xp[j], 64, 1) if j < 4 else xp[j - 4]
        pp_ref[j, 8:56, :] = jnp.where(low_core, before, pltpu.roll(ext_ref[16 + j, 8:56, :], 64, 1))
        pp_ref[32 + j, 8:56, :] = jnp.where(low_core, pltpu.roll(ext_ref[j, 8:56, :], 64, 1), after)


def correct(tissue_ref, cp_ref, new_ref, seen_ref, tables, work):
    fwd_z_ref, inv_z_ref, fwd_yc_ref, inv_y_ref = tables
    z_ref, spec_ref, kr_ref, ki_ref, fil_ref, core_ref, q_ref = work
    low_core = low_lanes((E, 128))
    filter_planes(spec_ref, kr_ref, ki_ref, fil_ref, False)
    inverse_planes(fil_ref, z_ref, core_ref, inv_y_ref, inv_z_ref)

    lane = lax.broadcasted_iota(jnp.int32, (E, 128), 1) % 64
    inside = (lane >= MARGIN) & (lane < MARGIN + E)

    def ratio_body(it, carry):
        for o in [it * 4 + j for j in range(4)]:
            q_ref[o + 8] = jnp.where(inside, seen_ref[o] / jnp.where(inside, core_ref[o], 1.0), 0.0)
        return carry

    lax.fori_loop(0, HALF // 4, ratio_body, 0)
    for j in range(8):
        q_ref[j] = pltpu.roll(jnp.where(low_core, q_ref[24 + j], 0.0), 64, 1)
        q_ref[32 + j] = pltpu.roll(jnp.where(low_core, 0.0, q_ref[8 + j]), 64, 1)

    forward_planes(q_ref, z_ref, spec_ref, E, fwd_z_ref, fwd_yc_ref)
    filter_planes(spec_ref, kr_ref, ki_ref, fil_ref, True)
    inverse_planes(fil_ref, z_ref, core_ref, inv_y_ref, inv_z_ref)

    alive = tissue_ref[0] > 0

    def finish(it, carry):
        for o in [it * 4 + j for j in range(4)]:
            old = cp_ref[o]
            new_ref[o] = jnp.where(jnp.logical_and(inside, alive), old * core_ref[o], old)
        return carry

    lax.fori_loop(0, HALF // 4, finish, 0)


VMEM = pl.BlockSpec(memory_space=pltpu.VMEM)
SMEM = pl.BlockSpec(memory_space=pltpu.SMEM)


def fwd_y_core():
    full = TABLES["fwd_y"]
    return np.concatenate([full[:, s * PAD + MARGIN : s * PAD + MARGIN + E] for s in range(4)], axis=1)


GRID = (4, 4, 8)


def coords_of(b):
    return (
        b % 2 + 2 * ((b // 8) % 2),
        (b // 2) % 2 + 2 * ((b // 16) % 2),
        (b // 64) % 2 + 2 * ((b // 4) % 2) + 4 * ((b // 32) % 2),
    )


def block_at(c):
    return (
        c[0] % 2 + 2 * (c[1] % 2) + 4 * ((c[2] // 2) % 2) + 8 * (c[0] // 2) + 16 * (c[1] // 2)
        + 32 * (c[2] // 4) + 64 * (c[2] % 2)
    )


def neighbour_of(b, axis, step):
    c = list(coords_of(b))
    c[axis] = (c[axis] + step + GRID[axis]) % GRID[axis]
    return block_at(c)


MESH = pl.DeviceIdType.MESH
NEAR = 8
FAR = 16


def near_peers(me):
    base = me // NEAR * NEAR
    return [base + (me % NEAR + s) % NEAR for s in range(1, NEAR)]


def far_peers(me):
    return [(me // NEAR + s) % FAR * NEAR + me % NEAR for s in range(1, FAR)]


def face_peers(me):
    return [neighbour_of(me, f // 2, -1 if f % 2 == 0 else 1) for f in range(6)]


def face_copies(faces, halos, peers, send, recv):
    return [
        pltpu.make_async_remote_copy(
            src_ref=faces[f],
            dst_ref=halos[f ^ 1],
            send_sem=send.at[f],
            recv_sem=recv.at[f],
            device_id=(peers[f],),
            device_id_type=MESH,
        )
        for f in range(6)
    ]


def remote(src, dst, send, recv, peer):
    return pltpu.make_async_remote_copy(
        src_ref=src, dst_ref=dst, send_sem=send, recv_sem=recv, device_id=(peer,), device_id_type=MESH
    )


def blend_cells(u, cells_ref, weights_ref, pick, scaled_ref, parts_ref):
    for a in range(NEAR):
        cell = cells_ref[a]
        total = jnp.sum(jnp.sum(cell, axis=0, keepdims=True), axis=1, keepdims=True)
        scaled_ref[a] = cell / total

    def body(it, carry):
        for dest in [it * 8 + j for j in range(8)]:
            share = jnp.sum(weights_ref[dest, u : u + 1, :] * pick, axis=1, keepdims=True)
            total = share[0:1, :] * scaled_ref[0]
            for a in range(1, NEAR):
                total = total + share[a : a + 1, :] * scaled_ref[a]
            parts_ref[dest] = total
        return carry

    lax.fori_loop(0, FAR // 8, body, 0)


def whole_kernel(*refs):
    order_ref, list_ref, blend_ref, tissue_ref, next_ref = refs[:5]
    inputs = refs[5 : 5 + INPUTS]
    out_ref = refs[5 + INPUTS]
    local_refs = refs[6 + INPUTS : 6 + 2 * INPUTS]
    load_sem = refs[6 + 2 * INPUTS]
    refs = refs[7 + 2 * INPUTS :]
    loads = [pltpu.make_async_copy(inputs[i], local_refs[i], load_sem.at[i]) for i in range(INPUTS)]
    cells_ref, est_ref, pack_ref, cell_row_ref, seen_in, place_ref = local_refs[:6]
    fwd_z_ref, fwd_y_ref, tap_z_ref, tap_y_ref, inv_y_ref, inv_z_ref, fwd_yc_ref = local_refs[6:]
    for load in loads:
        load.start()
    cp_refs, own_ref, weights_ref = refs[:2], refs[2], refs[3]
    faces = (refs[4:10], refs[10:16])
    halos = (refs[16:22], refs[22:28])
    near_all, weights_all, parts, held = refs[28:30], refs[30], refs[31:33], refs[33:35]
    scaled_ref, kernel_ref, taps_ref, ext_ref, pp_ref, z_ref, spec_ref = refs[35:42]
    kr_ref, ki_ref, fil_ref, core_ref, q_ref, wide_ref, flat_ref = refs[42:49]
    own_sem, near_send, near_recv, share_send, share_recv = refs[49:54]
    far_send, far_recv, face_send, face_recv = refs[54:58]
    row_ref = flat_ref.reshape(HALF * E, 128)
    tables = (fwd_z_ref, inv_z_ref, fwd_yc_ref, inv_y_ref)
    work = (z_ref, spec_ref, kr_ref, ki_ref, fil_ref, core_ref, q_ref)

    me = lax.axis_index("blk")
    near, far, across = near_peers(me), far_peers(me), face_peers(me)
    barrier = pltpu.get_barrier_semaphore()
    for peer in near + far + across:
        pl.semaphore_signal(barrier, inc=1, device_id=(peer,), device_id_type=MESH)

    loads[0].wait()
    prepare_cells(order_ref, list_ref, blend_ref, cells_ref, weights_ref, own_ref)
    taps_ref[...] = jnp.zeros_like(taps_ref)
    pl.semaphore_wait(barrier, len(near + far + across))

    near_copies = [
        [
            remote(own_ref.at[u], near_all[u].at[me % NEAR], near_send.at[u, s], near_recv.at[u, s], peer)
            for s, peer in enumerate(near)
        ]
        + [pltpu.make_async_copy(own_ref.at[u], near_all[u].at[me % NEAR], own_sem.at[u])]
        for u in range(UPDATES)
    ]
    share_copies = [
        remote(weights_ref, weights_all.at[me // NEAR], share_send.at[s], share_recv.at[s], peer)
        for s, peer in enumerate(far)
    ] + [pltpu.make_async_copy(weights_ref, weights_all.at[me // NEAR], own_sem.at[2])]
    face_copies = [
        [
            remote(faces[u][f], halos[u][f ^ 1], face_send.at[u, f], face_recv.at[u, f], across[f])
            for f in range(6)
        ]
        for u in range(UPDATES)
    ]
    far_copies = [
        [
            remote(parts[u].at[(me // NEAR + 1 + s) % FAR], held[u].at[s], far_send.at[u, s], far_recv.at[u, s], peer)
            for s, peer in enumerate(far)
        ]
        for u in range(UPDATES)
    ]

    def start(copies):
        for copy in copies:
            copy.start()

    def wait(copies):
        for copy in copies:
            copy.wait()

    base = me // NEAR * NEAR

    def widen(it, carry):
        for j in range(8):
            at = pl.multiple_of(it * 1024 + j * 128, 128)
            wide_ref[pl.ds(pl.multiple_of(it * 64 + j * 8, 8), 6), :] = seen_in[:, pl.ds(at, 128)].astype(F32)
        return carry

    def seen_pairs(u):
        view = order_ref[u]

        def load(k, half):
            return wide_ref[pl.ds((half * 3 * GROUPS + k) * 8 + view, GROUPS, stride=24), :]

        flat_to_pairs(load, store_rows(row_ref))

    def spectra(u):
        total = parts[u][me // NEAR]
        for s in range(FAR - 1):
            total = total + held[u][s]
        kernel_ref[...] = total
        tap_spectra(kernel_ref, taps_ref, z_ref, kr_ref, ki_ref, tap_z_ref, tap_y_ref)

    def padded_spectra(u):
        wait(face_copies[u])
        assemble(next_ref, cp_refs[u], halos[u], place_ref, ext_ref, pp_ref)
        forward_planes(pp_ref, z_ref, spec_ref, PAD, fwd_z_ref, fwd_y_ref)

    start(near_copies[0])
    start(share_copies)
    for load in loads[1:3]:
        load.wait()
    prepare_block(est_ref, pack_ref, cp_refs[0], faces[0])
    start(face_copies[0])
    for load in loads[3:]:
        load.wait()
    pick = (cell_row_ref[...] == base + lax.broadcasted_iota(jnp.int32, (NEAR, 128), 0)).astype(F32)
    lax.fori_loop(0, FLAT // 8, widen, 0)
    wait(near_copies[0])
    wait(share_copies)
    blend_cells(0, near_all[0], weights_all, pick, scaled_ref, parts[0])
    start(far_copies[0])
    start(near_copies[1])
    seen_pairs(0)
    padded_spectra(0)
    wait(near_copies[1])
    blend_cells(1, near_all[1], weights_all, pick, scaled_ref, parts[1])
    wait(far_copies[0])
    start(far_copies[1])
    spectra(0)
    correct(tissue_ref, cp_refs[0], cp_refs[1], flat_ref, tables, work)
    emit_faces(cp_refs[1], pack_ref, faces[1])
    start(face_copies[1])
    wait(far_copies[1])
    spectra(1)
    seen_pairs(1)
    padded_spectra(1)
    correct(tissue_ref, cp_refs[1], flat_ref, flat_ref, tables, work)

    def load_new(j):
        return row_ref[pl.ds(j, GROUPS, stride=8), :]

    def store_new(k, half, rows):
        out_ref[pl.ds(half * 3 * GROUPS + k, GROUPS, stride=3), :] = rows

    pairs_to_flat(load_new, store_new)


HALO_SHAPES = [FACE_SHAPES[f ^ 1] for f in range(6)]
DMA = pltpu.SemaphoreType.DMA
INPUTS = 13


def whole_call(scalars, est, cells, cell_row, seen):
    inputs = [
        cells,
        est,
        jnp.asarray(TABLES["pack"]),
        cell_row,
        seen,
        jnp.asarray(TABLES["place"]),
        jnp.asarray(TABLES["fwd_z"]),
        jnp.asarray(TABLES["fwd_y"]),
        jnp.asarray(TABLES["tap_z"]),
        jnp.asarray(TABLES["tap_y"]),
        jnp.asarray(TABLES["inv_y"]),
        jnp.asarray(TABLES["inv_z"]),
        jnp.asarray(fwd_y_core()),
    ]
    f32 = [
        (NEAR, CELLROWS, 128),
        (NEAR, CELLROWS, 128),
        (FAR, 8, 128),
        (FAR, CELLROWS, 128),
        (FAR, CELLROWS, 128),
        (FAR - 1, CELLROWS, 128),
        (FAR - 1, CELLROWS, 128),
        (NEAR, CELLROWS, 128),
        (CELLROWS, 128),
        (KS, TAPROWS, 128),
        (HALF, PAD, 128),
        (PLANES, PAD, 128),
        (PLANES, PAD, 128),
        (PLANES, PAD, 128),
        (KS, PAD, 128),
        (KS, PAD, 128),
        (HALF, PAD, 128),
        (HALF, E, 128),
        (PLANES, E, 128),
        (FLAT * 8, 128),
        (HALF, E, 128),
    ]
    scratch = [pltpu.VMEM(x.shape, x.dtype) for x in inputs] + [DMA((INPUTS,))]
    scratch += [pltpu.VMEM(s, F32) for s in [(HALF, E, 128)] * 2 + [(UPDATES, CELLROWS, 128), (8, 128)]]
    scratch += [pltpu.VMEM(s, BF16) for s in FACE_SHAPES * 2 + HALO_SHAPES * 2]
    scratch += [pltpu.VMEM(s, F32) for s in f32]
    scratch += [DMA((3,)), DMA((2, NEAR - 1)), DMA((2, NEAR - 1)), DMA((FAR - 1,)), DMA((FAR - 1,))]
    scratch += [DMA((2, FAR - 1)), DMA((2, FAR - 1)), DMA((2, 6)), DMA((2, 6))]
    return pl.pallas_call(
        whole_kernel,
        out_shape=jax.ShapeDtypeStruct((FLAT, 128), F32),
        in_specs=[SMEM] * 5 + [pl.BlockSpec(memory_space=pl.ANY)] * INPUTS,
        out_specs=VMEM,
        scratch_shapes=scratch,
        compiler_params=pltpu.CompilerParams(collective_id=0, has_side_effects=True),
        name="whole",
    )(*scalars, *inputs)


def local(
    estimate, observed, psf_cells, tissue, neighbours, psf_list, psf_blend, cell_row, view_order
):
    scalars = (
        view_order,
        psf_list.transpose(0, 2, 1).reshape(2, 6),
        psf_blend.transpose(0, 2, 1).reshape(2, 6),
        tissue,
        neighbours,
    )
    result = whole_call(
        scalars,
        estimate.reshape(FLAT, 128),
        psf_cells.reshape(6, 1, KS3),
        cell_row.reshape(1, 128),
        observed.reshape(6, E3),
    )
    return result.reshape(1, E3)


def solution(mesh):
    return jax.shard_map(
        local,
        mesh=mesh,
        in_specs=(
            P("blk", None),
            P("blk", None, None),
            P("blk", None, None),
            P("blk"),
            P("blk", None),
            P("blk", None, None),
            P("blk", None, None),
            P(),
            P(),
        ),
        out_specs=P("blk", None),
        check_vma=False,
    )
```

```python
import functools
import math

import jax
import jax.numpy as jnp
import numpy as np
from jax import lax
from jax.experimental import pallas as pl
from jax.experimental.pallas import tpu as pltpu
from jax.sharding import PartitionSpec as P

E = 48
MARGIN = 8
UPDATES = 2
PAD = 64
KS = 17
E3 = 110592
KS3 = 4913
HALF = 24
PLANES = 40
TAPROWS = 32

CELLROWS = 40
ROWS = UPDATES * CELLROWS

F32 = jnp.float32
BF16 = jnp.bfloat16


def split_np(table):
    hi = np.asarray(table, np.float32).astype(jnp.bfloat16)
    lo = (np.asarray(table, np.float64) - hi.astype(np.float64)).astype(np.float32).astype(jnp.bfloat16)
    return hi, lo


def lane_table(table):
    hi, lo = split_np(table)
    row = np.concatenate([hi, lo], axis=1)
    return np.concatenate([row, row], axis=0)


def row_table(table):
    hi, lo = split_np(table)
    return np.concatenate([hi, hi, lo], axis=1)


def make_tables():
    step = 2.0 * math.pi / PAD
    k = np.arange(PAD)
    ang = (k[:, None] * k[None, :] % PAD) * step
    cos, sin = np.cos(ang), np.sin(ang)
    fwd_z = np.block([[cos, -sin], [sin, cos]])
    inv_z = np.block([[cos, sin], [-sin, cos]]) / PAD
    half = (np.arange(PAD // 2)[:, None] + 0.5) * step
    fwd_y = np.concatenate([np.cos(half * k), np.sin(half * k)], axis=0)
    core = k[MARGIN : MARGIN + E]
    inv_y = np.concatenate([np.cos(half * core), np.sin(half * core)], axis=0).T / PAD
    t = np.arange(KS) - MARGIN
    ang_t = (t[:, None] * k[None, :]) % PAD * step
    tap_z = np.zeros((128, 128))
    tap_z[:KS, :PAD] = np.cos(ang_t)
    tap_z[:KS, PAD:] = -np.sin(ang_t)
    tap_y = np.zeros((PAD, TAPROWS))
    tap_y[:, :KS] = np.concatenate([np.cos(half * t), np.sin(half * t)], axis=0)
    pack = np.zeros((2, 8 * 128, 128), np.float32)
    place = np.zeros((2, 128, 8 * 128), np.float32)
    for p in range(8):
        for s in range(2):
            for z in range(MARGIN):
                slot = p * 16 + s * 8 + z
                pack[0, p * 128 + s * 64 + MARGIN + z, slot] = 1
                pack[1, p * 128 + s * 64 + E + z, slot] = 1
                place[0, slot, p * 128 + s * 64 + z] = 1
                place[1, slot, p * 128 + s * 64 + MARGIN + E + z] = 1
    return dict(
        fwd_z=lane_table(fwd_z),
        inv_z=lane_table(inv_z),
        tap_z=lane_table(tap_z),
        fwd_y=row_table(fwd_y),
        inv_y=row_table(inv_y),
        tap_y=row_table(tap_y),
        pack=pack.astype(jnp.bfloat16),
        place=place.astype(jnp.bfloat16),
    )


TABLES = make_tables()


def split(values):
    hi = values.astype(BF16)
    lo = (values - hi.astype(F32)).astype(BF16)
    return hi, lo


def low_lanes(shape):
    return lax.broadcasted_iota(jnp.int32, shape, len(shape) - 1) < 64


def lane_sign(shape):
    return jnp.where(low_lanes(shape), 1.0, -1.0).astype(F32)


def dot(a, b):
    return lax.dot_general(a, b, (((1,), (0,)), ((), ())), preferred_element_type=F32)


def lanes_dft(rows, table):
    hi, lo = split(rows)
    both = dot(jnp.concatenate([hi, lo], axis=1), table)
    return both[:, :128] + both[:, 128:]


def rows_dot(planes, table):
    out = []
    for a in range(0, len(planes), 2):
        cols = []
        for plane in planes[a : a + 2]:
            hi, lo = split(plane)
            cols.append(jnp.concatenate([hi, lo, hi], axis=0))
        both = dot(table, jnp.concatenate(cols, axis=1) if len(cols) > 1 else cols[0])
        out += [both[:, b * 128 : (b + 1) * 128] for b in range(len(cols))]
    return out


def rows_forward(planes, table):
    sign = lane_sign((PAD // 2, 128))
    out = []
    for both in rows_dot(planes, table):
        turned = sign * pltpu.roll(both[PAD // 2 :], 64, 1)
        out.append((both[: PAD // 2] + turned, both[: PAD // 2] - turned))
    return out


def rows_inverse(planes, table):
    sign = -lane_sign((PAD // 2, 128))
    folded = []
    for plane in planes:
        plus, minus = plane[: PAD // 2], plane[PAD // 2 :]
        folded.append(jnp.concatenate([plus + minus, sign * pltpu.roll(plus - minus, 64, 1)], axis=0))
    return rows_dot(folded, table)


def emit_faces(cp_ref, pack_ref, faces):
    xm_ref, xp_ref, ym_ref, yp_ref, zm_ref, zp_ref = faces
    low = low_lanes((E, 128))
    for j in range(4):
        near = jnp.where(low, cp_ref[j], pltpu.roll(cp_ref[4 + j], 64, 1))
        xm_ref[j * E : (j + 1) * E, :] = near.astype(BF16)
        near = jnp.where(low, pltpu.roll(cp_ref[16 + j], 64, 1), cp_ref[20 + j])
        xp_ref[j * E : (j + 1) * E, :] = near.astype(BF16)
    ym_ref[...] = cp_ref[:, 0:8, :].reshape(HALF * 8, 128).astype(BF16)
    yp_ref[...] = cp_ref[:, E - 8 : E, :].reshape(HALF * 8, 128).astype(BF16)
    for g in range(3):
        wide = jnp.concatenate([cp_ref[g * 8 + p].astype(BF16) for p in range(8)], axis=1)
        zm_ref[g * E : (g + 1) * E, :] = dot(wide, pack_ref[0]).astype(BF16)
        zp_ref[g * E : (g + 1) * E, :] = dot(wide, pack_ref[1]).astype(BF16)


FACE_SHAPES = [(4 * E, 128), (4 * E, 128), (HALF * 8, 128), (HALF * 8, 128), (3 * E, 128), (3 * E, 128)]


def flat_to_pairs(load, store):
    for j in range(8):
        total = None
        for half in range(2):
            first = 48 * j
            k, lane = first // 128, first % 128
            base = MARGIN + 64 * half
            value = load(k, half)
            part = value if lane == base else pltpu.roll(value, (base - lane) % 128, 1)
            at = lax.broadcasted_iota(jnp.int32, part.shape, 1) - base
            length = min(48, 128 - lane)
            picked = jnp.where((at >= 0) & (at < length), part, 0.0)
            if length < 48:
                more = pltpu.roll(load(k + 1, half), base + length, 1)
                picked = jnp.where((at >= length) & (at < 48), more, picked)
            total = picked if total is None else total + picked
        store(j, total)


def pairs_to_flat(load, store):
    for half in range(2):
        for k in range(3):
            total = None
            for j in range(8):
                lane = 48 * j - 128 * k
                if lane <= -48 or lane >= 128:
                    continue
                value = pltpu.roll(load(j), (lane - MARGIN - 64 * half) % 128, 1)
                at = lax.broadcasted_iota(jnp.int32, value.shape, 1) - lane
                picked = jnp.where((at >= 0) & (at < 48), value, 0.0)
                total = picked if total is None else total + picked
            store(k, half, total)


GROUPS = HALF * E // 8
FLAT = E3 // 128


def load_flat(ref):
    return lambda k, half: ref[pl.ds(half * 3 * GROUPS + k, GROUPS, stride=3), :]


def store_rows(ref):
    def store(j, rows):
        ref[pl.ds(j, GROUPS, stride=8), :] = rows

    return store


def prepare_cells(order_ref, list_ref, blend_ref, cells_ref, weights_ref, own_ref):
    number = lax.broadcasted_iota(jnp.int32, (1, 128), 1)
    weights_ref[...] = jnp.zeros_like(weights_ref)
    own_ref[...] = jnp.zeros_like(own_ref)
    for u in range(UPDATES):
        view = order_ref[u]
        first = jnp.full((1, 128), blend_ref[0, view], F32)
        second = jnp.full((1, 128), blend_ref[1, view], F32)
        total = first + second
        weights_ref[u : u + 1, :] = jnp.where(number == list_ref[0, view], first / total, 0.0) + jnp.where(
            number == list_ref[1, view], second / total, 0.0
        )
        for i in range(KS3 // 128):
            own_ref[u, i : i + 1, :] = cells_ref[view, :, i * 128 : (i + 1) * 128]
        tail = KS3 // 128 * 128
        i = KS3 // 128
        own_ref[u, i : i + 1, 0 : KS3 - tail] = cells_ref[view, :, tail:KS3]


def prepare_block(est_ref, pack_ref, cp_ref, faces):
    row_ref = cp_ref.reshape(HALF * E, 128)
    flat_to_pairs(load_flat(est_ref), store_rows(row_ref))
    emit_faces(cp_ref, pack_ref, faces)


def forward_planes(src_ref, z_ref, spec_ref, rows, fwd_z_ref, fwd_y_ref):
    group = 20

    def z_body(it, carry):
        block = src_ref[pl.ds(it * group, group)].reshape(group * rows, 128)
        z_ref[pl.ds(it * group, group), 0:rows, :] = lanes_dft(block, fwd_z_ref[...]).reshape(group, rows, 128)
        return carry

    lax.fori_loop(0, PLANES // group, z_body, 0)

    def y_body(it, carry):
        planes = [z_ref[it * group + j, 0:rows, :] for j in range(group)]
        for j, (plus, minus) in enumerate(rows_forward(planes, fwd_y_ref[...])):
            spec_ref[it * group + j, 0 : PAD // 2, :] = plus
            spec_ref[it * group + j, PAD // 2 : PAD, :] = minus
        return carry

    lax.fori_loop(0, PLANES // group, y_body, 0)


def filter_planes(spec_ref, kr_ref, ki_ref, out_ref, conjugate):
    group = 12
    sign = lane_sign((8, 128))
    if not conjugate:
        sign = -sign

    def body(kb, carry):
        rows = pl.ds(pl.multiple_of(kb * 8, 8), 8)
        for first in range(0, HALF, group):
            values = {}
            acc_r, acc_i = [None] * group, [None] * group
            for d in range(KS):
                tap = d if conjugate else KS - 1 - d
                kr = kr_ref[tap, rows, :]
                ki = ki_ref[tap, rows, :]
                for j in range(group):
                    m = first + j + d
                    if m not in values:
                        values[m] = spec_ref[m, rows, :]
                    if d == 0:
                        acc_r[j] = kr * values[m]
                        acc_i[j] = ki * values[m]
                    else:
                        acc_r[j] = acc_r[j] + kr * values[m]
                        acc_i[j] = acc_i[j] + ki * values[m]
            for j in range(group):
                out_ref[first + j, rows, :] = acc_r[j] + sign * pltpu.roll(acc_i[j], 64, 1)
        return carry

    lax.fori_loop(0, PAD // 8, body, 0)


def inverse_planes(spec_ref, y_ref, out_ref, inv_y_ref, inv_z_ref):
    group = 12

    def y_body(it, carry):
        planes = [spec_ref[it * group + j] for j in range(group)]
        for j, plane in enumerate(rows_inverse(planes, inv_y_ref[...])):
            y_ref[it * group + j, 0:E, :] = plane
        return carry

    lax.fori_loop(0, HALF // group, y_body, 0)

    def z_body(it, carry):
        block = y_ref[pl.ds(it * group, group), 0:E, :].reshape(group * E, 128)
        out_ref[pl.ds(it * group, group)] = lanes_dft(block, inv_z_ref[...]).reshape(group, E, 128)
        return carry

    lax.fori_loop(0, HALF // group, z_body, 0)


def tap_spectra(flat_ref, taps_ref, z_ref, kr_ref, ki_ref, tap_z_ref, tap_y_ref):
    lane = lax.broadcasted_iota(jnp.int32, (1, 128), 1)
    for r in range(KS * KS):
        i, at = KS * r // 128, KS * r % 128
        run = pltpu.roll(flat_ref[i : i + 1, :], (-at) % 128, 1)
        if at + KS > 128:
            more = pltpu.roll(flat_ref[i + 1 : i + 2, :], (-at) % 128, 1)
            run = jnp.where(lane < 128 - at, run, more)
        taps_ref[r // KS, r % KS : r % KS + 1, :] = run
    low = low_lanes((PAD // 2, 128))
    rows = lanes_dft(taps_ref[...].reshape(KS * TAPROWS, 128), tap_z_ref[...])
    z_ref[0:KS, 0:TAPROWS, :] = rows.reshape(KS, TAPROWS, 128)
    planes = [z_ref[d, 0:TAPROWS, :] for d in range(KS)]
    for d, specs in enumerate(rows_forward(planes, tap_y_ref[...])):
        for h, spec in enumerate(specs):
            other = pltpu.roll(spec, 64, 1)
            kr_ref[d, h * 32 : h * 32 + 32, :] = jnp.where(low, spec, other)
            ki_ref[d, h * 32 : h * 32 + 32, :] = jnp.where(low, other, spec)


def assemble(next_ref, cp_ref, halos, place_ref, ext_ref, pp_ref):
    hxm_ref, hxp_ref, hym_ref, hyp_ref, hzm_ref, hzp_ref = halos
    low_core = low_lanes((E, 128))
    low_row = low_lanes((8, 128))

    def face(ref, f):
        return jnp.where(next_ref[0, f] >= 0, ref[...].astype(F32), 0.0)

    ext_ref[:, 0:8, :] = face(hym_ref, 2).reshape(HALF, 8, 128)
    ext_ref[:, 56:64, :] = face(hyp_ref, 3).reshape(HALF, 8, 128)
    zm_all = face(hzm_ref, 4).astype(BF16)
    zp_all = face(hzp_ref, 5).astype(BF16)
    for g in range(3):
        zm = dot(zm_all[g * E : (g + 1) * E], place_ref[0])
        zp = dot(zp_all[g * E : (g + 1) * E], place_ref[1])
        for p in range(8):
            lanes = slice(p * 128, (p + 1) * 128)
            ext_ref[g * 8 + p, 8:56, :] = cp_ref[g * 8 + p] + zm[:, lanes] + zp[:, lanes]
    xm = face(hxm_ref, 0).reshape(4, E, 128)
    xp = face(hxp_ref, 1).reshape(4, E, 128)
    pp_ref[8:32] = ext_ref[...]
    for j in range(8):
        for rows in (slice(0, 8), slice(56, 64)):
            near = ext_ref[16 + j, rows, :]
            pp_ref[j, rows, :] = pltpu.roll(jnp.where(low_row, near, 0.0), 64, 1)
            near = ext_ref[j, rows, :]
            pp_ref[32 + j, rows, :] = pltpu.roll(jnp.where(low_row, 0.0, near), 64, 1)
        before = xm[j] if j < 4 else pltpu.roll(xm[j - 4], 64, 1)
        after = pltpu.roll(xp[j], 64, 1) if j < 4 else xp[j - 4]
        pp_ref[j, 8:56, :] = jnp.where(low_core, before, pltpu.roll(ext_ref[16 + j, 8:56, :], 64, 1))
        pp_ref[32 + j, 8:56, :] = jnp.where(low_core, pltpu.roll(ext_ref[j, 8:56, :], 64, 1), after)


def correct(tissue_ref, cp_ref, new_ref, seen_ref, tables, work):
    fwd_z_ref, inv_z_ref, fwd_yc_ref, inv_y_ref = tables
    z_ref, spec_ref, kr_ref, ki_ref, fil_ref, core_ref, q_ref = work
    low_core = low_lanes((E, 128))
    filter_planes(spec_ref, kr_ref, ki_ref, fil_ref, False)
    inverse_planes(fil_ref, z_ref, core_ref, inv_y_ref, inv_z_ref)

    lane = lax.broadcasted_iota(jnp.int32, (E, 128), 1) % 64
    inside = (lane >= MARGIN) & (lane < MARGIN + E)

    def ratio_body(it, carry):
        for o in [it * 4 + j for j in range(4)]:
            q_ref[o + 8] = jnp.where(inside, seen_ref[o] / jnp.where(inside, core_ref[o], 1.0), 0.0)
        return carry

    lax.fori_loop(0, HALF // 4, ratio_body, 0)
    for j in range(8):
        q_ref[j] = pltpu.roll(jnp.where(low_core, q_ref[24 + j], 0.0), 64, 1)
        q_ref[32 + j] = pltpu.roll(jnp.where(low_core, 0.0, q_ref[8 + j]), 64, 1)

    forward_planes(q_ref, z_ref, spec_ref, E, fwd_z_ref, fwd_yc_ref)
    filter_planes(spec_ref, kr_ref, ki_ref, fil_ref, True)
    inverse_planes(fil_ref, z_ref, core_ref, inv_y_ref, inv_z_ref)

    alive = tissue_ref[0] > 0

    def finish(it, carry):
        for o in [it * 4 + j for j in range(4)]:
            old = cp_ref[o]
            new_ref[o] = jnp.where(jnp.logical_and(inside, alive), old * core_ref[o], old)
        return carry

    lax.fori_loop(0, HALF // 4, finish, 0)


VMEM = pl.BlockSpec(memory_space=pltpu.VMEM)
SMEM = pl.BlockSpec(memory_space=pltpu.SMEM)


def fwd_y_core():
    full = TABLES["fwd_y"]
    return np.concatenate([full[:, s * PAD + MARGIN : s * PAD + MARGIN + E] for s in range(3)], axis=1)


GRID = (4, 4, 8)


def coords_of(b):
    return (
        b % 2 + 2 * ((b // 8) % 2),
        (b // 2) % 2 + 2 * ((b // 16) % 2),
        (b // 64) % 2 + 2 * ((b // 4) % 2) + 4 * ((b // 32) % 2),
    )


def block_at(c):
    return (
        c[0] % 2 + 2 * (c[1] % 2) + 4 * ((c[2] // 2) % 2) + 8 * (c[0] // 2) + 16 * (c[1] // 2)
        + 32 * (c[2] // 4) + 64 * (c[2] % 2)
    )


def neighbour_of(b, axis, step):
    c = list(coords_of(b))
    c[axis] = (c[axis] + step + GRID[axis]) % GRID[axis]
    return block_at(c)


MESH = pl.DeviceIdType.MESH
NEAR = 8
FAR = 16


def near_peers(me):
    base = me // NEAR * NEAR
    return [base + (me % NEAR + s) % NEAR for s in range(1, NEAR)]


def far_peers(me):
    return [(me // NEAR + s) % FAR * NEAR + me % NEAR for s in range(1, FAR)]


def face_peers(me):
    return [neighbour_of(me, f // 2, -1 if f % 2 == 0 else 1) for f in range(6)]


def face_copies(faces, halos, peers, send, recv):
    return [
        pltpu.make_async_remote_copy(
            src_ref=faces[f],
            dst_ref=halos[f ^ 1],
            send_sem=send.at[f],
            recv_sem=recv.at[f],
            device_id=(peers[f],),
            device_id_type=MESH,
        )
        for f in range(6)
    ]


def remote(src, dst, send, recv, peer):
    return pltpu.make_async_remote_copy(
        src_ref=src, dst_ref=dst, send_sem=send, recv_sem=recv, device_id=(peer,), device_id_type=MESH
    )


def blend_cells(u, cells_ref, weights_ref, pick, scaled_ref, parts_ref):
    for a in range(NEAR):
        cell = cells_ref[a]
        total = jnp.sum(jnp.sum(cell, axis=0, keepdims=True), axis=1, keepdims=True)
        scaled_ref[a] = cell / total

    def body(it, carry):
        for dest in [it * 8 + j for j in range(8)]:
            share = jnp.sum(weights_ref[dest, u : u + 1, :] * pick, axis=1, keepdims=True)
            total = share[0:1, :] * scaled_ref[0]
            for a in range(1, NEAR):
                total = total + share[a : a + 1, :] * scaled_ref[a]
            parts_ref[dest] = total
        return carry

    lax.fori_loop(0, FAR // 8, body, 0)


def whole_kernel(*refs):
    order_ref, list_ref, blend_ref, tissue_ref, next_ref = refs[:5]
    inputs = refs[5 : 5 + INPUTS]
    out_ref = refs[5 + INPUTS]
    local_refs = refs[6 + INPUTS : 6 + 2 * INPUTS]
    load_sem = refs[6 + 2 * INPUTS]
    refs = refs[7 + 2 * INPUTS :]
    loads = [pltpu.make_async_copy(inputs[i], local_refs[i], load_sem.at[i]) for i in range(INPUTS)]
    cells_ref, est_ref, pack_ref, cell_row_ref, seen_in, place_ref = local_refs[:6]
    fwd_z_ref, fwd_y_ref, tap_z_ref, tap_y_ref, inv_y_ref, inv_z_ref, fwd_yc_ref = local_refs[6:]
    for load in loads:
        load.start()
    cp_refs, own_ref, weights_ref = refs[:2], refs[2], refs[3]
    faces = (refs[4:10], refs[10:16])
    halos = (refs[16:22], refs[22:28])
    near_all, weights_all, parts, held = refs[28:30], refs[30], refs[31:33], refs[33:35]
    scaled_ref, kernel_ref, taps_ref, ext_ref, pp_ref, z_ref, spec_ref = refs[35:42]
    kr_ref, ki_ref, fil_ref, core_ref, q_ref, wide_ref, flat_ref = refs[42:49]
    own_sem, near_send, near_recv, share_send, share_recv = refs[49:54]
    far_send, far_recv, face_send, face_recv = refs[54:58]
    row_ref = flat_ref.reshape(HALF * E, 128)
    tables = (fwd_z_ref, inv_z_ref, fwd_yc_ref, inv_y_ref)
    work = (z_ref, spec_ref, kr_ref, ki_ref, fil_ref, core_ref, q_ref)

    me = lax.axis_index("blk")
    near, far, across = near_peers(me), far_peers(me), face_peers(me)
    barrier = pltpu.get_barrier_semaphore()
    for peer in near + far + across:
        pl.semaphore_signal(barrier, inc=1, device_id=(peer,), device_id_type=MESH)

    loads[0].wait()
    prepare_cells(order_ref, list_ref, blend_ref, cells_ref, weights_ref, own_ref)
    taps_ref[...] = jnp.zeros_like(taps_ref)
    pl.semaphore_wait(barrier, len(near + far + across))

    near_copies = [
        [
            remote(own_ref.at[u], near_all[u].at[me % NEAR], near_send.at[u, s], near_recv.at[u, s], peer)
            for s, peer in enumerate(near)
        ]
        + [pltpu.make_async_copy(own_ref.at[u], near_all[u].at[me % NEAR], own_sem.at[u])]
        for u in range(UPDATES)
    ]
    share_copies = [
        remote(weights_ref, weights_all.at[me // NEAR], share_send.at[s], share_recv.at[s], peer)
        for s, peer in enumerate(far)
    ] + [pltpu.make_async_copy(weights_ref, weights_all.at[me // NEAR], own_sem.at[2])]
    face_copies = [
        [
            remote(faces[u][f], halos[u][f ^ 1], face_send.at[u, f], face_recv.at[u, f], across[f])
            for f in range(6)
        ]
        for u in range(UPDATES)
    ]
    far_copies = [
        [
            remote(parts[u].at[(me // NEAR + 1 + s) % FAR], held[u].at[s], far_send.at[u, s], far_recv.at[u, s], peer)
            for s, peer in enumerate(far)
        ]
        for u in range(UPDATES)
    ]

    def start(copies):
        for copy in copies:
            copy.start()

    def wait(copies):
        for copy in copies:
            copy.wait()

    base = me // NEAR * NEAR

    def widen(it, carry):
        for j in range(8):
            at = pl.multiple_of(it * 1024 + j * 128, 128)
            wide_ref[pl.ds(pl.multiple_of(it * 64 + j * 8, 8), 6), :] = seen_in[:, pl.ds(at, 128)].astype(F32)
        return carry

    def seen_pairs(u):
        view = order_ref[u]

        def load(k, half):
            return wide_ref[pl.ds((half * 3 * GROUPS + k) * 8 + view, GROUPS, stride=24), :]

        flat_to_pairs(load, store_rows(row_ref))

    def spectra(u):
        total = parts[u][me // NEAR]
        for s in range(FAR - 1):
            total = total + held[u][s]
        kernel_ref[...] = total
        tap_spectra(kernel_ref, taps_ref, z_ref, kr_ref, ki_ref, tap_z_ref, tap_y_ref)

    def padded_spectra(u):
        wait(face_copies[u])
        assemble(next_ref, cp_refs[u], halos[u], place_ref, ext_ref, pp_ref)
        forward_planes(pp_ref, z_ref, spec_ref, PAD, fwd_z_ref, fwd_y_ref)

    start(near_copies[0])
    start(share_copies)
    for load in loads[1:3]:
        load.wait()
    prepare_block(est_ref, pack_ref, cp_refs[0], faces[0])
    start(face_copies[0])
    for load in loads[3:]:
        load.wait()
    pick = (cell_row_ref[...] == base + lax.broadcasted_iota(jnp.int32, (NEAR, 128), 0)).astype(F32)
    lax.fori_loop(0, FLAT // 8, widen, 0)
    wait(near_copies[0])
    wait(share_copies)
    blend_cells(0, near_all[0], weights_all, pick, scaled_ref, parts[0])
    start(far_copies[0])
    start(near_copies[1])
    seen_pairs(0)
    padded_spectra(0)
    wait(near_copies[1])
    blend_cells(1, near_all[1], weights_all, pick, scaled_ref, parts[1])
    wait(far_copies[0])
    start(far_copies[1])
    spectra(0)
    correct(tissue_ref, cp_refs[0], cp_refs[1], flat_ref, tables, work)
    emit_faces(cp_refs[1], pack_ref, faces[1])
    start(face_copies[1])
    wait(far_copies[1])
    spectra(1)
    seen_pairs(1)
    padded_spectra(1)
    correct(tissue_ref, cp_refs[1], flat_ref, flat_ref, tables, work)

    def load_new(j):
        return row_ref[pl.ds(j, GROUPS, stride=8), :]

    def store_new(k, half, rows):
        out_ref[pl.ds(half * 3 * GROUPS + k, GROUPS, stride=3), :] = rows

    pairs_to_flat(load_new, store_new)


HALO_SHAPES = [FACE_SHAPES[f ^ 1] for f in range(6)]
DMA = pltpu.SemaphoreType.DMA
INPUTS = 13


def whole_call(scalars, est, cells, cell_row, seen):
    inputs = [
        cells,
        est,
        jnp.asarray(TABLES["pack"]),
        cell_row,
        seen,
        jnp.asarray(TABLES["place"]),
        jnp.asarray(TABLES["fwd_z"]),
        jnp.asarray(TABLES["fwd_y"]),
        jnp.asarray(TABLES["tap_z"]),
        jnp.asarray(TABLES["tap_y"]),
        jnp.asarray(TABLES["inv_y"]),
        jnp.asarray(TABLES["inv_z"]),
        jnp.asarray(fwd_y_core()),
    ]
    f32 = [
        (NEAR, CELLROWS, 128),
        (NEAR, CELLROWS, 128),
        (FAR, 8, 128),
        (FAR, CELLROWS, 128),
        (FAR, CELLROWS, 128),
        (FAR - 1, CELLROWS, 128),
        (FAR - 1, CELLROWS, 128),
        (NEAR, CELLROWS, 128),
        (CELLROWS, 128),
        (KS, TAPROWS, 128),
        (HALF, PAD, 128),
        (PLANES, PAD, 128),
        (PLANES, PAD, 128),
        (PLANES, PAD, 128),
        (KS, PAD, 128),
        (KS, PAD, 128),
        (HALF, PAD, 128),
        (HALF, E, 128),
        (PLANES, E, 128),
        (FLAT * 8, 128),
        (HALF, E, 128),
    ]
    scratch = [pltpu.VMEM(x.shape, x.dtype) for x in inputs] + [DMA((INPUTS,))]
    scratch += [pltpu.VMEM(s, F32) for s in [(HALF, E, 128)] * 2 + [(UPDATES, CELLROWS, 128), (8, 128)]]
    scratch += [pltpu.VMEM(s, BF16) for s in FACE_SHAPES * 2 + HALO_SHAPES * 2]
    scratch += [pltpu.VMEM(s, F32) for s in f32]
    scratch += [DMA((3,)), DMA((2, NEAR - 1)), DMA((2, NEAR - 1)), DMA((FAR - 1,)), DMA((FAR - 1,))]
    scratch += [DMA((2, FAR - 1)), DMA((2, FAR - 1)), DMA((2, 6)), DMA((2, 6))]
    return pl.pallas_call(
        whole_kernel,
        out_shape=jax.ShapeDtypeStruct((FLAT, 128), F32),
        in_specs=[SMEM] * 5 + [pl.BlockSpec(memory_space=pl.ANY)] * INPUTS,
        out_specs=VMEM,
        scratch_shapes=scratch,
        compiler_params=pltpu.CompilerParams(collective_id=0, has_side_effects=True),
        name="whole",
    )(*scalars, *inputs)


def local(
    estimate, observed, psf_cells, tissue, neighbours, psf_list, psf_blend, cell_row, view_order
):
    scalars = (
        view_order,
        psf_list.transpose(0, 2, 1).reshape(2, 6),
        psf_blend.transpose(0, 2, 1).reshape(2, 6),
        tissue,
        neighbours,
    )
    result = whole_call(
        scalars,
        estimate.reshape(FLAT, 128),
        psf_cells.reshape(6, 1, KS3),
        cell_row.reshape(1, 128),
        observed.reshape(6, E3),
    )
    return result.reshape(1, E3)


def solution(mesh):
    return jax.shard_map(
        local,
        mesh=mesh,
        in_specs=(
            P("blk", None),
            P("blk", None, None),
            P("blk", None, None),
            P("blk"),
            P("blk", None),
            P("blk", None, None),
            P("blk", None, None),
            P(),
            P(),
        ),
        out_specs=P("blk", None),
        check_vma=False,
    )
```

```python
import functools
import math

import jax
import jax.numpy as jnp
import numpy as np
from jax import lax
from jax.experimental import pallas as pl
from jax.experimental.pallas import tpu as pltpu
from jax.sharding import PartitionSpec as P

E = 48
MARGIN = 8
UPDATES = 2
PAD = 64
KS = 17
E3 = 110592
KS3 = 4913
HALF = 24
PLANES = 40
TAPROWS = 32

CELLROWS = 40
ROWS = UPDATES * CELLROWS

F32 = jnp.float32
BF16 = jnp.bfloat16


def split_np(table):
    hi = np.asarray(table, np.float32).astype(jnp.bfloat16)
    lo = (np.asarray(table, np.float64) - hi.astype(np.float64)).astype(np.float32).astype(jnp.bfloat16)
    return hi, lo


def lane_table(table):
    hi, lo = split_np(table)
    row = np.concatenate([hi, lo], axis=1)
    return np.concatenate([row, row], axis=0)


def row_table(table):
    hi, lo = split_np(table)
    return np.concatenate([hi, hi, lo], axis=1)


def make_tables():
    step = 2.0 * math.pi / PAD
    k = np.arange(PAD)
    ang = (k[:, None] * k[None, :] % PAD) * step
    cos, sin = np.cos(ang), np.sin(ang)
    fwd_z = np.block([[cos, -sin], [sin, cos]])
    inv_z = np.block([[cos, sin], [-sin, cos]]) / PAD
    half = (np.arange(PAD // 2)[:, None] + 0.5) * step
    fwd_y = np.concatenate([np.cos(half * k), np.sin(half * k)], axis=0)
    core = k[MARGIN : MARGIN + E]
    inv_y = np.concatenate([np.cos(half * core), np.sin(half * core)], axis=0).T / PAD
    t = np.arange(KS) - MARGIN
    ang_t = (t[:, None] * k[None, :]) % PAD * step
    tap_z = np.zeros((128, 128))
    tap_z[:KS, :PAD] = np.cos(ang_t)
    tap_z[:KS, PAD:] = -np.sin(ang_t)
    tap_y = np.zeros((PAD, TAPROWS))
    tap_y[:, :KS] = np.concatenate([np.cos(half * t), np.sin(half * t)], axis=0)
    pack = np.zeros((8 * 128, 256), np.float32)
    place = np.zeros((256, 8 * 128), np.float32)
    for p in range(8):
        for s in range(2):
            for z in range(MARGIN):
                slot = p * 16 + s * 8 + z
                pack[p * 128 + s * 64 + MARGIN + z, slot] = 1
                pack[p * 128 + s * 64 + E + z, 128 + slot] = 1
                place[slot, p * 128 + s * 64 + z] = 1
                place[128 + slot, p * 128 + s * 64 + MARGIN + E + z] = 1
    return dict(
        fwd_z=lane_table(fwd_z),
        inv_z=lane_table(inv_z),
        tap_z=lane_table(tap_z),
        fwd_y=row_table(fwd_y),
        inv_y=row_table(inv_y),
        tap_y=row_table(tap_y),
        pack=pack.astype(jnp.bfloat16),
        place=place.astype(jnp.bfloat16),
    )


TABLES = make_tables()


def split(values):
    hi = values.astype(BF16)
    lo = (values - hi.astype(F32)).astype(BF16)
    return hi, lo


def low_lanes(shape):
    return lax.broadcasted_iota(jnp.int32, shape, len(shape) - 1) < 64


def lane_sign(shape):
    return jnp.where(low_lanes(shape), 1.0, -1.0).astype(F32)


def dot(a, b):
    return lax.dot_general(a, b, (((1,), (0,)), ((), ())), preferred_element_type=F32)


def lanes_dft(rows, table):
    hi, lo = split(rows)
    both = dot(jnp.concatenate([hi, lo], axis=1), table)
    return both[:, :128] + both[:, 128:]


def rows_dot(planes, table):
    out = []
    for a in range(0, len(planes), 2):
        cols = []
        for plane in planes[a : a + 2]:
            hi, lo = split(plane)
            cols.append(jnp.concatenate([hi, lo, hi], axis=0))
        both = dot(table, jnp.concatenate(cols, axis=1) if len(cols) > 1 else cols[0])
        out += [both[:, b * 128 : (b + 1) * 128] for b in range(len(cols))]
    return out


def rows_forward(planes, table):
    sign = lane_sign((PAD // 2, 128))
    out = []
    for both in rows_dot(planes, table):
        turned = sign * pltpu.roll(both[PAD // 2 :], 64, 1)
        out.append((both[: PAD // 2] + turned, both[: PAD // 2] - turned))
    return out


def rows_inverse(planes, table):
    sign = -lane_sign((PAD // 2, 128))
    folded = []
    for plane in planes:
        plus, minus = plane[: PAD // 2], plane[PAD // 2 :]
        folded.append(jnp.concatenate([plus + minus, sign * pltpu.roll(plus - minus, 64, 1)], axis=0))
    return rows_dot(folded, table)


def emit_faces(cp_ref, pack_ref, faces):
    xm_ref, xp_ref, ym_ref, yp_ref, zm_ref, zp_ref = faces
    wide = [
        jnp.concatenate([cp_ref[g * 8 + p].astype(BF16) for p in range(8)], axis=1) for g in range(3)
    ]
    both = dot(jnp.concatenate(wide, axis=0), pack_ref[...])
    zm_ref[...] = both[:, :128].astype(BF16)
    zp_ref[...] = both[:, 128:].astype(BF16)
    low = low_lanes((E, 128))
    for j in range(4):
        near = jnp.where(low, cp_ref[j], pltpu.roll(cp_ref[4 + j], 64, 1))
        xm_ref[j * E : (j + 1) * E, :] = near.astype(BF16)
        near = jnp.where(low, pltpu.roll(cp_ref[16 + j], 64, 1), cp_ref[20 + j])
        xp_ref[j * E : (j + 1) * E, :] = near.astype(BF16)
    ym_ref[...] = cp_ref[:, 0:8, :].reshape(HALF * 8, 128).astype(BF16)
    yp_ref[...] = cp_ref[:, E - 8 : E, :].reshape(HALF * 8, 128).astype(BF16)

FACE_SHAPES = [(4 * E, 128), (4 * E, 128), (HALF * 8, 128), (HALF * 8, 128), (3 * E, 128), (3 * E, 128)]


def flat_to_pairs(load, store):
    for j in range(8):
        total = None
        for half in range(2):
            first = 48 * j
            k, lane = first // 128, first % 128
            base = MARGIN + 64 * half
            value = load(k, half)
            part = value if lane == base else pltpu.roll(value, (base - lane) % 128, 1)
            at = lax.broadcasted_iota(jnp.int32, part.shape, 1) - base
            length = min(48, 128 - lane)
            picked = jnp.where((at >= 0) & (at < length), part, 0.0)
            if length < 48:
                more = pltpu.roll(load(k + 1, half), base + length, 1)
                picked = jnp.where((at >= length) & (at < 48), more, picked)
            total = picked if total is None else total + picked
        store(j, total)


def pairs_to_flat(load, store):
    for half in range(2):
        for k in range(3):
            total = None
            for j in range(8):
                lane = 48 * j - 128 * k
                if lane <= -48 or lane >= 128:
                    continue
                value = pltpu.roll(load(j), (lane - MARGIN - 64 * half) % 128, 1)
                at = lax.broadcasted_iota(jnp.int32, value.shape, 1) - lane
                picked = jnp.where((at >= 0) & (at < 48), value, 0.0)
                total = picked if total is None else total + picked
            store(k, half, total)


GROUPS = HALF * E // 8
FLAT = E3 // 128


def load_flat(ref):
    return lambda k, half: ref[pl.ds(half * 3 * GROUPS + k, GROUPS, stride=3), :]


def store_rows(ref):
    def store(j, rows):
        ref[pl.ds(j, GROUPS, stride=8), :] = rows

    return store


def prepare_cells(order_ref, list_ref, blend_ref, cells_ref, weights_ref, own_ref):
    number = lax.broadcasted_iota(jnp.int32, (1, 128), 1)
    weights_ref[...] = jnp.zeros_like(weights_ref)
    own_ref[...] = jnp.zeros_like(own_ref)
    for u in range(UPDATES):
        view = order_ref[u]
        first = jnp.full((1, 128), blend_ref[0, view], F32)
        second = jnp.full((1, 128), blend_ref[1, view], F32)
        total = first + second
        weights_ref[u : u + 1, :] = jnp.where(number == list_ref[0, view], first / total, 0.0) + jnp.where(
            number == list_ref[1, view], second / total, 0.0
        )
        for i in range(KS3 // 128):
            own_ref[u, i : i + 1, :] = cells_ref[view, :, i * 128 : (i + 1) * 128]
        tail = KS3 // 128 * 128
        i = KS3 // 128
        own_ref[u, i : i + 1, 0 : KS3 - tail] = cells_ref[view, :, tail:KS3]


def prepare_block(est_ref, pack_ref, cp_ref, faces):
    row_ref = cp_ref.reshape(HALF * E, 128)
    flat_to_pairs(load_flat(est_ref), store_rows(row_ref))
    emit_faces(cp_ref, pack_ref, faces)


def forward_planes(src_ref, z_ref, spec_ref, rows, fwd_z_ref, fwd_y_ref):
    group = PLANES

    def z_body(it, carry):
        block = src_ref[pl.ds(it * group, group)].reshape(group * rows, 128)
        z_ref[pl.ds(it * group, group), 0:rows, :] = lanes_dft(block, fwd_z_ref[...]).reshape(group, rows, 128)
        return carry

    lax.fori_loop(0, PLANES // group, z_body, 0)

    def y_body(it, carry):
        planes = [z_ref[it * group + j, 0:rows, :] for j in range(group)]
        for j, (plus, minus) in enumerate(rows_forward(planes, fwd_y_ref[...])):
            spec_ref[it * group + j, 0 : PAD // 2, :] = plus
            spec_ref[it * group + j, PAD // 2 : PAD, :] = minus
        return carry

    lax.fori_loop(0, PLANES // group, y_body, 0)


def filter_planes(spec_ref, kr_ref, ki_ref, out_ref, conjugate):
    group = 12
    sign = lane_sign((8, 128))
    if not conjugate:
        sign = -sign

    def body(kb, carry):
        rows = pl.ds(pl.multiple_of(kb * 8, 8), 8)
        for first in range(0, HALF, group):
            values = {}
            acc_r, acc_i = [None] * group, [None] * group
            for d in range(KS):
                tap = d if conjugate else KS - 1 - d
                kr = kr_ref[tap, rows, :]
                ki = ki_ref[tap, rows, :]
                for j in range(group):
                    m = first + j + d
                    if m not in values:
                        values[m] = spec_ref[m, rows, :]
                    if d == 0:
                        acc_r[j] = kr * values[m]
                        acc_i[j] = ki * values[m]
                    else:
                        acc_r[j] = acc_r[j] + kr * values[m]
                        acc_i[j] = acc_i[j] + ki * values[m]
            for j in range(group):
                out_ref[first + j, rows, :] = acc_r[j] + sign * pltpu.roll(acc_i[j], 64, 1)
        return carry

    lax.fori_loop(0, PAD // 8, body, 0)


def inverse_planes(spec_ref, y_ref, out_ref, inv_y_ref, inv_z_ref):
    group = 12

    def y_body(it, carry):
        planes = [spec_ref[it * group + j] for j in range(group)]
        for j, plane in enumerate(rows_inverse(planes, inv_y_ref[...])):
            y_ref[it * group + j, 0:E, :] = plane
        return carry

    lax.fori_loop(0, HALF // group, y_body, 0)

    def z_body(it, carry):
        block = y_ref[pl.ds(it * group, group), 0:E, :].reshape(group * E, 128)
        out_ref[pl.ds(it * group, group)] = lanes_dft(block, inv_z_ref[...]).reshape(group, E, 128)
        return carry

    lax.fori_loop(0, HALF // group, z_body, 0)


def tap_spectra(flat_ref, taps_ref, z_ref, kr_ref, ki_ref, tap_z_ref, tap_y_ref):
    lane = lax.broadcasted_iota(jnp.int32, (1, 128), 1)
    for r in range(KS * KS):
        i, at = KS * r // 128, KS * r % 128
        run = pltpu.roll(flat_ref[i : i + 1, :], (-at) % 128, 1)
        if at + KS > 128:
            more = pltpu.roll(flat_ref[i + 1 : i + 2, :], (-at) % 128, 1)
            run = jnp.where(lane < 128 - at, run, more)
        taps_ref[r // KS, r % KS : r % KS + 1, :] = run
    low = low_lanes((PAD // 2, 128))
    rows = lanes_dft(taps_ref[...].reshape(KS * TAPROWS, 128), tap_z_ref[...])
    z_ref[0:KS, 0:TAPROWS, :] = rows.reshape(KS, TAPROWS, 128)
    planes = [z_ref[d, 0:TAPROWS, :] for d in range(KS)]
    for d, specs in enumerate(rows_forward(planes, tap_y_ref[...])):
        for h, spec in enumerate(specs):
            other = pltpu.roll(spec, 64, 1)
            kr_ref[d, h * 32 : h * 32 + 32, :] = jnp.where(low, spec, other)
            ki_ref[d, h * 32 : h * 32 + 32, :] = jnp.where(low, other, spec)


def assemble(next_ref, cp_ref, halos, place_ref, ext_ref, pp_ref):
    hxm_ref, hxp_ref, hym_ref, hyp_ref, hzm_ref, hzp_ref = halos
    low_core = low_lanes((E, 128))
    low_row = low_lanes((8, 128))

    def face(ref, f):
        return jnp.where(next_ref[0, f] >= 0, ref[...].astype(F32), 0.0)

    ext_ref[:, 0:8, :] = face(hym_ref, 2).reshape(HALF, 8, 128)
    ext_ref[:, 56:64, :] = face(hyp_ref, 3).reshape(HALF, 8, 128)
    both = jnp.concatenate([face(hzm_ref, 4).astype(BF16), face(hzp_ref, 5).astype(BF16)], axis=1)
    margins = dot(both, place_ref[...])
    for g in range(3):
        for p in range(8):
            ext_ref[g * 8 + p, 8:56, :] = cp_ref[g * 8 + p] + margins[g * E : (g + 1) * E, p * 128 : (p + 1) * 128]
    xm = face(hxm_ref, 0).reshape(4, E, 128)
    xp = face(hxp_ref, 1).reshape(4, E, 128)
    pp_ref[8:32] = ext_ref[...]
    for j in range(8):
        for rows in (slice(0, 8), slice(56, 64)):
            near = ext_ref[16 + j, rows, :]
            pp_ref[j, rows, :] = pltpu.roll(jnp.where(low_row, near, 0.0), 64, 1)
            near = ext_ref[j, rows, :]
            pp_ref[32 + j, rows, :] = pltpu.roll(jnp.where(low_row, 0.0, near), 64, 1)
        before = xm[j] if j < 4 else pltpu.roll(xm[j - 4], 64, 1)
        after = pltpu.roll(xp[j], 64, 1) if j < 4 else xp[j - 4]
        pp_ref[j, 8:56, :] = jnp.where(low_core, before, pltpu.roll(ext_ref[16 + j, 8:56, :], 64, 1))
        pp_ref[32 + j, 8:56, :] = jnp.where(low_core, pltpu.roll(ext_ref[j, 8:56, :], 64, 1), after)


def correct(tissue_ref, cp_ref, new_ref, seen_ref, tables, work):
    fwd_z_ref, inv_z_ref, fwd_yc_ref, inv_y_ref = tables
    z_ref, spec_ref, kr_ref, ki_ref, fil_ref, core_ref, q_ref = work
    low_core = low_lanes((E, 128))
    filter_planes(spec_ref, kr_ref, ki_ref, fil_ref, False)
    inverse_planes(fil_ref, z_ref, core_ref, inv_y_ref, inv_z_ref)

    lane = lax.broadcasted_iota(jnp.int32, (E, 128), 1) % 64
    inside = (lane >= MARGIN) & (lane < MARGIN + E)

    def ratio_body(it, carry):
        for o in [it * 4 + j for j in range(4)]:
            q_ref[o + 8] = jnp.where(inside, seen_ref[o] / jnp.where(inside, core_ref[o], 1.0), 0.0)
        return carry

    lax.fori_loop(0, HALF // 4, ratio_body, 0)
    for j in range(8):
        q_ref[j] = pltpu.roll(jnp.where(low_core, q_ref[24 + j], 0.0), 64, 1)
        q_ref[32 + j] = pltpu.roll(jnp.where(low_core, 0.0, q_ref[8 + j]), 64, 1)

    forward_planes(q_ref, z_ref, spec_ref, E, fwd_z_ref, fwd_yc_ref)
    filter_planes(spec_ref, kr_ref, ki_ref, fil_ref, True)
    inverse_planes(fil_ref, z_ref, core_ref, inv_y_ref, inv_z_ref)

    alive = tissue_ref[0] > 0

    def finish(it, carry):
        for o in [it * 4 + j for j in range(4)]:
            old = cp_ref[o]
            new_ref[o] = jnp.where(jnp.logical_and(inside, alive), old * core_ref[o], old)
        return carry

    lax.fori_loop(0, HALF // 4, finish, 0)


VMEM = pl.BlockSpec(memory_space=pltpu.VMEM)
SMEM = pl.BlockSpec(memory_space=pltpu.SMEM)


def fwd_y_core():
    full = TABLES["fwd_y"]
    return np.concatenate([full[:, s * PAD + MARGIN : s * PAD + MARGIN + E] for s in range(3)], axis=1)


GRID = (4, 4, 8)


def coords_of(b):
    return (
        b % 2 + 2 * ((b // 8) % 2),
        (b // 2) % 2 + 2 * ((b // 16) % 2),
        (b // 64) % 2 + 2 * ((b // 4) % 2) + 4 * ((b // 32) % 2),
    )


def block_at(c):
    return (
        c[0] % 2 + 2 * (c[1] % 2) + 4 * ((c[2] // 2) % 2) + 8 * (c[0] // 2) + 16 * (c[1] // 2)
        + 32 * (c[2] // 4) + 64 * (c[2] % 2)
    )


def neighbour_of(b, axis, step):
    c = list(coords_of(b))
    c[axis] = (c[axis] + step + GRID[axis]) % GRID[axis]
    return block_at(c)


MESH = pl.DeviceIdType.MESH
NEAR = 8
FAR = 16


def near_peers(me):
    base = me // NEAR * NEAR
    return [base + (me % NEAR + s) % NEAR for s in range(1, NEAR)]


def far_peers(me):
    return [(me // NEAR + s) % FAR * NEAR + me % NEAR for s in range(1, FAR)]


def face_peers(me):
    return [neighbour_of(me, f // 2, -1 if f % 2 == 0 else 1) for f in range(6)]


def face_copies(faces, halos, peers, send, recv):
    return [
        pltpu.make_async_remote_copy(
            src_ref=faces[f],
            dst_ref=halos[f ^ 1],
            send_sem=send.at[f],
            recv_sem=recv.at[f],
            device_id=(peers[f],),
            device_id_type=MESH,
        )
        for f in range(6)
    ]


def remote(src, dst, send, recv, peer):
    return pltpu.make_async_remote_copy(
        src_ref=src, dst_ref=dst, send_sem=send, recv_sem=recv, device_id=(peer,), device_id_type=MESH
    )


def blend_cells(u, cells_ref, weights_ref, pick, scaled_ref, parts_ref):
    for a in range(NEAR):
        cell = cells_ref[a]
        total = jnp.sum(jnp.sum(cell, axis=0, keepdims=True), axis=1, keepdims=True)
        scaled_ref[a] = cell / total

    def body(it, carry):
        for dest in [it * 8 + j for j in range(8)]:
            share = jnp.sum(weights_ref[dest, u : u + 1, :] * pick, axis=1, keepdims=True)
            total = share[0:1, :] * scaled_ref[0]
            for a in range(1, NEAR):
                total = total + share[a : a + 1, :] * scaled_ref[a]
            parts_ref[dest] = total
        return carry

    lax.fori_loop(0, FAR // 8, body, 0)


def whole_kernel(*refs):
    order_ref, list_ref, blend_ref, tissue_ref, next_ref = refs[:5]
    inputs = refs[5 : 5 + INPUTS]
    out_ref = refs[5 + INPUTS]
    local_refs = refs[6 + INPUTS : 6 + 2 * INPUTS]
    load_sem = refs[6 + 2 * INPUTS]
    refs = refs[7 + 2 * INPUTS :]
    loads = [pltpu.make_async_copy(inputs[i], local_refs[i], load_sem.at[i]) for i in range(INPUTS)]
    cells_ref, est_ref, pack_ref, cell_row_ref, seen_in, place_ref = local_refs[:6]
    fwd_z_ref, fwd_y_ref, tap_z_ref, tap_y_ref, inv_y_ref, inv_z_ref, fwd_yc_ref = local_refs[6:]
    for load in loads:
        load.start()
    cp_refs, own_ref, weights_ref = refs[:2], refs[2], refs[3]
    faces = (refs[4:10], refs[10:16])
    halos = (refs[16:22], refs[22:28])
    near_all, weights_all, parts, held = refs[28:30], refs[30], refs[31:33], refs[33:35]
    scaled_ref, kernel_ref, taps_ref, ext_ref, pp_ref, z_ref, spec_ref = refs[35:42]
    kr_ref, ki_ref, fil_ref, core_ref, q_ref, wide_ref, flat_ref = refs[42:49]
    own_sem, near_send, near_recv, share_send, share_recv = refs[49:54]
    far_send, far_recv, face_send, face_recv = refs[54:58]
    row_ref = flat_ref.reshape(HALF * E, 128)
    tables = (fwd_z_ref, inv_z_ref, fwd_yc_ref, inv_y_ref)
    work = (z_ref, spec_ref, kr_ref, ki_ref, fil_ref, core_ref, q_ref)

    me = lax.axis_index("blk")
    near, far, across = near_peers(me), far_peers(me), face_peers(me)
    barrier = pltpu.get_barrier_semaphore()
    for peer in near + far + across:
        pl.semaphore_signal(barrier, inc=1, device_id=(peer,), device_id_type=MESH)

    loads[0].wait()
    prepare_cells(order_ref, list_ref, blend_ref, cells_ref, weights_ref, own_ref)
    taps_ref[...] = jnp.zeros_like(taps_ref)
    pl.semaphore_wait(barrier, len(near + far + across))

    near_copies = [
        [
            remote(own_ref.at[u], near_all[u].at[me % NEAR], near_send.at[u, s], near_recv.at[u, s], peer)
            for s, peer in enumerate(near)
        ]
        + [pltpu.make_async_copy(own_ref.at[u], near_all[u].at[me % NEAR], own_sem.at[u])]
        for u in range(UPDATES)
    ]
    share_copies = [
        remote(weights_ref, weights_all.at[me // NEAR], share_send.at[s], share_recv.at[s], peer)
        for s, peer in enumerate(far)
    ] + [pltpu.make_async_copy(weights_ref, weights_all.at[me // NEAR], own_sem.at[2])]
    face_copies = [
        [
            remote(faces[u][f], halos[u][f ^ 1], face_send.at[u, f], face_recv.at[u, f], across[f])
            for f in (4, 5, 0, 1, 2, 3)
        ]
        for u in range(UPDATES)
    ]
    far_copies = [
        [
            remote(parts[u].at[(me // NEAR + 1 + s) % FAR], held[u].at[s], far_send.at[u, s], far_recv.at[u, s], peer)
            for s, peer in enumerate(far)
        ]
        for u in range(UPDATES)
    ]

    def start(copies):
        for copy in copies:
            copy.start()

    def wait(copies):
        for copy in copies:
            copy.wait()

    base = me // NEAR * NEAR

    def widen(it, carry):
        for j in range(8):
            at = pl.multiple_of(it * 1024 + j * 128, 128)
            wide_ref[pl.ds(pl.multiple_of(it * 64 + j * 8, 8), 6), :] = seen_in[:, pl.ds(at, 128)].astype(F32)
        return carry

    def seen_pairs(u):
        view = order_ref[u]

        def load(k, half):
            return wide_ref[pl.ds((half * 3 * GROUPS + k) * 8 + view, GROUPS, stride=24), :]

        flat_to_pairs(load, store_rows(row_ref))

    def spectra(u):
        total = parts[u][me // NEAR]
        for s in range(FAR - 1):
            total = total + held[u][s]
        kernel_ref[...] = total
        tap_spectra(kernel_ref, taps_ref, z_ref, kr_ref, ki_ref, tap_z_ref, tap_y_ref)

    def padded_spectra(u):
        wait(face_copies[u])
        assemble(next_ref, cp_refs[u], halos[u], place_ref, ext_ref, pp_ref)
        forward_planes(pp_ref, z_ref, spec_ref, PAD, fwd_z_ref, fwd_y_ref)

    start(near_copies[0])
    start(share_copies)
    for load in loads[1:3]:
        load.wait()
    prepare_block(est_ref, pack_ref, cp_refs[0], faces[0])
    start(face_copies[0])
    for load in loads[3:]:
        load.wait()
    pick = (cell_row_ref[...] == base + lax.broadcasted_iota(jnp.int32, (NEAR, 128), 0)).astype(F32)
    lax.fori_loop(0, FLAT // 8, widen, 0)
    wait(near_copies[0])
    wait(share_copies)
    blend_cells(0, near_all[0], weights_all, pick, scaled_ref, parts[0])
    start(far_copies[0])
    start(near_copies[1])
    seen_pairs(0)
    padded_spectra(0)
    wait(near_copies[1])
    blend_cells(1, near_all[1], weights_all, pick, scaled_ref, parts[1])
    wait(far_copies[0])
    start(far_copies[1])
    spectra(0)
    correct(tissue_ref, cp_refs[0], cp_refs[1], flat_ref, tables, work)
    emit_faces(cp_refs[1], pack_ref, faces[1])
    start(face_copies[1])
    wait(far_copies[1])
    spectra(1)
    seen_pairs(1)
    padded_spectra(1)
    correct(tissue_ref, cp_refs[1], flat_ref, flat_ref, tables, work)

    def load_new(j):
        return row_ref[pl.ds(j, GROUPS, stride=8), :]

    def store_new(k, half, rows):
        out_ref[pl.ds(half * 3 * GROUPS + k, GROUPS, stride=3), :] = rows

    pairs_to_flat(load_new, store_new)


HALO_SHAPES = [FACE_SHAPES[f ^ 1] for f in range(6)]
DMA = pltpu.SemaphoreType.DMA
INPUTS = 13


def whole_call(scalars, est, cells, cell_row, seen):
    inputs = [
        cells,
        est,
        jnp.asarray(TABLES["pack"]),
        cell_row,
        seen,
        jnp.asarray(TABLES["place"]),
        jnp.asarray(TABLES["fwd_z"]),
        jnp.asarray(TABLES["fwd_y"]),
        jnp.asarray(TABLES["tap_z"]),
        jnp.asarray(TABLES["tap_y"]),
        jnp.asarray(TABLES["inv_y"]),
        jnp.asarray(TABLES["inv_z"]),
        jnp.asarray(fwd_y_core()),
    ]
    f32 = [
        (NEAR, CELLROWS, 128),
        (NEAR, CELLROWS, 128),
        (FAR, 8, 128),
        (FAR, CELLROWS, 128),
        (FAR, CELLROWS, 128),
        (FAR - 1, CELLROWS, 128),
        (FAR - 1, CELLROWS, 128),
        (NEAR, CELLROWS, 128),
        (CELLROWS, 128),
        (KS, TAPROWS, 128),
        (HALF, PAD, 128),
        (PLANES, PAD, 128),
        (PLANES, PAD, 128),
        (PLANES, PAD, 128),
        (KS, PAD, 128),
        (KS, PAD, 128),
        (HALF, PAD, 128),
        (HALF, E, 128),
        (PLANES, E, 128),
        (FLAT * 8, 128),
        (HALF, E, 128),
    ]
    scratch = [pltpu.VMEM(x.shape, x.dtype) for x in inputs] + [DMA((INPUTS,))]
    scratch += [pltpu.VMEM(s, F32) for s in [(HALF, E, 128)] * 2 + [(UPDATES, CELLROWS, 128), (8, 128)]]
    scratch += [pltpu.VMEM(s, BF16) for s in FACE_SHAPES * 2 + HALO_SHAPES * 2]
    scratch += [pltpu.VMEM(s, F32) for s in f32]
    scratch += [DMA((3,)), DMA((2, NEAR - 1)), DMA((2, NEAR - 1)), DMA((FAR - 1,)), DMA((FAR - 1,))]
    scratch += [DMA((2, FAR - 1)), DMA((2, FAR - 1)), DMA((2, 6)), DMA((2, 6))]
    return pl.pallas_call(
        whole_kernel,
        out_shape=pltpu.VMEM((FLAT, 128), F32),
        in_specs=[SMEM] * 5 + [pl.BlockSpec(memory_space=pl.ANY)] * INPUTS,
        out_specs=VMEM,
        scratch_shapes=scratch,
        compiler_params=pltpu.CompilerParams(collective_id=0, has_side_effects=True),
        name="whole",
    )(*scalars, *inputs)


def local(
    estimate, observed, psf_cells, tissue, neighbours, psf_list, psf_blend, cell_row, view_order
):
    scalars = (
        view_order,
        psf_list.transpose(0, 2, 1).reshape(2, 6),
        psf_blend.transpose(0, 2, 1).reshape(2, 6),
        tissue,
        neighbours,
    )
    result = whole_call(
        scalars,
        estimate.reshape(FLAT, 128),
        psf_cells.reshape(6, 1, KS3),
        cell_row.reshape(1, 128),
        observed.reshape(6, E3),
    )
    return result.reshape(1, E3)


def solution(mesh):
    return jax.shard_map(
        local,
        mesh=mesh,
        in_specs=(
            P("blk", None),
            P("blk", None, None),
            P("blk", None, None),
            P("blk"),
            P("blk", None),
            P("blk", None, None),
            P("blk", None, None),
            P(),
            P(),
        ),
        out_specs=P("blk", None),
        check_vma=False,
    )
```

```python
import functools
import math

import jax
import jax.numpy as jnp
import numpy as np
from jax import lax
from jax.experimental import pallas as pl
from jax.experimental.pallas import tpu as pltpu
from jax.sharding import PartitionSpec as P

E = 48
MARGIN = 8
UPDATES = 2
PAD = 64
KS = 17
E3 = 110592
KS3 = 4913
HALF = 24
PLANES = 40
TAPROWS = 32

CELLROWS = 40
ROWS = UPDATES * CELLROWS

F32 = jnp.float32
BF16 = jnp.bfloat16


def split_np(table):
    hi = np.asarray(table, np.float32).astype(jnp.bfloat16)
    lo = (np.asarray(table, np.float64) - hi.astype(np.float64)).astype(np.float32).astype(jnp.bfloat16)
    return hi, lo


def lane_table(table):
    hi, lo = split_np(table)
    row = np.concatenate([hi, lo], axis=1)
    return np.concatenate([row, row], axis=0)


def row_table(table):
    hi, lo = split_np(table)
    return np.concatenate([hi, hi, lo], axis=1)


def make_tables():
    step = 2.0 * math.pi / PAD
    k = np.arange(PAD)
    ang = (k[:, None] * k[None, :] % PAD) * step
    cos, sin = np.cos(ang), np.sin(ang)
    fwd_z = np.block([[cos, -sin], [sin, cos]])
    inv_z = np.block([[cos, sin], [-sin, cos]]) / PAD
    half = (np.arange(PAD // 2)[:, None] + 0.5) * step
    fwd_y = np.concatenate([np.cos(half * k), np.sin(half * k)], axis=0)
    core = k[MARGIN : MARGIN + E]
    inv_y = np.concatenate([np.cos(half * core), np.sin(half * core)], axis=0).T / PAD
    t = np.arange(KS) - MARGIN
    ang_t = (t[:, None] * k[None, :]) % PAD * step
    tap_z = np.zeros((128, 128))
    tap_z[:KS, :PAD] = np.cos(ang_t)
    tap_z[:KS, PAD:] = -np.sin(ang_t)
    tap_y = np.zeros((PAD, TAPROWS))
    tap_y[:, :KS] = np.concatenate([np.cos(half * t), np.sin(half * t)], axis=0)
    pack = np.zeros((8 * 128, 256), np.float32)
    place = np.zeros((256, 8 * 128), np.float32)
    for p in range(8):
        for s in range(2):
            for z in range(MARGIN):
                slot = p * 16 + s * 8 + z
                pack[p * 128 + s * 64 + MARGIN + z, slot] = 1
                pack[p * 128 + s * 64 + E + z, 128 + slot] = 1
                place[slot, p * 128 + s * 64 + z] = 1
                place[128 + slot, p * 128 + s * 64 + MARGIN + E + z] = 1
    return dict(
        fwd_z=lane_table(fwd_z),
        inv_z=lane_table(inv_z),
        tap_z=lane_table(tap_z),
        fwd_y=row_table(fwd_y),
        inv_y=row_table(inv_y),
        tap_y=row_table(tap_y),
        pack=pack.astype(jnp.bfloat16),
        place=place.astype(jnp.bfloat16),
    )


TABLES = make_tables()


def split(values):
    hi = values.astype(BF16)
    lo = (values - hi.astype(F32)).astype(BF16)
    return hi, lo


def low_lanes(shape):
    return lax.broadcasted_iota(jnp.int32, shape, len(shape) - 1) < 64


def lane_sign(shape):
    return jnp.where(low_lanes(shape), 1.0, -1.0).astype(F32)


def dot(a, b):
    return lax.dot_general(a, b, (((1,), (0,)), ((), ())), preferred_element_type=F32)


def lanes_dft(rows, table):
    hi, lo = split(rows)
    both = dot(jnp.concatenate([hi, lo], axis=1), table)
    return both[:, :128] + both[:, 128:]


def rows_dot(planes, table):
    out = []
    for a in range(0, len(planes), 2):
        cols = []
        for plane in planes[a : a + 2]:
            hi, lo = split(plane)
            cols.append(jnp.concatenate([hi, lo, hi], axis=0))
        both = dot(table, jnp.concatenate(cols, axis=1) if len(cols) > 1 else cols[0])
        out += [both[:, b * 128 : (b + 1) * 128] for b in range(len(cols))]
    return out


def rows_forward(planes, table):
    sign = lane_sign((PAD // 2, 128))
    out = []
    for both in rows_dot(planes, table):
        turned = sign * pltpu.roll(both[PAD // 2 :], 64, 1)
        out.append((both[: PAD // 2] + turned, both[: PAD // 2] - turned))
    return out


def rows_inverse(planes, table):
    sign = -lane_sign((PAD // 2, 128))
    folded = []
    for plane in planes:
        plus, minus = plane[: PAD // 2], plane[PAD // 2 :]
        folded.append(jnp.concatenate([plus + minus, sign * pltpu.roll(plus - minus, 64, 1)], axis=0))
    return rows_dot(folded, table)


def emit_faces(cp_ref, pack_ref, faces):
    xm_ref, xp_ref, ym_ref, yp_ref, zm_ref, zp_ref = faces
    wide = [
        jnp.concatenate([cp_ref[g * 8 + p].astype(BF16) for p in range(8)], axis=1) for g in range(3)
    ]
    both = dot(jnp.concatenate(wide, axis=0), pack_ref[...])
    zm_ref[...] = both[:, :128].astype(BF16)
    zp_ref[...] = both[:, 128:].astype(BF16)
    low = low_lanes((E, 128))
    for j in range(4):
        near = jnp.where(low, cp_ref[j], pltpu.roll(cp_ref[4 + j], 64, 1))
        xm_ref[j * E : (j + 1) * E, :] = near.astype(BF16)
        near = jnp.where(low, pltpu.roll(cp_ref[16 + j], 64, 1), cp_ref[20 + j])
        xp_ref[j * E : (j + 1) * E, :] = near.astype(BF16)
    ym_ref[...] = cp_ref[:, 0:8, :].reshape(HALF * 8, 128).astype(BF16)
    yp_ref[...] = cp_ref[:, E - 8 : E, :].reshape(HALF * 8, 128).astype(BF16)

FACE_SHAPES = [(4 * E, 128), (4 * E, 128), (HALF * 8, 128), (HALF * 8, 128), (3 * E, 128), (3 * E, 128)]


def flat_to_pairs(load, store):
    for j in range(8):
        total = None
        for half in range(2):
            first = 48 * j
            k, lane = first // 128, first % 128
            base = MARGIN + 64 * half
            value = load(k, half)
            part = value if lane == base else pltpu.roll(value, (base - lane) % 128, 1)
            at = lax.broadcasted_iota(jnp.int32, part.shape, 1) - base
            length = min(48, 128 - lane)
            picked = jnp.where((at >= 0) & (at < length), part, 0.0)
            if length < 48:
                more = pltpu.roll(load(k + 1, half), base + length, 1)
                picked = jnp.where((at >= length) & (at < 48), more, picked)
            total = picked if total is None else total + picked
        store(j, total)


def pairs_to_flat(load, store):
    for half in range(2):
        for k in range(3):
            total = None
            for j in range(8):
                lane = 48 * j - 128 * k
                if lane <= -48 or lane >= 128:
                    continue
                value = pltpu.roll(load(j), (lane - MARGIN - 64 * half) % 128, 1)
                at = lax.broadcasted_iota(jnp.int32, value.shape, 1) - lane
                picked = jnp.where((at >= 0) & (at < 48), value, 0.0)
                total = picked if total is None else total + picked
            store(k, half, total)


GROUPS = HALF * E // 8
FLAT = E3 // 128


def load_flat(ref):
    return lambda k, half: ref[pl.ds(half * 3 * GROUPS + k, GROUPS, stride=3), :]


def store_rows(ref):
    def store(j, rows):
        ref[pl.ds(j, GROUPS, stride=8), :] = rows

    return store


def prepare_cells(order_ref, list_ref, blend_ref, cells_ref, weights_ref, own_ref):
    number = lax.broadcasted_iota(jnp.int32, (1, 128), 1)
    weights_ref[...] = jnp.zeros_like(weights_ref)
    own_ref[...] = jnp.zeros_like(own_ref)
    for u in range(UPDATES):
        view = order_ref[u]
        first = jnp.full((1, 128), blend_ref[0, view], F32)
        second = jnp.full((1, 128), blend_ref[1, view], F32)
        total = first + second
        weights_ref[u : u + 1, :] = jnp.where(number == list_ref[0, view], first / total, 0.0) + jnp.where(
            number == list_ref[1, view], second / total, 0.0
        )
        for i in range(KS3 // 128):
            own_ref[u, i : i + 1, :] = cells_ref[view, :, i * 128 : (i + 1) * 128]
        tail = KS3 // 128 * 128
        i = KS3 // 128
        own_ref[u, i : i + 1, 0 : KS3 - tail] = cells_ref[view, :, tail:KS3]


def prepare_block(est_ref, pack_ref, cp_ref, faces):
    row_ref = cp_ref.reshape(HALF * E, 128)
    flat_to_pairs(load_flat(est_ref), store_rows(row_ref))
    emit_faces(cp_ref, pack_ref, faces)


def forward_planes(src_ref, z_ref, spec_ref, rows, fwd_z_ref, fwd_y_ref):
    group = PLANES

    def z_body(it, carry):
        block = src_ref[pl.ds(it * group, group)].reshape(group * rows, 128)
        z_ref[pl.ds(it * group, group), 0:rows, :] = lanes_dft(block, fwd_z_ref[...]).reshape(group, rows, 128)
        return carry

    lax.fori_loop(0, PLANES // group, z_body, 0)

    def y_body(it, carry):
        planes = [z_ref[it * group + j, 0:rows, :] for j in range(group)]
        for j, (plus, minus) in enumerate(rows_forward(planes, fwd_y_ref[...])):
            spec_ref[it * group + j, 0 : PAD // 2, :] = plus
            spec_ref[it * group + j, PAD // 2 : PAD, :] = minus
        return carry

    lax.fori_loop(0, PLANES // group, y_body, 0)


def filter_planes(spec_ref, kr_ref, ki_ref, out_ref, conjugate):
    group = 12
    sign = lane_sign((8, 128))
    if not conjugate:
        sign = -sign

    def body(kb, carry):
        rows = pl.ds(pl.multiple_of(kb * 8, 8), 8)
        for first in range(0, HALF, group):
            values = {}
            acc_r, acc_i = [None] * group, [None] * group
            for d in range(KS):
                tap = d if conjugate else KS - 1 - d
                kr = kr_ref[tap, rows, :]
                ki = ki_ref[tap, rows, :]
                for j in range(group):
                    m = first + j + d
                    if m not in values:
                        values[m] = spec_ref[m, rows, :]
                    if d == 0:
                        acc_r[j] = kr * values[m]
                        acc_i[j] = ki * values[m]
                    else:
                        acc_r[j] = acc_r[j] + kr * values[m]
                        acc_i[j] = acc_i[j] + ki * values[m]
            for j in range(group):
                out_ref[first + j, rows, :] = acc_r[j] + sign * pltpu.roll(acc_i[j], 64, 1)
        return carry

    lax.fori_loop(0, PAD // 8, body, 0)


def inverse_planes(spec_ref, y_ref, out_ref, inv_y_ref, inv_z_ref):
    group = 12

    def y_body(it, carry):
        planes = [spec_ref[it * group + j] for j in range(group)]
        for j, plane in enumerate(rows_inverse(planes, inv_y_ref[...])):
            y_ref[it * group + j, 0:E, :] = plane
        return carry

    lax.fori_loop(0, HALF // group, y_body, 0)

    def z_body(it, carry):
        block = y_ref[pl.ds(it * group, group), 0:E, :].reshape(group * E, 128)
        out_ref[pl.ds(it * group, group)] = lanes_dft(block, inv_z_ref[...]).reshape(group, E, 128)
        return carry

    lax.fori_loop(0, HALF // group, z_body, 0)


def tap_spectra(flat_ref, taps_ref, z_ref, kr_ref, ki_ref, tap_z_ref, tap_y_ref):
    lane = lax.broadcasted_iota(jnp.int32, (1, 128), 1)
    for r in range(KS * KS):
        i, at = KS * r // 128, KS * r % 128
        run = pltpu.roll(flat_ref[i : i + 1, :], (-at) % 128, 1)
        if at + KS > 128:
            more = pltpu.roll(flat_ref[i + 1 : i + 2, :], (-at) % 128, 1)
            run = jnp.where(lane < 128 - at, run, more)
        taps_ref[r // KS, r % KS : r % KS + 1, :] = run
    low = low_lanes((PAD // 2, 128))
    rows = lanes_dft(taps_ref[...].reshape(KS * TAPROWS, 128), tap_z_ref[...])
    z_ref[0:KS, 0:TAPROWS, :] = rows.reshape(KS, TAPROWS, 128)
    planes = [z_ref[d, 0:TAPROWS, :] for d in range(KS)]
    for d, specs in enumerate(rows_forward(planes, tap_y_ref[...])):
        for h, spec in enumerate(specs):
            other = pltpu.roll(spec, 64, 1)
            kr_ref[d, h * 32 : h * 32 + 32, :] = jnp.where(low, spec, other)
            ki_ref[d, h * 32 : h * 32 + 32, :] = jnp.where(low, other, spec)


def assemble(next_ref, cp_ref, halos, place_ref, ext_ref, pp_ref):
    hxm_ref, hxp_ref, hym_ref, hyp_ref, hzm_ref, hzp_ref = halos
    low_core = low_lanes((E, 128))
    low_row = low_lanes((8, 128))

    def face(ref, f):
        return jnp.where(next_ref[0, f] >= 0, ref[...].astype(F32), 0.0)

    ext_ref[:, 0:8, :] = face(hym_ref, 2).reshape(HALF, 8, 128)
    ext_ref[:, 56:64, :] = face(hyp_ref, 3).reshape(HALF, 8, 128)
    both = jnp.concatenate([face(hzm_ref, 4).astype(BF16), face(hzp_ref, 5).astype(BF16)], axis=1)
    margins = dot(both, place_ref[...])
    for g in range(3):
        for p in range(8):
            ext_ref[g * 8 + p, 8:56, :] = cp_ref[g * 8 + p] + margins[g * E : (g + 1) * E, p * 128 : (p + 1) * 128]
    xm = face(hxm_ref, 0).reshape(4, E, 128)
    xp = face(hxp_ref, 1).reshape(4, E, 128)
    pp_ref[8:32] = ext_ref[...]
    for j in range(8):
        for rows in (slice(0, 8), slice(56, 64)):
            near = ext_ref[16 + j, rows, :]
            pp_ref[j, rows, :] = pltpu.roll(jnp.where(low_row, near, 0.0), 64, 1)
            near = ext_ref[j, rows, :]
            pp_ref[32 + j, rows, :] = pltpu.roll(jnp.where(low_row, 0.0, near), 64, 1)
        before = xm[j] if j < 4 else pltpu.roll(xm[j - 4], 64, 1)
        after = pltpu.roll(xp[j], 64, 1) if j < 4 else xp[j - 4]
        pp_ref[j, 8:56, :] = jnp.where(low_core, before, pltpu.roll(ext_ref[16 + j, 8:56, :], 64, 1))
        pp_ref[32 + j, 8:56, :] = jnp.where(low_core, pltpu.roll(ext_ref[j, 8:56, :], 64, 1), after)


def correct(tissue_ref, cp_ref, new_ref, seen_ref, tables, work):
    fwd_z_ref, inv_z_ref, fwd_yc_ref, inv_y_ref = tables
    z_ref, spec_ref, kr_ref, ki_ref, fil_ref, core_ref, q_ref = work
    low_core = low_lanes((E, 128))
    filter_planes(spec_ref, kr_ref, ki_ref, fil_ref, False)
    inverse_planes(fil_ref, z_ref, core_ref, inv_y_ref, inv_z_ref)

    lane = lax.broadcasted_iota(jnp.int32, (E, 128), 1) % 64
    inside = (lane >= MARGIN) & (lane < MARGIN + E)

    def ratio_body(it, carry):
        for o in [it * 4 + j for j in range(4)]:
            q_ref[o + 8] = jnp.where(inside, seen_ref[o] / jnp.where(inside, core_ref[o], 1.0), 0.0)
        return carry

    lax.fori_loop(0, HALF // 4, ratio_body, 0)
    for j in range(8):
        q_ref[j] = pltpu.roll(jnp.where(low_core, q_ref[24 + j], 0.0), 64, 1)
        q_ref[32 + j] = pltpu.roll(jnp.where(low_core, 0.0, q_ref[8 + j]), 64, 1)

    forward_planes(q_ref, z_ref, spec_ref, E, fwd_z_ref, fwd_yc_ref)
    filter_planes(spec_ref, kr_ref, ki_ref, fil_ref, True)
    inverse_planes(fil_ref, z_ref, core_ref, inv_y_ref, inv_z_ref)

    alive = tissue_ref[0] > 0

    def finish(it, carry):
        for o in [it * 4 + j for j in range(4)]:
            old = cp_ref[o]
            new_ref[o] = jnp.where(jnp.logical_and(inside, alive), old * core_ref[o], old)
        return carry

    lax.fori_loop(0, HALF // 4, finish, 0)


VMEM = pl.BlockSpec(memory_space=pltpu.VMEM)
SMEM = pl.BlockSpec(memory_space=pltpu.SMEM)


def fwd_y_core():
    full = TABLES["fwd_y"]
    return np.concatenate([full[:, s * PAD + MARGIN : s * PAD + MARGIN + E] for s in range(3)], axis=1)


GRID = (4, 4, 8)


def coords_of(b):
    return (
        b % 2 + 2 * ((b // 8) % 2),
        (b // 2) % 2 + 2 * ((b // 16) % 2),
        (b // 64) % 2 + 2 * ((b // 4) % 2) + 4 * ((b // 32) % 2),
    )


def block_at(c):
    return (
        c[0] % 2 + 2 * (c[1] % 2) + 4 * ((c[2] // 2) % 2) + 8 * (c[0] // 2) + 16 * (c[1] // 2)
        + 32 * (c[2] // 4) + 64 * (c[2] % 2)
    )


def neighbour_of(b, axis, step):
    c = list(coords_of(b))
    c[axis] = (c[axis] + step + GRID[axis]) % GRID[axis]
    return block_at(c)


MESH = pl.DeviceIdType.MESH
NEAR = 8
FAR = 16


NEAR_ORDER = (4, 3, 5, 2, 6, 1, 7)
FAR_ORDER = (10, 6, 14, 9, 11, 5, 7, 13, 15, 2, 8, 1, 3, 4, 12)


def near_peers(me):
    base = me // NEAR * NEAR
    return [base + (me % NEAR + s) % NEAR for s in NEAR_ORDER]


def far_peers(me):
    return [(me // NEAR + s) % FAR * NEAR + me % NEAR for s in FAR_ORDER]


def face_peers(me):
    return [neighbour_of(me, f // 2, -1 if f % 2 == 0 else 1) for f in range(6)]


def face_copies(faces, halos, peers, send, recv):
    return [
        pltpu.make_async_remote_copy(
            src_ref=faces[f],
            dst_ref=halos[f ^ 1],
            send_sem=send.at[f],
            recv_sem=recv.at[f],
            device_id=(peers[f],),
            device_id_type=MESH,
        )
        for f in range(6)
    ]


def remote(src, dst, send, recv, peer):
    return pltpu.make_async_remote_copy(
        src_ref=src, dst_ref=dst, send_sem=send, recv_sem=recv, device_id=(peer,), device_id_type=MESH
    )


def blend_cells(u, cells_ref, weights_ref, pick, scaled_ref, parts_ref):
    for a in range(NEAR):
        cell = cells_ref[a]
        total = jnp.sum(jnp.sum(cell, axis=0, keepdims=True), axis=1, keepdims=True)
        scaled_ref[a] = cell / total

    def body(it, carry):
        for dest in [it * 8 + j for j in range(8)]:
            share = jnp.sum(weights_ref[dest, u : u + 1, :] * pick, axis=1, keepdims=True)
            total = share[0:1, :] * scaled_ref[0]
            for a in range(1, NEAR):
                total = total + share[a : a + 1, :] * scaled_ref[a]
            parts_ref[dest] = total
        return carry

    lax.fori_loop(0, FAR // 8, body, 0)


def whole_kernel(*refs):
    order_ref, list_ref, blend_ref, tissue_ref, next_ref = refs[:5]
    inputs = refs[5 : 5 + INPUTS]
    out_ref = refs[5 + INPUTS]
    local_refs = refs[6 + INPUTS : 6 + 2 * INPUTS]
    load_sem = refs[6 + 2 * INPUTS]
    refs = refs[7 + 2 * INPUTS :]
    loads = [pltpu.make_async_copy(inputs[i], local_refs[i], load_sem.at[i]) for i in range(INPUTS)]
    cells_ref, est_ref, pack_ref, cell_row_ref, seen_in, place_ref = local_refs[:6]
    fwd_z_ref, fwd_y_ref, tap_z_ref, tap_y_ref, inv_y_ref, inv_z_ref, fwd_yc_ref = local_refs[6:]
    for load in loads:
        load.start()
    cp_refs, own_ref, weights_ref = refs[:2], refs[2], refs[3]
    faces = (refs[4:10], refs[10:16])
    halos = (refs[16:22], refs[22:28])
    near_all, weights_all, parts, held = refs[28:30], refs[30], refs[31:33], refs[33:35]
    scaled_ref, kernel_ref, taps_ref, ext_ref, pp_ref, z_ref, spec_ref = refs[35:42]
    kr_ref, ki_ref, fil_ref, core_ref, q_ref, wide_ref, flat_ref = refs[42:49]
    own_sem, near_send, near_recv, share_send, share_recv = refs[49:54]
    far_send, far_recv, face_send, face_recv = refs[54:58]
    row_ref = flat_ref.reshape(HALF * E, 128)
    tables = (fwd_z_ref, inv_z_ref, fwd_yc_ref, inv_y_ref)
    work = (z_ref, spec_ref, kr_ref, ki_ref, fil_ref, core_ref, q_ref)

    me = lax.axis_index("blk")
    near, far, across = near_peers(me), far_peers(me), face_peers(me)
    barrier = pltpu.get_barrier_semaphore()
    for peer in near + far + across:
        pl.semaphore_signal(barrier, inc=1, device_id=(peer,), device_id_type=MESH)

    loads[0].wait()
    prepare_cells(order_ref, list_ref, blend_ref, cells_ref, weights_ref, own_ref)
    taps_ref[...] = jnp.zeros_like(taps_ref)
    pl.semaphore_wait(barrier, len(near + far + across))

    near_copies = [
        [
            remote(own_ref.at[u], near_all[u].at[me % NEAR], near_send.at[u, s], near_recv.at[u, s], peer)
            for s, peer in enumerate(near)
        ]
        + [pltpu.make_async_copy(own_ref.at[u], near_all[u].at[me % NEAR], own_sem.at[u])]
        for u in range(UPDATES)
    ]
    share_copies = [
        remote(weights_ref, weights_all.at[me // NEAR], share_send.at[s], share_recv.at[s], peer)
        for s, peer in enumerate(far)
    ] + [pltpu.make_async_copy(weights_ref, weights_all.at[me // NEAR], own_sem.at[2])]
    face_copies = [
        [
            remote(faces[u][f], halos[u][f ^ 1], face_send.at[u, f], face_recv.at[u, f], across[f])
            for f in (4, 5, 2, 3, 0, 1)
        ]
        for u in range(UPDATES)
    ]
    far_copies = [
        [
            remote(parts[u].at[(me // NEAR + FAR_ORDER[s]) % FAR], held[u].at[s], far_send.at[u, s], far_recv.at[u, s], peer)
            for s, peer in enumerate(far)
        ]
        for u in range(UPDATES)
    ]

    def start(copies):
        for copy in copies:
            copy.start()

    def wait(copies):
        for copy in copies:
            copy.wait()

    base = me // NEAR * NEAR

    def widen(it, carry):
        for j in range(8):
            at = pl.multiple_of(it * 1024 + j * 128, 128)
            wide_ref[pl.ds(pl.multiple_of(it * 64 + j * 8, 8), 6), :] = seen_in[:, pl.ds(at, 128)].astype(F32)
        return carry

    def seen_pairs(u):
        view = order_ref[u]

        def load(k, half):
            return wide_ref[pl.ds((half * 3 * GROUPS + k) * 8 + view, GROUPS, stride=24), :]

        flat_to_pairs(load, store_rows(row_ref))

    def spectra(u):
        total = parts[u][me // NEAR]
        for s in range(FAR - 1):
            total = total + held[u][s]
        kernel_ref[...] = total
        tap_spectra(kernel_ref, taps_ref, z_ref, kr_ref, ki_ref, tap_z_ref, tap_y_ref)

    def padded_spectra(u):
        wait(face_copies[u])
        assemble(next_ref, cp_refs[u], halos[u], place_ref, ext_ref, pp_ref)
        forward_planes(pp_ref, z_ref, spec_ref, PAD, fwd_z_ref, fwd_y_ref)

    start(near_copies[0])
    start(share_copies)
    for load in loads[1:3]:
        load.wait()
    prepare_block(est_ref, pack_ref, cp_refs[0], faces[0])
    start(face_copies[0])
    for load in loads[3:]:
        load.wait()
    pick = (cell_row_ref[...] == base + lax.broadcasted_iota(jnp.int32, (NEAR, 128), 0)).astype(F32)
    lax.fori_loop(0, FLAT // 8, widen, 0)
    wait(near_copies[0])
    wait(share_copies)
    blend_cells(0, near_all[0], weights_all, pick, scaled_ref, parts[0])
    start(far_copies[0])
    start(near_copies[1])
    seen_pairs(0)
    padded_spectra(0)
    wait(near_copies[1])
    blend_cells(1, near_all[1], weights_all, pick, scaled_ref, parts[1])
    wait(far_copies[0])
    start(far_copies[1])
    spectra(0)
    correct(tissue_ref, cp_refs[0], cp_refs[1], flat_ref, tables, work)
    emit_faces(cp_refs[1], pack_ref, faces[1])
    start(face_copies[1])
    wait(far_copies[1])
    spectra(1)
    seen_pairs(1)
    padded_spectra(1)
    correct(tissue_ref, cp_refs[1], flat_ref, flat_ref, tables, work)

    def load_new(j):
        return row_ref[pl.ds(j, GROUPS, stride=8), :]

    def store_new(k, half, rows):
        out_ref[pl.ds(half * 3 * GROUPS + k, GROUPS, stride=3), :] = rows

    pairs_to_flat(load_new, store_new)


HALO_SHAPES = [FACE_SHAPES[f ^ 1] for f in range(6)]
DMA = pltpu.SemaphoreType.DMA
INPUTS = 13


def whole_call(scalars, est, cells, cell_row, seen):
    inputs = [
        cells,
        est,
        jnp.asarray(TABLES["pack"]),
        cell_row,
        seen,
        jnp.asarray(TABLES["place"]),
        jnp.asarray(TABLES["fwd_z"]),
        jnp.asarray(TABLES["fwd_y"]),
        jnp.asarray(TABLES["tap_z"]),
        jnp.asarray(TABLES["tap_y"]),
        jnp.asarray(TABLES["inv_y"]),
        jnp.asarray(TABLES["inv_z"]),
        jnp.asarray(fwd_y_core()),
    ]
    f32 = [
        (NEAR, CELLROWS, 128),
        (NEAR, CELLROWS, 128),
        (FAR, 8, 128),
        (FAR, CELLROWS, 128),
        (FAR, CELLROWS, 128),
        (FAR - 1, CELLROWS, 128),
        (FAR - 1, CELLROWS, 128),
        (NEAR, CELLROWS, 128),
        (CELLROWS, 128),
        (KS, TAPROWS, 128),
        (HALF, PAD, 128),
        (PLANES, PAD, 128),
        (PLANES, PAD, 128),
        (PLANES, PAD, 128),
        (KS, PAD, 128),
        (KS, PAD, 128),
        (HALF, PAD, 128),
        (HALF, E, 128),
        (PLANES, E, 128),
        (FLAT * 8, 128),
        (HALF, E, 128),
    ]
    scratch = [pltpu.VMEM(x.shape, x.dtype) for x in inputs] + [DMA((INPUTS,))]
    scratch += [pltpu.VMEM(s, F32) for s in [(HALF, E, 128)] * 2 + [(UPDATES, CELLROWS, 128), (8, 128)]]
    scratch += [pltpu.VMEM(s, BF16) for s in FACE_SHAPES * 2 + HALO_SHAPES * 2]
    scratch += [pltpu.VMEM(s, F32) for s in f32]
    scratch += [DMA((3,)), DMA((2, NEAR - 1)), DMA((2, NEAR - 1)), DMA((FAR - 1,)), DMA((FAR - 1,))]
    scratch += [DMA((2, FAR - 1)), DMA((2, FAR - 1)), DMA((2, 6)), DMA((2, 6))]
    return pl.pallas_call(
        whole_kernel,
        out_shape=pltpu.VMEM((FLAT, 128), F32),
        in_specs=[SMEM] * 5 + [pl.BlockSpec(memory_space=pl.ANY)] * INPUTS,
        out_specs=VMEM,
        scratch_shapes=scratch,
        compiler_params=pltpu.CompilerParams(collective_id=0, has_side_effects=True),
        name="whole",
    )(*scalars, *inputs)


def local(
    estimate, observed, psf_cells, tissue, neighbours, psf_list, psf_blend, cell_row, view_order
):
    scalars = (
        view_order,
        psf_list.transpose(0, 2, 1).reshape(2, 6),
        psf_blend.transpose(0, 2, 1).reshape(2, 6),
        tissue,
        neighbours,
    )
    result = whole_call(
        scalars,
        estimate.reshape(FLAT, 128),
        psf_cells.reshape(6, 1, KS3),
        cell_row.reshape(1, 128),
        observed.reshape(6, E3),
    )
    return result.reshape(1, E3)


def solution(mesh):
    return jax.shard_map(
        local,
        mesh=mesh,
        in_specs=(
            P("blk", None),
            P("blk", None, None),
            P("blk", None, None),
            P("blk"),
            P("blk", None),
            P("blk", None, None),
            P("blk", None, None),
            P(),
            P(),
        ),
        out_specs=P("blk", None),
        check_vma=False,
    )
```

```python
import functools
import math

import jax
import jax.numpy as jnp
import numpy as np
from jax import lax
from jax.experimental import pallas as pl
from jax.experimental.pallas import tpu as pltpu
from jax.sharding import PartitionSpec as P

E = 48
MARGIN = 8
UPDATES = 2
PAD = 64
KS = 17
E3 = 110592
KS3 = 4913
HALF = 24
PLANES = 40
TAPROWS = 32

CELLROWS = 40
ROWS = UPDATES * CELLROWS

F32 = jnp.float32
BF16 = jnp.bfloat16


def split_np(table):
    hi = np.asarray(table, np.float32).astype(jnp.bfloat16)
    lo = (np.asarray(table, np.float64) - hi.astype(np.float64)).astype(np.float32).astype(jnp.bfloat16)
    return hi, lo


def lane_table(table):
    hi, lo = split_np(table)
    row = np.concatenate([hi, lo], axis=1)
    return np.concatenate([row, row], axis=0)


def row_table(table):
    hi, lo = split_np(table)
    return np.concatenate([hi, hi, lo], axis=1)


def make_tables():
    step = 2.0 * math.pi / PAD
    k = np.arange(PAD)
    ang = (k[:, None] * k[None, :] % PAD) * step
    cos, sin = np.cos(ang), np.sin(ang)
    fwd_z = np.block([[cos, -sin], [sin, cos]])
    inv_z = np.block([[cos, sin], [-sin, cos]]) / PAD
    half = (np.arange(PAD // 2)[:, None] + 0.5) * step
    fwd_y = np.concatenate([np.cos(half * k), np.sin(half * k)], axis=0)
    core = k[MARGIN : MARGIN + E]
    inv_y = np.concatenate([np.cos(half * core), np.sin(half * core)], axis=0).T / PAD
    t = np.arange(KS) - MARGIN
    ang_t = (t[:, None] * k[None, :]) % PAD * step
    tap_z = np.zeros((128, 128))
    tap_z[:KS, :PAD] = np.cos(ang_t)
    tap_z[:KS, PAD:] = -np.sin(ang_t)
    tap_y = np.zeros((PAD, TAPROWS))
    tap_y[:, :KS] = np.concatenate([np.cos(half * t), np.sin(half * t)], axis=0)
    pack = np.zeros((8 * 128, 256), np.float32)
    place = np.zeros((256, 8 * 128), np.float32)
    for p in range(8):
        for s in range(2):
            for z in range(MARGIN):
                slot = p * 16 + s * 8 + z
                pack[p * 128 + s * 64 + MARGIN + z, slot] = 1
                pack[p * 128 + s * 64 + E + z, 128 + slot] = 1
                place[slot, p * 128 + s * 64 + z] = 1
                place[128 + slot, p * 128 + s * 64 + MARGIN + E + z] = 1
    return dict(
        fwd_z=lane_table(fwd_z),
        inv_z=lane_table(inv_z),
        tap_z=lane_table(tap_z),
        fwd_y=row_table(fwd_y),
        inv_y=row_table(inv_y),
        tap_y=row_table(tap_y),
        pack=pack.astype(jnp.bfloat16),
        place=place.astype(jnp.bfloat16),
    )


TABLES = make_tables()


def split(values):
    hi = values.astype(BF16)
    lo = (values - hi.astype(F32)).astype(BF16)
    return hi, lo


def low_lanes(shape):
    return lax.broadcasted_iota(jnp.int32, shape, len(shape) - 1) < 64


def lane_sign(shape):
    return jnp.where(low_lanes(shape), 1.0, -1.0).astype(F32)


def dot(a, b):
    return lax.dot_general(a, b, (((1,), (0,)), ((), ())), preferred_element_type=F32)


def lanes_dft(rows, table):
    hi, lo = split(rows)
    both = dot(jnp.concatenate([hi, lo], axis=1), table)
    return both[:, :128] + both[:, 128:]


def rows_dot(planes, table):
    out = []
    for a in range(0, len(planes), 2):
        cols = []
        for plane in planes[a : a + 2]:
            hi, lo = split(plane)
            cols.append(jnp.concatenate([hi, lo, hi], axis=0))
        both = dot(table, jnp.concatenate(cols, axis=1) if len(cols) > 1 else cols[0])
        out += [both[:, b * 128 : (b + 1) * 128] for b in range(len(cols))]
    return out


def rows_forward(planes, table):
    sign = lane_sign((PAD // 2, 128))
    out = []
    for both in rows_dot(planes, table):
        turned = sign * pltpu.roll(both[PAD // 2 :], 64, 1)
        out.append((both[: PAD // 2] + turned, both[: PAD // 2] - turned))
    return out


def rows_inverse(planes, table):
    sign = -lane_sign((PAD // 2, 128))
    folded = []
    for plane in planes:
        plus, minus = plane[: PAD // 2], plane[PAD // 2 :]
        folded.append(jnp.concatenate([plus + minus, sign * pltpu.roll(plus - minus, 64, 1)], axis=0))
    return rows_dot(folded, table)


def emit_faces(cp_ref, pack_ref, faces):
    xm_ref, xp_ref, ym_ref, yp_ref, zm_ref, zp_ref = faces
    wide = [
        jnp.concatenate([cp_ref[g * 8 + p].astype(BF16) for p in range(8)], axis=1) for g in range(3)
    ]
    both = dot(jnp.concatenate(wide, axis=0), pack_ref[...])
    zm_ref[...] = both[:, :128].astype(BF16)
    zp_ref[...] = both[:, 128:].astype(BF16)
    low = low_lanes((E, 128))
    for j in range(4):
        near = jnp.where(low, cp_ref[j], pltpu.roll(cp_ref[4 + j], 64, 1))
        xm_ref[j * E : (j + 1) * E, :] = near.astype(BF16)
        near = jnp.where(low, pltpu.roll(cp_ref[16 + j], 64, 1), cp_ref[20 + j])
        xp_ref[j * E : (j + 1) * E, :] = near.astype(BF16)
    ym_ref[...] = cp_ref[:, 0:8, :].reshape(HALF * 8, 128).astype(BF16)
    yp_ref[...] = cp_ref[:, E - 8 : E, :].reshape(HALF * 8, 128).astype(BF16)

FACE_SHAPES = [(4 * E, 128), (4 * E, 128), (HALF * 8, 128), (HALF * 8, 128), (3 * E, 128), (3 * E, 128)]


def flat_to_pairs(load, store):
    for j in range(8):
        total = None
        for half in range(2):
            first = 48 * j
            k, lane = first // 128, first % 128
            base = MARGIN + 64 * half
            value = load(k, half)
            part = value if lane == base else pltpu.roll(value, (base - lane) % 128, 1)
            at = lax.broadcasted_iota(jnp.int32, part.shape, 1) - base
            length = min(48, 128 - lane)
            picked = jnp.where((at >= 0) & (at < length), part, 0.0)
            if length < 48:
                more = pltpu.roll(load(k + 1, half), base + length, 1)
                picked = jnp.where((at >= length) & (at < 48), more, picked)
            total = picked if total is None else total + picked
        store(j, total)


def pairs_to_flat(load, store):
    for half in range(2):
        for k in range(3):
            total = None
            for j in range(8):
                lane = 48 * j - 128 * k
                if lane <= -48 or lane >= 128:
                    continue
                value = pltpu.roll(load(j), (lane - MARGIN - 64 * half) % 128, 1)
                at = lax.broadcasted_iota(jnp.int32, value.shape, 1) - lane
                picked = jnp.where((at >= 0) & (at < 48), value, 0.0)
                total = picked if total is None else total + picked
            store(k, half, total)


GROUPS = HALF * E // 8
FLAT = E3 // 128


def load_flat(ref):
    return lambda k, half: ref[pl.ds(half * 3 * GROUPS + k, GROUPS, stride=3), :]


def store_rows(ref):
    def store(j, rows):
        ref[pl.ds(j, GROUPS, stride=8), :] = rows

    return store


def prepare_cells(order_ref, list_ref, blend_ref, cells_ref, weights_ref, own_ref):
    number = lax.broadcasted_iota(jnp.int32, (1, 128), 1)
    for u in range(UPDATES):
        view = order_ref[u]
        first = jnp.full((1, 128), blend_ref[0, view], F32)
        second = jnp.full((1, 128), blend_ref[1, view], F32)
        total = first + second
        weights_ref[u : u + 1, :] = jnp.where(number == list_ref[0, view], first / total, 0.0) + jnp.where(
            number == list_ref[1, view], second / total, 0.0
        )
        for i in range(KS3 // 128):
            own_ref[u, i : i + 1, :] = cells_ref[view, :, i * 128 : (i + 1) * 128]
        tail = KS3 // 128 * 128
        i = KS3 // 128
        own_ref[u, i : i + 1, 0 : KS3 - tail] = cells_ref[view, :, tail:KS3]


def prepare_block(est_ref, pack_ref, cp_ref, faces):
    row_ref = cp_ref.reshape(HALF * E, 128)
    flat_to_pairs(load_flat(est_ref), store_rows(row_ref))
    emit_faces(cp_ref, pack_ref, faces)


def forward_planes(src_ref, z_ref, spec_ref, rows, fwd_z_ref, fwd_y_ref):
    group = PLANES

    def z_body(it, carry):
        block = src_ref[pl.ds(it * group, group)].reshape(group * rows, 128)
        z_ref[pl.ds(it * group, group), 0:rows, :] = lanes_dft(block, fwd_z_ref[...]).reshape(group, rows, 128)
        return carry

    lax.fori_loop(0, PLANES // group, z_body, 0)

    def y_body(it, carry):
        planes = [z_ref[it * group + j, 0:rows, :] for j in range(group)]
        for j, (plus, minus) in enumerate(rows_forward(planes, fwd_y_ref[...])):
            spec_ref[it * group + j, 0 : PAD // 2, :] = plus
            spec_ref[it * group + j, PAD // 2 : PAD, :] = minus
        return carry

    lax.fori_loop(0, PLANES // group, y_body, 0)


def filter_planes(spec_ref, kr_ref, ki_ref, out_ref, conjugate):
    group = 12
    sign = lane_sign((8, 128))
    if not conjugate:
        sign = -sign

    def body(kb, carry):
        rows = pl.ds(pl.multiple_of(kb * 8, 8), 8)
        for first in range(0, HALF, group):
            values = {}
            acc_r, acc_i = [None] * group, [None] * group
            for d in range(KS):
                tap = d if conjugate else KS - 1 - d
                kr = kr_ref[tap, rows, :]
                ki = ki_ref[tap, rows, :]
                for j in range(group):
                    m = first + j + d
                    if m not in values:
                        values[m] = spec_ref[m, rows, :]
                    if d == 0:
                        acc_r[j] = kr * values[m]
                        acc_i[j] = ki * values[m]
                    else:
                        acc_r[j] = acc_r[j] + kr * values[m]
                        acc_i[j] = acc_i[j] + ki * values[m]
            for j in range(group):
                out_ref[first + j, rows, :] = acc_r[j] + sign * pltpu.roll(acc_i[j], 64, 1)
        return carry

    lax.fori_loop(0, PAD // 8, body, 0)


def inverse_planes(spec_ref, y_ref, out_ref, inv_y_ref, inv_z_ref):
    group = 12

    def y_body(it, carry):
        planes = [spec_ref[it * group + j] for j in range(group)]
        for j, plane in enumerate(rows_inverse(planes, inv_y_ref[...])):
            y_ref[it * group + j, 0:E, :] = plane
        return carry

    lax.fori_loop(0, HALF // group, y_body, 0)

    def z_body(it, carry):
        block = y_ref[pl.ds(it * group, group), 0:E, :].reshape(group * E, 128)
        out_ref[pl.ds(it * group, group)] = lanes_dft(block, inv_z_ref[...]).reshape(group, E, 128)
        return carry

    lax.fori_loop(0, HALF // group, z_body, 0)


def tap_spectra(flat_ref, taps_ref, z_ref, kr_ref, ki_ref, tap_z_ref, tap_y_ref):
    lane = lax.broadcasted_iota(jnp.int32, (1, 128), 1)
    for r in range(KS * KS):
        i, at = KS * r // 128, KS * r % 128
        run = pltpu.roll(flat_ref[i : i + 1, :], (-at) % 128, 1)
        if at + KS > 128:
            more = pltpu.roll(flat_ref[i + 1 : i + 2, :], (-at) % 128, 1)
            run = jnp.where(lane < 128 - at, run, more)
        taps_ref[r // KS, r % KS : r % KS + 1, :] = run
    low = low_lanes((PAD // 2, 128))
    rows = lanes_dft(taps_ref[...].reshape(KS * TAPROWS, 128), tap_z_ref[...])
    z_ref[0:KS, 0:TAPROWS, :] = rows.reshape(KS, TAPROWS, 128)
    planes = [z_ref[d, 0:TAPROWS, :] for d in range(KS)]
    for d, specs in enumerate(rows_forward(planes, tap_y_ref[...])):
        for h, spec in enumerate(specs):
            other = pltpu.roll(spec, 64, 1)
            kr_ref[d, h * 32 : h * 32 + 32, :] = jnp.where(low, spec, other)
            ki_ref[d, h * 32 : h * 32 + 32, :] = jnp.where(low, other, spec)


def assemble(next_ref, cp_ref, halos, place_ref, ext_ref, pp_ref):
    hxm_ref, hxp_ref, hym_ref, hyp_ref, hzm_ref, hzp_ref = halos
    low_core = low_lanes((E, 128))
    low_row = low_lanes((8, 128))

    def face(ref, f):
        return jnp.where(next_ref[0, f] >= 0, ref[...].astype(F32), 0.0)

    ext_ref[:, 0:8, :] = face(hym_ref, 2).reshape(HALF, 8, 128)
    ext_ref[:, 56:64, :] = face(hyp_ref, 3).reshape(HALF, 8, 128)
    both = jnp.concatenate([face(hzm_ref, 4).astype(BF16), face(hzp_ref, 5).astype(BF16)], axis=1)
    margins = dot(both, place_ref[...])
    for g in range(3):
        for p in range(8):
            ext_ref[g * 8 + p, 8:56, :] = cp_ref[g * 8 + p] + margins[g * E : (g + 1) * E, p * 128 : (p + 1) * 128]
    xm = face(hxm_ref, 0).reshape(4, E, 128)
    xp = face(hxp_ref, 1).reshape(4, E, 128)
    pp_ref[8:32] = ext_ref[...]
    for j in range(8):
        for rows in (slice(0, 8), slice(56, 64)):
            near = ext_ref[16 + j, rows, :]
            pp_ref[j, rows, :] = pltpu.roll(jnp.where(low_row, near, 0.0), 64, 1)
            near = ext_ref[j, rows, :]
            pp_ref[32 + j, rows, :] = pltpu.roll(jnp.where(low_row, 0.0, near), 64, 1)
        before = xm[j] if j < 4 else pltpu.roll(xm[j - 4], 64, 1)
        after = pltpu.roll(xp[j], 64, 1) if j < 4 else xp[j - 4]
        pp_ref[j, 8:56, :] = jnp.where(low_core, before, pltpu.roll(ext_ref[16 + j, 8:56, :], 64, 1))
        pp_ref[32 + j, 8:56, :] = jnp.where(low_core, pltpu.roll(ext_ref[j, 8:56, :], 64, 1), after)


def correct(tissue_ref, cp_ref, new_ref, seen_ref, tables, work):
    fwd_z_ref, inv_z_ref, fwd_yc_ref, inv_y_ref = tables
    z_ref, spec_ref, kr_ref, ki_ref, fil_ref, core_ref, q_ref = work
    low_core = low_lanes((E, 128))
    filter_planes(spec_ref, kr_ref, ki_ref, fil_ref, False)
    inverse_planes(fil_ref, z_ref, core_ref, inv_y_ref, inv_z_ref)

    lane = lax.broadcasted_iota(jnp.int32, (E, 128), 1) % 64
    inside = (lane >= MARGIN) & (lane < MARGIN + E)

    def ratio_body(it, carry):
        for o in [it * 4 + j for j in range(4)]:
            q_ref[o + 8] = jnp.where(inside, seen_ref[o] / jnp.where(inside, core_ref[o], 1.0), 0.0)
        return carry

    lax.fori_loop(0, HALF // 4, ratio_body, 0)
    for j in range(8):
        q_ref[j] = pltpu.roll(jnp.where(low_core, q_ref[24 + j], 0.0), 64, 1)
        q_ref[32 + j] = pltpu.roll(jnp.where(low_core, 0.0, q_ref[8 + j]), 64, 1)

    forward_planes(q_ref, z_ref, spec_ref, E, fwd_z_ref, fwd_yc_ref)
    filter_planes(spec_ref, kr_ref, ki_ref, fil_ref, True)
    inverse_planes(fil_ref, z_ref, core_ref, inv_y_ref, inv_z_ref)

    alive = tissue_ref[0] > 0

    def finish(it, carry):
        for o in [it * 4 + j for j in range(4)]:
            old = cp_ref[o]
            new_ref[o] = jnp.where(jnp.logical_and(inside, alive), old * core_ref[o], old)
        return carry

    lax.fori_loop(0, HALF // 4, finish, 0)


VMEM = pl.BlockSpec(memory_space=pltpu.VMEM)
SMEM = pl.BlockSpec(memory_space=pltpu.SMEM)


def fwd_y_core():
    full = TABLES["fwd_y"]
    return np.concatenate([full[:, s * PAD + MARGIN : s * PAD + MARGIN + E] for s in range(3)], axis=1)


GRID = (4, 4, 8)


def coords_of(b):
    return (
        b % 2 + 2 * ((b // 8) % 2),
        (b // 2) % 2 + 2 * ((b // 16) % 2),
        (b // 64) % 2 + 2 * ((b // 4) % 2) + 4 * ((b // 32) % 2),
    )


def block_at(c):
    return (
        c[0] % 2 + 2 * (c[1] % 2) + 4 * ((c[2] // 2) % 2) + 8 * (c[0] // 2) + 16 * (c[1] // 2)
        + 32 * (c[2] // 4) + 64 * (c[2] % 2)
    )


def neighbour_of(b, axis, step):
    c = list(coords_of(b))
    c[axis] = (c[axis] + step + GRID[axis]) % GRID[axis]
    return block_at(c)


MESH = pl.DeviceIdType.MESH
NEAR = 8
FAR = 16


NEAR_ORDER = (4, 3, 5, 2, 6, 1, 7)
FAR_ORDER = (10, 6, 14, 9, 11, 5, 7, 13, 15, 2, 8, 1, 3, 4, 12)


def near_peers(me):
    base = me // NEAR * NEAR
    return [base + (me % NEAR + s) % NEAR for s in NEAR_ORDER]


def far_peers(me):
    return [(me // NEAR + s) % FAR * NEAR + me % NEAR for s in FAR_ORDER]


def face_peers(me):
    return [neighbour_of(me, f // 2, -1 if f % 2 == 0 else 1) for f in range(6)]


def face_copies(faces, halos, peers, send, recv):
    return [
        pltpu.make_async_remote_copy(
            src_ref=faces[f],
            dst_ref=halos[f ^ 1],
            send_sem=send.at[f],
            recv_sem=recv.at[f],
            device_id=(peers[f],),
            device_id_type=MESH,
        )
        for f in range(6)
    ]


def remote(src, dst, send, recv, peer):
    return pltpu.make_async_remote_copy(
        src_ref=src, dst_ref=dst, send_sem=send, recv_sem=recv, device_id=(peer,), device_id_type=MESH
    )


def blend_cells(u, cells_ref, weights_ref, pick, scaled_ref, parts_ref):
    for a in range(NEAR):
        cell = cells_ref[a]
        total = jnp.sum(jnp.sum(cell, axis=0, keepdims=True), axis=1, keepdims=True)
        scaled_ref[a] = cell / total

    def body(it, carry):
        for dest in [it * 8 + j for j in range(8)]:
            share = jnp.sum(weights_ref[dest, u : u + 1, :] * pick, axis=1, keepdims=True)
            total = share[0:1, :] * scaled_ref[0]
            for a in range(1, NEAR):
                total = total + share[a : a + 1, :] * scaled_ref[a]
            parts_ref[dest] = total
        return carry

    lax.fori_loop(0, FAR // 8, body, 0)


def whole_kernel(*refs):
    order_ref, list_ref, blend_ref, tissue_ref, next_ref = refs[:5]
    inputs = refs[5 : 5 + INPUTS]
    out_ref = refs[5 + INPUTS]
    local_refs = refs[6 + INPUTS : 6 + 2 * INPUTS]
    load_sem = refs[6 + 2 * INPUTS]
    refs = refs[7 + 2 * INPUTS :]
    loads = [pltpu.make_async_copy(inputs[i], local_refs[i], load_sem.at[i]) for i in range(INPUTS)]
    cells_ref, est_ref, pack_ref, cell_row_ref, seen_in, place_ref = local_refs[:6]
    fwd_z_ref, fwd_y_ref, tap_z_ref, tap_y_ref, inv_y_ref, inv_z_ref, fwd_yc_ref = local_refs[6:]
    for load in loads:
        load.start()
    cp_refs, own_ref, weights_ref = refs[:2], refs[2], refs[3]
    faces = (refs[4:10], refs[10:16])
    halos = (refs[16:22], refs[22:28])
    near_all, weights_all, parts, held = refs[28:30], refs[30], refs[31:33], refs[33:35]
    scaled_ref, kernel_ref, taps_ref, ext_ref, pp_ref, z_ref, spec_ref = refs[35:42]
    kr_ref, ki_ref, fil_ref, core_ref, q_ref, wide_ref, flat_ref = refs[42:49]
    own_sem, near_send, near_recv, share_send, share_recv = refs[49:54]
    far_send, far_recv, face_send, face_recv = refs[54:58]
    row_ref = flat_ref.reshape(HALF * E, 128)
    tables = (fwd_z_ref, inv_z_ref, fwd_yc_ref, inv_y_ref)
    work = (z_ref, spec_ref, kr_ref, ki_ref, fil_ref, core_ref, q_ref)

    me = lax.axis_index("blk")
    near, far, across = near_peers(me), far_peers(me), face_peers(me)
    barrier = pltpu.get_barrier_semaphore()
    for peer in near + far + across:
        pl.semaphore_signal(barrier, inc=1, device_id=(peer,), device_id_type=MESH)

    weights_ref[...] = jnp.zeros_like(weights_ref)
    own_ref[...] = jnp.zeros_like(own_ref)
    taps_ref[...] = jnp.zeros_like(taps_ref)
    loads[0].wait()
    prepare_cells(order_ref, list_ref, blend_ref, cells_ref, weights_ref, own_ref)
    pl.semaphore_wait(barrier, len(near + far + across))

    near_copies = [
        [
            remote(own_ref.at[u], near_all[u].at[me % NEAR], near_send.at[u, s], near_recv.at[u, s], peer)
            for s, peer in enumerate(near)
        ]
        + [pltpu.make_async_copy(own_ref.at[u], near_all[u].at[me % NEAR], own_sem.at[u])]
        for u in range(UPDATES)
    ]
    share_copies = [
        remote(weights_ref, weights_all.at[me // NEAR], share_send.at[s], share_recv.at[s], peer)
        for s, peer in enumerate(far)
    ] + [pltpu.make_async_copy(weights_ref, weights_all.at[me // NEAR], own_sem.at[2])]
    face_copies = [
        [
            remote(faces[u][f], halos[u][f ^ 1], face_send.at[u, f], face_recv.at[u, f], across[f])
            for f in (4, 5, 2, 3, 0, 1)
        ]
        for u in range(UPDATES)
    ]
    far_copies = [
        [
            remote(parts[u].at[(me // NEAR + FAR_ORDER[s]) % FAR], held[u].at[s], far_send.at[u, s], far_recv.at[u, s], peer)
            for s, peer in enumerate(far)
        ]
        for u in range(UPDATES)
    ]

    def start(copies):
        for copy in copies:
            copy.start()

    def wait(copies):
        for copy in copies:
            copy.wait()

    base = me // NEAR * NEAR

    def widen(it, carry):
        for j in range(8):
            at = pl.multiple_of(it * 1024 + j * 128, 128)
            wide_ref[pl.ds(pl.multiple_of(it * 64 + j * 8, 8), 6), :] = seen_in[:, pl.ds(at, 128)].astype(F32)
        return carry

    def seen_pairs(u):
        view = order_ref[u]

        def load(k, half):
            return wide_ref[pl.ds((half * 3 * GROUPS + k) * 8 + view, GROUPS, stride=24), :]

        flat_to_pairs(load, store_rows(row_ref))

    def spectra(u):
        total = parts[u][me // NEAR]
        for s in range(FAR - 1):
            total = total + held[u][s]
        kernel_ref[...] = total
        tap_spectra(kernel_ref, taps_ref, z_ref, kr_ref, ki_ref, tap_z_ref, tap_y_ref)

    def padded_spectra(u):
        wait(face_copies[u])
        assemble(next_ref, cp_refs[u], halos[u], place_ref, ext_ref, pp_ref)
        forward_planes(pp_ref, z_ref, spec_ref, PAD, fwd_z_ref, fwd_y_ref)

    start(near_copies[0])
    start(share_copies)
    for load in loads[1:3]:
        load.wait()
    prepare_block(est_ref, pack_ref, cp_refs[0], faces[0])
    start(face_copies[0])
    for load in loads[3:]:
        load.wait()
    pick = (cell_row_ref[...] == base + lax.broadcasted_iota(jnp.int32, (NEAR, 128), 0)).astype(F32)
    lax.fori_loop(0, FLAT // 8, widen, 0)
    wait(near_copies[0])
    wait(share_copies)
    blend_cells(0, near_all[0], weights_all, pick, scaled_ref, parts[0])
    start(far_copies[0])
    start(near_copies[1])
    seen_pairs(0)
    padded_spectra(0)
    wait(near_copies[1])
    blend_cells(1, near_all[1], weights_all, pick, scaled_ref, parts[1])
    wait(far_copies[0])
    start(far_copies[1])
    spectra(0)
    correct(tissue_ref, cp_refs[0], cp_refs[1], flat_ref, tables, work)
    emit_faces(cp_refs[1], pack_ref, faces[1])
    start(face_copies[1])
    wait(far_copies[1])
    spectra(1)
    seen_pairs(1)
    padded_spectra(1)
    correct(tissue_ref, cp_refs[1], flat_ref, flat_ref, tables, work)

    def load_new(j):
        return row_ref[pl.ds(j, GROUPS, stride=8), :]

    def store_new(k, half, rows):
        out_ref[pl.ds(half * 3 * GROUPS + k, GROUPS, stride=3), :] = rows

    pairs_to_flat(load_new, store_new)


HALO_SHAPES = [FACE_SHAPES[f ^ 1] for f in range(6)]
DMA = pltpu.SemaphoreType.DMA
INPUTS = 13


def whole_call(scalars, est, cells, cell_row, seen):
    inputs = [
        cells,
        est,
        jnp.asarray(TABLES["pack"]),
        cell_row,
        seen,
        jnp.asarray(TABLES["place"]),
        jnp.asarray(TABLES["fwd_z"]),
        jnp.asarray(TABLES["fwd_y"]),
        jnp.asarray(TABLES["tap_z"]),
        jnp.asarray(TABLES["tap_y"]),
        jnp.asarray(TABLES["inv_y"]),
        jnp.asarray(TABLES["inv_z"]),
        jnp.asarray(fwd_y_core()),
    ]
    f32 = [
        (NEAR, CELLROWS, 128),
        (NEAR, CELLROWS, 128),
        (FAR, 8, 128),
        (FAR, CELLROWS, 128),
        (FAR, CELLROWS, 128),
        (FAR - 1, CELLROWS, 128),
        (FAR - 1, CELLROWS, 128),
        (NEAR, CELLROWS, 128),
        (CELLROWS, 128),
        (KS, TAPROWS, 128),
        (HALF, PAD, 128),
        (PLANES, PAD, 128),
        (PLANES, PAD, 128),
        (PLANES, PAD, 128),
        (KS, PAD, 128),
        (KS, PAD, 128),
        (HALF, PAD, 128),
        (HALF, E, 128),
        (PLANES, E, 128),
        (FLAT * 8, 128),
        (HALF, E, 128),
    ]
    scratch = [pltpu.VMEM(x.shape, x.dtype) for x in inputs] + [DMA((INPUTS,))]
    scratch += [pltpu.VMEM(s, F32) for s in [(HALF, E, 128)] * 2 + [(UPDATES, CELLROWS, 128), (8, 128)]]
    scratch += [pltpu.VMEM(s, BF16) for s in FACE_SHAPES * 2 + HALO_SHAPES * 2]
    scratch += [pltpu.VMEM(s, F32) for s in f32]
    scratch += [DMA((3,)), DMA((2, NEAR - 1)), DMA((2, NEAR - 1)), DMA((FAR - 1,)), DMA((FAR - 1,))]
    scratch += [DMA((2, FAR - 1)), DMA((2, FAR - 1)), DMA((2, 6)), DMA((2, 6))]
    return pl.pallas_call(
        whole_kernel,
        out_shape=pltpu.VMEM((FLAT, 128), F32),
        in_specs=[SMEM] * 5 + [pl.BlockSpec(memory_space=pl.ANY)] * INPUTS,
        out_specs=VMEM,
        scratch_shapes=scratch,
        compiler_params=pltpu.CompilerParams(collective_id=0, has_side_effects=True),
        name="whole",
    )(*scalars, *inputs)


def local(
    estimate, observed, psf_cells, tissue, neighbours, psf_list, psf_blend, cell_row, view_order
):
    scalars = (
        view_order,
        psf_list.transpose(0, 2, 1).reshape(2, 6),
        psf_blend.transpose(0, 2, 1).reshape(2, 6),
        tissue,
        neighbours,
    )
    result = whole_call(
        scalars,
        estimate.reshape(FLAT, 128),
        psf_cells.reshape(6, 1, KS3),
        cell_row.reshape(1, 128),
        observed.reshape(6, E3),
    )
    return result.reshape(1, E3)


def solution(mesh):
    return jax.shard_map(
        local,
        mesh=mesh,
        in_specs=(
            P("blk", None),
            P("blk", None, None),
            P("blk", None, None),
            P("blk"),
            P("blk", None),
            P("blk", None, None),
            P("blk", None, None),
            P(),
            P(),
        ),
        out_specs=P("blk", None),
        check_vma=False,
    )
```
